32 devices in a mesh: rep: 4 (over y, core), shard: 8 (over z, x).
Axes of the slice: x: 2, y: 2, z: 4, core: 2. Of those that a mesh axis runs over, the one named last changes fastest.
Arguments:
- tokens: bfloat16 [32, 512, 1152], P(('rep', 'shard')), may hold values from -6 to 6
- cotangent: bfloat16 [32, 512, 1152], P(('rep', 'shard')), may hold values from -6 to 6
- adapter_ids: int32 [32, 1], P(('rep', 'shard')), may hold values from 0 to 7
- gain_one: float32 [1152], replicated, may hold values from 0.5 to 1.5
- shift_one: float32 [1152], replicated, may hold values from -1.5 to 1.5
- gain_two: float32 [1152], replicated, may hold values from 0.5 to 1.5
- shift_two: float32 [1152], replicated, may hold values from -1.5 to 1.5
- qkv_weight: bfloat16 [3, 1152, 1152], P(None, 'shard'), may hold values from -0.1875 to 0.1875
- out_weight: bfloat16 [1152, 1152], P('shard'), may hold values from -0.5 to 0.5
- mlp_first: bfloat16 [1152, 4304], P('shard'), may hold values from -0.1875 to 0.1875
- mlp_second: bfloat16 [4304, 1152], P(None, 'shard'), may hold values from -0.09375 to 0.09375
- down_narrow: bfloat16 [5, 128, 1152], P(None, 'shard'), may hold values from -0.1875 to 0.1875
- down_wide: bfloat16 [128, 4304], P('shard'), may hold values from -0.09375 to 0.09375
- up_narrow: bfloat16 [5, 128, 1152], P(None, 'shard'), may hold values from -1.5 to 1.5
- up_wide: bfloat16 [128, 4304], P('shard'), may hold values from -1.5 to 1.5
Outputs:
- output: bfloat16 [32, 512, 1152], P(('rep', 'shard'))
- input_grad: bfloat16 [32, 512, 1152], P(('rep', 'shard'))
- grad_down_narrow: float32 [5, 128, 1152], P(None, 'shard')
- grad_down_wide: float32 [128, 4304], P('shard')
- grad_up_narrow: float32 [5, 128, 1152], P(None, 'shard')
- grad_up_wide: float32 [128, 4304], P('shard')
The draws below stay inside these ranges and needn't reach their ends.
Inputs may be any that keep to these rules, and one draw needn't show every extreme that they name: `adapter_ids`: every adapter is used by some image.
All inputs are finite; a program needn't handle non-finite values.
Results may differ from the reference program's by a relative error of at most 0.019.
The reference program's roundings to bfloat16 on the way count: a program that leaves them out, or rounds other values in their place, can miss the bound.
Values may be sent and summed in bfloat16 or wider, within the bound.
A program may use at most 256 MiB of HBM per device.

```python
import math
import jax
import jax.numpy as jnp
from jax import lax

D = 1152
HEADS = 16
HEAD_DIM = 72
FF = 4304
RANK = 16
NAD = 8
SEQ = 512
IMAGES = 32


def shard_levels(stream_key, extent, shards, smallest, largest):
    def one(axis_at, shards_of):
        draws = jax.random.uniform(jax.random.fold_in(jax.random.fold_in(stream_key, 6), axis_at), (shards_of,), jnp.float32, smallest / len(shards), largest / len(shards))
        return jnp.repeat(jnp.exp(draws), extent[axis_at] // shards_of).reshape((-1,) + (1,) * (len(extent) - axis_at - 1))

    level = one(*shards[0])
    for cut in shards[1:]:
        level = level * one(*cut)
    return level


def picks_of(stream_key, rows, amount, top, lift):
    order = jax.random.permutation(jax.random.fold_in(stream_key, 1), amount)
    boost = order
    for power in range(3):
        boost = boost * boost // amount
    boost = boost * lift // amount
    lots = jax.random.randint(jax.random.fold_in(stream_key, 2), (rows, amount), 0, 4096) + boost
    sure = jax.random.permutation(jax.random.fold_in(stream_key, 3), rows)[jnp.arange(amount) % rows]
    lots = jnp.where(jnp.arange(rows)[:, None] == sure[None, :], 1 << 14, lots)
    priority = lots * amount + jnp.arange(amount)
    return lax.top_k(priority.astype(jnp.int32), top)[1].astype(jnp.int32)


def gaussian(stream_key, dims, scale, most, pieces=(), kind=jnp.bfloat16):
    entries = jax.random.normal(stream_key, dims, jnp.float32) * scale
    if len(pieces) > 0:
        entries = shard_levels(stream_key, dims, pieces, -0.22, 0.18) * entries
    return jnp.clip(entries, min=-most, max=most).astype(kind)


def setup_inputs(seed: int = 0) -> dict:
    key_of = jax.random.split(jax.random.key(seed), 16)
    return {
        "tokens": gaussian(key_of[0], (IMAGES, SEQ, D), 1.0, 6.0, ((0, 32),)),
        "cotangent": gaussian(key_of[1], (IMAGES, SEQ, D), 1.0, 6.0, ((0, 32),)),
        "adapter_ids": picks_of(key_of[2], IMAGES, NAD, 1, 2048),
        "gain_one": jnp.clip(1.0 + 0.1 * jax.random.normal(key_of[3], (D,), jnp.float32), 0.5, 1.5),
        "shift_one": gaussian(key_of[4], (D,), 0.3, 1.5, (), jnp.float32),
        "gain_two": jnp.clip(1.0 + 0.1 * jax.random.normal(key_of[5], (D,), jnp.float32), 0.5, 1.5),
        "shift_two": gaussian(key_of[6], (D,), 0.3, 1.5, (), jnp.float32),
        "qkv_weight": gaussian(key_of[7], (3, D, D), D ** -0.5, 0.1875, ((1, 8),)),
        "out_weight": gaussian(key_of[8], (D, D), (D // 8) ** -0.5, 0.5, ((0, 8),)),
        "mlp_first": gaussian(key_of[9], (D, FF), D ** -0.5, 0.1875, ((0, 8),)),
        "mlp_second": gaussian(key_of[10], (FF, D), FF ** -0.5, 0.09375, ((1, 8),)),
        "down_narrow": gaussian(key_of[11], (5, NAD * RANK, D), D ** -0.5, 0.1875, ((1, 8),)),
        "down_wide": gaussian(key_of[12], (NAD * RANK, FF), FF ** -0.5, 0.09375, ((0, 8),)),
        "up_narrow": gaussian(key_of[13], (5, NAD * RANK, D), RANK ** -0.5, 1.5, ((1, 8),)),
        "up_wide": gaussian(key_of[14], (NAD * RANK, FF), RANK ** -0.5, 1.5, ((0, 8),)),
    }


@jax.custom_vjp
def low(v):
    return lax.optimization_barrier(v.astype(jnp.bfloat16)).astype(jnp.float32)

@jax.custom_vjp
def low_back(v):
    return v

def low_keep(v):
    return (low(v), None)

def low_pass(kept, grad):
    return (grad,)

def back_keep(v):
    return (v, None)

def back_low(kept, grad):
    return (low(grad),)
low.defvjp(low_keep, low_pass)
low_back.defvjp(back_keep, back_low)

def both_ways(value):
    return low_back(low(value))

def product(left, right):
    return jnp.matmul(left, right, precision=lax.Precision.HIGHEST)

def layer_norm(value, gain, shift):
    average = lax.optimization_barrier(jnp.mean(value, axis=-1, keepdims=True))
    centred = value - average
    spread = lax.optimization_barrier(jnp.mean(centred * centred, axis=-1, keepdims=True))
    return centred * lax.rsqrt(spread + 1e-06) * gain + shift

def project(inputs, weight, down, up, select):
    primary = product(inputs, weight)
    inner = both_ways(product(inputs, jnp.swapaxes(down, 0, 1)) * select)
    return primary + product(inner, up)

def block(hidden_in, select, adapters, frozen):
    down_narrow, down_wide, up_narrow, up_wide = adapters
    gain_one, shift_one, gain_two, shift_two, qkv_weight, out_weight, mlp_first, mlp_second = frozen
    images_here = hidden_in.shape[0]
    seq_len = hidden_in.shape[1]
    shape_heads = (images_here, seq_len, HEADS, HEAD_DIM)
    normed = low(layer_norm(hidden_in, gain_one, shift_one))
    query = both_ways(project(normed, qkv_weight[0], down_narrow[0], up_narrow[0], select))
    keys = both_ways(project(normed, qkv_weight[1], down_narrow[1], up_narrow[1], select))
    values = both_ways(project(normed, qkv_weight[2], down_narrow[2], up_narrow[2], select))
    scores = jnp.einsum('gqhd,gkhd->ghqk', query.reshape(shape_heads), keys.reshape(shape_heads), precision=lax.Precision.HIGHEST) * HEAD_DIM ** (-0.5)
    scores = low_back(scores)
    probs = low(jax.nn.softmax(scores, axis=-1))
    attended = jnp.einsum('ghqk,gkhd->gqhd', probs, values.reshape(shape_heads), precision=lax.Precision.HIGHEST)
    attended = both_ways(attended.reshape(images_here, seq_len, D))
    branch = low_back(project(attended, out_weight, down_narrow[3], up_narrow[3], select))
    middle = hidden_in + branch
    normed_two = low(layer_norm(middle, gain_two, shift_two))
    before = low_back(project(normed_two, mlp_first, down_narrow[4], up_wide, select))
    active = low(jax.nn.gelu(before, approximate=True))
    after = low_back(project(active, mlp_second, down_wide, up_narrow[4], select))
    return middle + after

def reference(tokens, cotangent, adapter_ids, gain_one, shift_one, gain_two, shift_two, qkv_weight, out_weight, mlp_first, mlp_second, down_narrow, down_wide, up_narrow, up_wide):
    group = math.gcd(IMAGES, max(1, 4096 // SEQ))
    ranks = NAD * RANK
    columns = jnp.arange(ranks, dtype=jnp.int32) // RANK
    select = (columns[None, :] == adapter_ids[:, :1].astype(jnp.int32)).astype(jnp.float32)
    select = select.reshape(IMAGES // group, group, 1, ranks)
    frozen = tuple((member.astype(jnp.float32) for member in (gain_one, shift_one, gain_two, shift_two, qkv_weight, out_weight, mlp_first, mlp_second)))

    def forward(inputs, narrow_down, wide_down, narrow_up, wide_up):
        grouped = inputs.reshape(IMAGES // group, group, SEQ, D)

        def one_group(group_pair):
            return block(group_pair[0], group_pair[1], (narrow_down, wide_down, narrow_up, wide_up), frozen)
        outputs = lax.map(jax.checkpoint(one_group), (grouped, select))
        return outputs.reshape(IMAGES, SEQ, D)
    output, pullback = jax.vjp(forward, tokens.astype(jnp.float32), down_narrow.astype(jnp.float32), down_wide.astype(jnp.float32), up_narrow.astype(jnp.float32), up_wide.astype(jnp.float32))
    gradients = pullback(cotangent.astype(jnp.float32))
    return (output.astype(jnp.bfloat16), gradients[0].astype(jnp.bfloat16), gradients[1], gradients[2], gradients[3], gradients[4])
```

```python
import jax
import jax.numpy as jnp
from jax import lax
from jax.experimental import pallas as pl
from jax.experimental.pallas import tpu as pltpu
from jax.sharding import PartitionSpec as P

HEAD_DIM = 72
RANK = 16


GELU_SCALE = 0.7978845608028654
GELU_CUBE = 0.044715


MESH=pl.DeviceIdType.MESH
CH=[(c*384,384) for c in range(5)]+[(1920,256)]
class Net:
    def __init__(self, loc, buf, ss, rs):
        self.loc=loc; self.buf=buf; self.ss=ss; self.rs=rs
        r=lax.axis_index("rep"); s=lax.axis_index("shard")
        self.y=r//2; self.c=lax.rem(r,2); self.z=s//2; self.x=lax.rem(s,2)
    def piece(self,g,ry,rc,z,x,own=False):
        kind,i=g
        s=2*z+x; q=2*ry+rc
        N,A,M,W=self.loc if own else self.buf
        if kind=='N': return N.at[pl.ds(3*q,3)] if own else N.at[pl.ds(3*q,3),pl.ds(pl.multiple_of(16*s,16),16)]
        if kind=='A': return A.at[q,pl.ds(48*i,48)] if own else A.at[q,pl.ds(pl.multiple_of(144*s+48*i,16),48)]
        if kind=='M':
            o,w=CH[i]; cs=pl.ds(pl.multiple_of(ry*2176+o,128),w)
            return M.at[rc,:,cs] if own else M.at[rc,pl.ds(pl.multiple_of(144*s,16),144),cs]
        cs=pl.ds(pl.multiple_of(ry*2176,128),2176)
        return W.at[rc,:,cs] if own else W.at[rc,pl.ds(pl.multiple_of(16*s,16),16),cs]
    def dev(self,y=None,c=None,z=None,x=None):
        y=self.y if y is None else y; c=self.c if c is None else c
        z=self.z if z is None else z; x=self.x if x is None else x
        return (2*y+c,2*z+x)
    def cp(self,gi,slot,src,dst,dev):
        return pltpu.make_async_remote_copy(src,dst,self.ss.at[gi,slot],self.rs.at[gi,slot],device_id=dev,device_id_type=MESH)
    def Zc(self,gi,g,k):
        p=self.piece(g,self.y,self.c,self.z,self.x)
        return self.cp(gi,k-1,self.piece(g,self.y,self.c,self.z,self.x,True),p,self.dev(z=lax.rem(self.z+k,4)))
    def src(self,k): return lax.rem(self.z+4-k,4)
    def fwd(self,gi,g,slot,ry,z,x,dev,own=False):
        p=self.piece(g,ry,self.c,z,x)
        return self.cp(gi,slot,self.piece(g,ry,self.c,z,x,True) if own else p,p,dev)
    def X(self,gi,g,k,own=False): return self.fwd(gi,g,3+k,self.y,self.src(k),self.x,self.dev(x=1-self.x),own)
    def XD(self,gi,g): return self.fwd(gi,g,7,1-self.y,self.z,self.x,self.dev(x=1-self.x),True)
    def Y(self,gi,g,k): return self.fwd(gi,g,7+k,self.y,self.src(k),self.x,self.dev(y=1-self.y))
    def Dy(self,gi,g,k): return self.fwd(gi,g,10+k,self.y,self.src(k),1-self.x,self.dev(y=1-self.y))
    def Dx(self,gi,g,k): return self.fwd(gi,g,10+k,1-self.y,self.src(k),self.x,self.dev(x=1-self.x))
    def Cz(self,gi,g,k): return self.fwd(gi,g,13+k,self.y,self.src(k),self.x,self.dev(c=1-self.c))
    def Cx(self,gi,g,k): return self.fwd(gi,g,17+k,self.y,self.src(k),1-self.x,self.dev(c=1-self.c))
    def Cxd(self,gi,g): return self.fwd(gi,g,21,1-self.y,self.z,1-self.x,self.dev(c=1-self.c))
    def Cy(self,gi,g,k): return self.fwd(gi,g,21+k,1-self.y,self.src(k),self.x,self.dev(c=1-self.c))
    def Cd(self,gi,g,k): return self.fwd(gi,g,24+k,1-self.y,self.src(k),1-self.x,self.dev(c=1-self.c))
    def nx(self,gi): return 1 if gi%2 else 0
    def loop(self,lo,hi,f):
        def body(k,_):
            f(k); return 0
        lax.fori_loop(lo,hi,body,0)
    def A(self,gi,g):
        self.loop(1,4,lambda k: self.Zc(gi,g,k).start())
        self.X(gi,g,0,True).start(); self.XD(gi,g).start()
    def B(self,gi,g):
        def f(k):
            self.Zc(gi,g,k).wait_recv()
            self.X(gi,g,k).start(); self.Y(gi,g,k).start(); self.Cz(gi,g,k).start()
        self.loop(1,4,f)
    def C(self,gi,g):
        n=self.nx(gi)
        self.X(gi,g,0,True).wait_recv(); self.Cx(gi,g,0).start()
        self.XD(gi,g).wait_recv(); self.Cxd(gi,g).start()
        def f(k):
            self.Y(gi,g,k).wait_recv(); self.Cy(gi,g,k).start()
            self.X(gi,g,k).wait_recv(); self.Cx(gi,g,k).start()
        def fx(k):
            f(k); self.Dx(gi,g,k).start()
        def fy(k):
            f(k); self.Dy(gi,g,k).start()
        if n: self.loop(1,1+n,fx)
        self.loop(1+n,4,fy)
    def D(self,gi,g):
        def f(k):
            self.Dy(gi,g,k).wait_recv(); self.Cd(gi,g,k).start()
        self.loop(1,4,f)
    def E(self,gi,g):
        self.Cx(gi,g,0).wait_recv(); self.Cxd(gi,g).wait_recv()
        def f(k):
            self.Cz(gi,g,k).wait_recv(); self.Cx(gi,g,k).wait_recv(); self.Cy(gi,g,k).wait_recv(); self.Cd(gi,g,k).wait_recv()
        self.loop(1,4,f)
    def F(self,gi,g):
        def f(k):
            for h in (self.Zc,self.X,self.Y,self.Dy,self.Cz,self.Cx,self.Cy,self.Cd): h(gi,g,k).wait_send()
        self.loop(1,4,f)
        self.X(gi,g,0).wait_send(); self.XD(gi,g).wait_send(); self.Cx(gi,g,0).wait_send(); self.Cxd(gi,g).wait_send()
    def barrier(self):
        b=pltpu.get_barrier_semaphore()
        for k in (1,2,3): pl.semaphore_signal(b,1,device_id=self.dev(z=lax.rem(self.z+k,4)),device_id_type=MESH)
        pl.semaphore_signal(b,1,device_id=self.dev(x=1-self.x),device_id_type=MESH)
        pl.semaphore_signal(b,1,device_id=self.dev(y=1-self.y),device_id_type=MESH)
        pl.semaphore_signal(b,1,device_id=self.dev(c=1-self.c),device_id_type=MESH)
        pl.semaphore_wait(b,6)
GROUPS=[('N',0),('A',0),('A',1),('A',2),('W',0)]+[('M',c) for c in range(6)]
def schedule(n):
    out=[]
    for t in range(n+4):
        for st,lag in (('E',4),('D',3),('C',2),('B',1),('A',0)):
            g=t-lag
            if 0<=g<n: out.append((st,g))
    return out
def gather_kernel(nl,na,nm,nw,N,A,M,W,ss,rs,ls):
    net=Net((nl,na,nm,nw),(N,A,M,W),ss,rs)
    net.barrier()
    s=2*net.z+net.x
    l=[pltpu.make_async_copy(nl,N.at[:,pl.ds(pl.multiple_of(16*s,16),16)],ls.at[0]),
       pltpu.make_async_copy(na,A.at[:,pl.ds(pl.multiple_of(144*s,16),144)],ls.at[1]),
       pltpu.make_async_copy(nm,M.at[:,pl.ds(pl.multiple_of(144*s,16),144)],ls.at[2]),
       pltpu.make_async_copy(nw,W.at[:,pl.ds(pl.multiple_of(16*s,16),16)],ls.at[3])]
    for st,g in schedule(len(GROUPS)):
        getattr(net,st)(g,GROUPS[g])
        if st=='A' and g==1:
            for q in l: q.start()
    for q in l: q.wait()
    for g in range(len(GROUPS)): net.F(g,GROUPS[g])
def gather(nl,na,nm,nw):
    n=len(GROUPS)
    return pl.pallas_call(gather_kernel,
      out_shape=(jax.ShapeDtypeStruct((12,128,1152),jnp.bfloat16),jax.ShapeDtypeStruct((4,1152,1152),jnp.bfloat16),
        jax.ShapeDtypeStruct((2,1152,4352),jnp.bfloat16),jax.ShapeDtypeStruct((2,128,4352),jnp.bfloat16)),
      in_specs=[pl.BlockSpec(memory_space=pl.ANY)]*4,out_specs=[pl.BlockSpec(memory_space=pl.ANY)]*4,
      scratch_shapes=[pltpu.SemaphoreType.DMA((n,28)),pltpu.SemaphoreType.DMA((n,28)),pltpu.SemaphoreType.DMA((4,))],
      compiler_params=pltpu.CompilerParams(collective_id=1,has_side_effects=True),name="gather")(nl,na,nm,nw)


def dot_plain(left, right):
    return jnp.dot(left, right, preferred_element_type=jnp.float32)


def dot_last(left, right):
    return lax.dot_general(
        left, right, (((1,), (1,)), ((), ())), preferred_element_type=jnp.float32
    )


def dot_first(left, right):
    return lax.dot_general(
        left, right, (((0,), (0,)), ((), ())), preferred_element_type=jnp.float32
    )


def layer_stats(value):
    average = jnp.mean(value, axis=-1, keepdims=True)
    centred = value - average
    spread = jnp.mean(centred * centred, axis=-1, keepdims=True)
    inverse = lax.rsqrt(spread + 1e-06)
    return (centred * inverse, inverse)


def norm_back(gradient, normal_part, inverse, gain):
    scaled = gradient * gain
    return inverse * (
        scaled
        - jnp.mean(scaled, axis=-1, keepdims=True)
        - normal_part * jnp.mean(scaled * normal_part, axis=-1, keepdims=True)
    )


def gelu_slope(value):
    tangent = jnp.tanh(GELU_SCALE * (value + GELU_CUBE * value * value * value))
    return 0.5 * (1.0 + tangent) + 0.5 * value * (1.0 - tangent * tangent) * GELU_SCALE * (
        1.0 + 3.0 * GELU_CUBE * value * value
    )


def adapter_in(inputs, down, select):
    return (dot_last(inputs, down) * select).astype(jnp.bfloat16)


def adapter_back(grad_out, inputs, inner, down, up, select):
    grad_inner = dot_last(grad_out, up).astype(jnp.bfloat16) * select.astype(jnp.bfloat16)
    return (dot_plain(grad_inner, down), dot_first(grad_inner, inputs), dot_first(inner, grad_out))


def split_heads(value, heads):
    return value.reshape(value.shape[0], heads, value.shape[1] // heads)


def per_device(
    tokens,
    cotangent,
    adapter_ids,
    gain_one,
    shift_one,
    gain_two,
    shift_two,
    qkv_weight,
    out_weight,
    mlp_first,
    mlp_second,
    down_narrow,
    down_wide,
    up_narrow,
    up_wide,
):
    hidden_in = tokens[0].astype(jnp.float32)
    seq_len, width = hidden_in.shape
    heads = width // HEAD_DIM
    scaling = HEAD_DIM ** (-0.5)
    features = mlp_first.shape[1]
    wide = ((0, 0), (0, 0), (0, -features % 256))
    narrow_local = jnp.concatenate(
        [down_narrow[:3], up_narrow[:3], down_narrow[3:], up_narrow[3:], down_narrow[:2]]
    )
    attention_local = jnp.concatenate([qkv_weight, out_weight[None]])
    mlp_local = jnp.pad(jnp.stack([mlp_first, mlp_second.T]), wide)
    wide_local = jnp.pad(jnp.stack([up_wide, down_wide]), wide)
    locals_ = (narrow_local, attention_local, mlp_local, wide_local)
    if (lax.axis_size("rep"), lax.axis_size("shard")) == (4, 8):
        narrow, attention, mlp, wides = gather(*locals_)
    else:
        narrow, attention, mlp, wides = [
            lax.all_gather(each, "shard", axis=1, tiled=True) for each in locals_
        ]
    narrow_down = [narrow[0], narrow[1], narrow[2], narrow[6], narrow[7]]
    narrow_up = [narrow[3], narrow[4], narrow[5], narrow[8], narrow[9]]
    wide_up, wide_down = wides[0, :, :features], wides[1, :, :features]
    qkv_full, out_full = attention[:3], attention[3]
    first_full, second_full = mlp[0, :, :features], mlp[1, :, :features]
    ranks = narrow_down[0].shape[0]
    select = (lax.broadcasted_iota(jnp.int32, (1, ranks), 1) // RANK == adapter_ids[0, 0]).astype(
        jnp.float32
    )
    normal_one, inverse_one = layer_stats(hidden_in)
    normed = (normal_one * gain_one + shift_one).astype(jnp.bfloat16)
    columns = normed
    qkv_main = jnp.einsum(
        "tr,jre->jte",
        columns,
        qkv_full,
        preferred_element_type=jnp.float32,
    )
    inner_qkv = [adapter_in(normed, narrow_down[member], select) for member in range(3)]
    projected = [
        (qkv_main[member] + dot_plain(inner_qkv[member], narrow_up[member])).astype(jnp.bfloat16)
        for member in range(3)
    ]
    query_heads = split_heads(projected[0], heads)
    key_heads = split_heads(projected[1], heads)
    value_heads = split_heads(projected[2], heads)
    scores = (
        jnp.einsum("qhd,khd->hqk", query_heads, key_heads, preferred_element_type=jnp.float32)
        * scaling
    )
    row_top = jnp.max(scores, axis=-1, keepdims=True)
    exponent = jnp.exp(scores - row_top)
    row_total = jnp.sum(exponent, axis=-1, keepdims=True)
    log_total = row_top + jnp.log(row_total)
    probs_low = (exponent / row_total).astype(jnp.bfloat16)
    attended = jnp.einsum(
        "hqk,khd->qhd", probs_low, value_heads, preferred_element_type=jnp.float32
    )
    attended = attended.reshape(seq_len, width).astype(jnp.bfloat16)
    columns = attended
    out_main = dot_plain(columns, out_full)
    inner_out = adapter_in(attended, narrow_down[3], select)
    middle = hidden_in + (out_main + dot_plain(inner_out, narrow_up[3]))
    normal_two, inverse_two = layer_stats(middle)
    normed_two = (normal_two * gain_two + shift_two).astype(jnp.bfloat16)
    columns = normed_two
    first_main = dot_plain(columns, first_full)
    inner_one = adapter_in(normed_two, narrow_down[4], select)
    before = first_main + dot_plain(inner_one, wide_up)
    active = jax.nn.gelu(before, approximate=True).astype(jnp.bfloat16)
    second_main = dot_last(active, second_full)
    inner_two = adapter_in(active, wide_down, select)
    output = (middle + (second_main + dot_plain(inner_two, narrow_up[4]))).astype(jnp.bfloat16)
    grad_after = cotangent[0]
    columns = grad_after
    active_main = dot_plain(columns, second_full)
    back_two, grad_wide_down, grad_up_fc = adapter_back(
        grad_after, active, inner_two, wide_down, narrow_up[4], select
    )
    grad_before = ((active_main + back_two) * gelu_slope(before)).astype(jnp.bfloat16)
    normed_two_main = dot_last(grad_before, first_full)
    back_one, grad_down_fc, grad_wide_up = adapter_back(
        grad_before, normed_two, inner_one, narrow_down[4], wide_up, select
    )
    grad_middle = cotangent[0].astype(jnp.float32) + norm_back(
        normed_two_main + back_one, normal_two, inverse_two, gain_two
    )
    grad_branch = grad_middle.astype(jnp.bfloat16)
    attended_main = dot_last(grad_branch, out_full)
    back_out, grad_down_out, grad_up_out = adapter_back(
        grad_branch, attended, inner_out, narrow_down[3], narrow_up[3], select
    )
    grad_attended = split_heads((attended_main + back_out).astype(jnp.bfloat16), heads)
    again_scores = (
        jnp.einsum("qhd,khd->hqk", query_heads, key_heads, preferred_element_type=jnp.float32)
        * scaling
    )
    probs_again = jnp.exp(again_scores - log_total)
    grad_probs = jnp.einsum(
        "qhd,khd->hqk", grad_attended, value_heads, preferred_element_type=jnp.float32
    )
    grad_value = jnp.einsum(
        "hqk,qhd->khd",
        probs_again.astype(jnp.bfloat16),
        grad_attended,
        preferred_element_type=jnp.float32,
    )
    grad_scores = probs_again * (
        grad_probs - jnp.sum(grad_probs * probs_again, axis=-1, keepdims=True)
    )
    grad_scores = grad_scores.astype(jnp.bfloat16)
    grad_query = (
        jnp.einsum("hqk,khd->qhd", grad_scores, key_heads, preferred_element_type=jnp.float32)
        * scaling
    )
    grad_key = (
        jnp.einsum("hqk,qhd->khd", grad_scores, query_heads, preferred_element_type=jnp.float32)
        * scaling
    )
    grad_qkv = jnp.stack(
        [
            grad_query.reshape(seq_len, width),
            grad_key.reshape(seq_len, width),
            grad_value.reshape(seq_len, width),
        ]
    ).astype(jnp.bfloat16)
    normed_main = jnp.einsum(
        "jte,jre->tr",
        grad_qkv,
        qkv_full,
        preferred_element_type=jnp.float32,
    )
    grad_downs = []
    grad_ups = []
    for member in range(3):
        back_member, grad_down_member, grad_up_member = adapter_back(
            grad_qkv[member],
            normed,
            inner_qkv[member],
            narrow_down[member],
            narrow_up[member],
            select,
        )
        normed_main = normed_main + back_member
        grad_downs.append(grad_down_member)
        grad_ups.append(grad_up_member)
    input_grad = (grad_middle + norm_back(normed_main, normal_one, inverse_one, gain_one)).astype(
        jnp.bfloat16
    )
    parts = grad_downs + [grad_down_out, grad_down_fc] + grad_ups + [grad_up_out, grad_up_fc]
    parts = parts + [grad_wide_down, grad_wide_up]
    share = lax.psum_scatter(
        jnp.concatenate(parts, axis=1).astype(jnp.bfloat16),
        "shard",
        scatter_dimension=0,
        tiled=True,
    )
    total = lax.psum(share, "rep").astype(jnp.float32)
    narrows = total[:, : 10 * width].reshape(-1, 10, width).transpose(1, 0, 2)
    totals = (
        narrows[:5],
        total[:, 10 * width : 10 * width + features],
        narrows[5:],
        total[:, 10 * width + features :],
    )
    return (output[None], input_grad[None], totals[0], totals[1], totals[2], totals[3])


def solution(mesh):
    return jax.shard_map(
        per_device,
        mesh=mesh,
        in_specs=(
            P(("rep", "shard"), None, None),
            P(("rep", "shard"), None, None),
            P(("rep", "shard"), None),
            P(),
            P(),
            P(),
            P(),
            P(None, "shard", None),
            P("shard", None),
            P("shard", None),
            P(None, "shard"),
            P(None, "shard", None),
            P("shard", None),
            P(None, "shard", None),
            P("shard", None),
        ),
        out_specs=(
            P(("rep", "shard"), None, None),
            P(("rep", "shard"), None, None),
            P(None, "shard", None),
            P("shard", None),
            P(None, "shard", None),
            P("shard", None),
        ),
        check_vma=False,
    )
```

```python
import functools

import jax
import jax.numpy as jnp
from jax import lax
from jax.experimental import pallas as pl
from jax.experimental.pallas import tpu as pltpu
from jax.sharding import PartitionSpec as P

HEAD_DIM = 72
RANK = 16
GELU_SCALE = 0.7978845608028654
GELU_CUBE = 0.044715
MESH = pl.DeviceIdType.MESH
LANES = 128
BF16 = jnp.bfloat16
F32 = jnp.float32
CUTS = [(0, 512), (512, 512), (1024, 512), (1536, 512), (2048, 128)]
GROUPS = [("narrow", 0), ("square", 0), ("square", 1), ("square", 2), ("wide", 0)] + [
    ("mlp", cut) for cut in range(len(CUTS))
]
WIDE_GROUP = 4


def dot_nn(left, right):
    return jnp.dot(left, right, preferred_element_type=F32)


def dot_nt(left, right):
    return lax.dot_general(left, right, (((1,), (1,)), ((), ())), preferred_element_type=F32)


def dot_tn(left, right):
    return lax.dot_general(left, right, (((0,), (0,)), ((), ())), preferred_element_type=F32)


def repeat(low, high, step):
    def body(index, carry):
        step(index)
        return carry

    lax.fori_loop(low, high, body, 0)


def rows_of(index, count):
    return pl.ds(pl.multiple_of(index * count, count), count)


def layer_stats(value):
    average = jnp.mean(value, axis=-1, keepdims=True)
    centred = value - average
    spread = jnp.mean(centred * centred, axis=-1, keepdims=True)
    inverse = lax.rsqrt(spread + 1e-06)
    return (centred * inverse, inverse)


def norm_back(gradient, normal_part, inverse, gain):
    scaled = gradient * gain
    return inverse * (
        scaled
        - jnp.mean(scaled, axis=-1, keepdims=True)
        - normal_part * jnp.mean(scaled * normal_part, axis=-1, keepdims=True)
    )


class Gather:
    def __init__(self, local, whole, send, receive):
        self.local, self.whole, self.send, self.receive = local, whole, send, receive
        rep, shard = lax.axis_index("rep"), lax.axis_index("shard")
        self.y, self.c = rep // 2, lax.rem(rep, 2)
        self.z, self.x = shard // 2, lax.rem(shard, 2)

    def piece(self, group, y, c, z, x, own=False):
        kind, part = group
        narrow, square, mlp, wide = self.local if own else self.whole
        shard, quarter = 2 * z + x, 2 * y + c
        if kind == "narrow":
            three = pl.ds(3 * quarter, 3)
            return narrow.at[three] if own else narrow.at[three, rows_of(shard, 16)]
        if kind == "square":
            if own:
                return square.at[quarter, pl.ds(48 * part, 48)]
            return square.at[quarter, pl.ds(pl.multiple_of(144 * shard + 48 * part, 16), 48)]
        if kind == "mlp":
            start, width = CUTS[part]
            half = mlp.shape[2] // 2
            columns = pl.ds(pl.multiple_of(y * half + start, LANES), width)
            if own:
                return mlp.at[c, :, columns]
            return mlp.at[c, pl.ds(pl.multiple_of(144 * shard, 16), 144), columns]
        half = wide.shape[2] // 2
        columns = pl.ds(pl.multiple_of(y * half, LANES), half)
        return wide.at[c, :, columns] if own else wide.at[c, rows_of(shard, 16), columns]

    def device(self, y=None, c=None, z=None, x=None):
        y = self.y if y is None else y
        c = self.c if c is None else c
        z = self.z if z is None else z
        x = self.x if x is None else x
        return (2 * y + c, 2 * z + x)

    def source(self, hop):
        return lax.rem(self.z + 4 - hop, 4)

    def copy(self, at, slot, y, z, x, device, own=False):
        target = self.piece(GROUPS[at], y, self.c, z, x)
        start = self.piece(GROUPS[at], y, self.c, z, x, True) if own else target
        return pltpu.make_async_remote_copy(
            start,
            target,
            self.send.at[at, slot],
            self.receive.at[at, slot],
            device_id=device,
            device_id_type=MESH,
        )

    def along_z(self, at, hop):
        device = self.device(z=lax.rem(self.z + hop, 4))
        return self.copy(at, hop - 1, self.y, self.z, self.x, device, True)

    def over_x(self, at, hop, own=False):
        device = self.device(x=1 - self.x)
        return self.copy(at, 3 + hop, self.y, self.source(hop), self.x, device, own)

    def corner_here(self, at):
        return self.copy(at, 7, 1 - self.y, self.z, self.x, self.device(x=1 - self.x), True)

    def over_y(self, at, hop):
        device = self.device(y=1 - self.y)
        return self.copy(at, 7 + hop, self.y, self.source(hop), self.x, device)

    def corner_by_y(self, at, hop):
        device = self.device(y=1 - self.y)
        return self.copy(at, 10 + hop, self.y, self.source(hop), 1 - self.x, device)

    def corner_by_x(self, at, hop):
        device = self.device(x=1 - self.x)
        return self.copy(at, 10 + hop, 1 - self.y, self.source(hop), self.x, device)

    def to_core(self, at, slot, y, z, x):
        return self.copy(at, slot, y, z, x, self.device(c=1 - self.c))

    def core_z(self, at, hop):
        return self.to_core(at, 13 + hop, self.y, self.source(hop), self.x)

    def core_x(self, at, hop):
        return self.to_core(at, 17 + hop, self.y, self.source(hop), 1 - self.x)

    def core_here(self, at):
        return self.to_core(at, 21, 1 - self.y, self.z, 1 - self.x)

    def core_y(self, at, hop):
        return self.to_core(at, 21 + hop, 1 - self.y, self.source(hop), self.x)

    def core_corner(self, at, hop):
        return self.to_core(at, 24 + hop, 1 - self.y, self.source(hop), 1 - self.x)

    def barrier(self):
        ready = pltpu.get_barrier_semaphore()
        partners = [self.device(z=lax.rem(self.z + hop, 4)) for hop in (1, 2, 3)]
        partners += [self.device(x=1 - self.x), self.device(y=1 - self.y), self.device(c=1 - self.c)]
        for partner in partners:
            pl.semaphore_signal(ready, 1, device_id=partner, device_id_type=MESH)
        pl.semaphore_wait(ready, len(partners))

    def stage_send(self, at):
        repeat(1, 4, lambda hop: self.along_z(at, hop).start())
        self.over_x(at, 0, True).start()
        self.corner_here(at).start()

    def stage_planes(self, at):
        def step(hop):
            self.along_z(at, hop).wait_recv()
            self.over_x(at, hop).start()
            self.over_y(at, hop).start()
            self.core_z(at, hop).start()

        repeat(1, 4, step)

    def stage_corners(self, at):
        by_x = at % 2
        self.over_x(at, 0, True).wait_recv()
        self.core_x(at, 0).start()
        self.corner_here(at).wait_recv()
        self.core_here(at).start()

        def step(hop, corner):
            self.over_y(at, hop).wait_recv()
            self.core_y(at, hop).start()
            self.over_x(at, hop).wait_recv()
            self.core_x(at, hop).start()
            corner(at, hop).start()

        if by_x:
            repeat(1, 1 + by_x, lambda hop: step(hop, self.corner_by_x))
        repeat(1 + by_x, 4, lambda hop: step(hop, self.corner_by_y))

    def stage_core(self, at):
        def step(hop):
            self.corner_by_y(at, hop).wait_recv()
            self.core_corner(at, hop).start()

        repeat(1, 4, step)

    def stage_arrived(self, at):
        self.core_x(at, 0).wait_recv()
        self.core_here(at).wait_recv()

        def step(hop):
            for copy in (self.core_z, self.core_x, self.core_y, self.core_corner):
                copy(at, hop).wait_recv()

        repeat(1, 4, step)

    def sent(self, at):
        def step(hop):
            for copy in (
                self.along_z,
                self.over_x,
                self.over_y,
                self.corner_by_y,
                self.core_z,
                self.core_x,
                self.core_y,
                self.core_corner,
            ):
                copy(at, hop).wait_send()

        repeat(1, 4, step)
        for copy in (self.over_x(at, 0), self.corner_here(at), self.core_x(at, 0), self.core_here(at)):
            copy.wait_send()

    def advance(self, tick):
        stages = (
            self.stage_arrived,
            self.stage_core,
            self.stage_corners,
            self.stage_planes,
            self.stage_send,
        )
        for lag, stage in zip((4, 3, 2, 1, 0), stages):
            if 0 <= tick - lag < len(GROUPS):
                stage(tick - lag)


def layer_kernel(
    remote,
    tokens,
    cotangent,
    select,
    vectors,
    narrow_from,
    square_from,
    mlp_from,
    wide_from,
    output,
    input_grad,
    narrow_grads,
    wide_grads,
    narrow,
    square,
    mlp,
    wide,
    query,
    key,
    value,
    mixed,
    normed,
    attended,
    middle,
    normed_two,
    after,
    back,
    small,
    sums,
    hidden,
    local_sem,
    *link_sems,
):
    sources = (narrow_from, square_from, mlp_from, wide_from)
    wholes = (narrow, square, mlp, wide)
    seq_len, width = tokens.shape
    heads = width // HEAD_DIM
    scaling = HEAD_DIM ** (-0.5)
    block = 256
    blocks = seq_len // block
    half = mlp.shape[2] // 2
    if remote:
        net = Gather(sources, wholes, *link_sems)
        shard = lax.axis_index("shard")
        own = []
        for index, (source, whole) in enumerate(zip(sources, wholes)):
            place = whole.at[:, rows_of(shard, source.shape[1])]
            own.append(pltpu.make_async_copy(source, place, local_sem.at[index]))
        advance, sent = net.advance, net.sent
        net.barrier()
    else:
        own = [
            pltpu.make_async_copy(source, whole, local_sem.at[index])
            for index, (source, whole) in enumerate(zip(sources, wholes))
        ]
        advance = sent = lambda at: None
    gain_one, shift_one = vectors[0:1, :], vectors[1:2, :]
    gain_two, shift_two = vectors[2:3, :], vectors[3:4, :]
    chosen = select[...]

    advance(0)
    advance(1)
    for copy in own:
        copy.start()

    def first_norm(index):
        rows = rows_of(index, 64)
        normal, _ = layer_stats(tokens[rows, :].astype(F32))
        normed[rows, :] = (normal * gain_one + shift_one).astype(BF16)

    repeat(0, seq_len // 64, first_norm)
    lane = lax.rem(lax.broadcasted_iota(jnp.int32, (64, heads * LANES), 1), LANES)
    minus = jnp.where((lane >= HEAD_DIM) & (lane < HEAD_DIM + 3), -1.0, 0.0).astype(BF16)

    def clear(index):
        rows = rows_of(index, 64)
        query[rows, :] = jnp.zeros_like(minus)
        value[rows, :] = jnp.zeros_like(minus)
        key[rows, :] = minus

    repeat(0, seq_len // 64, clear)
    for tick in range(2, 8):
        advance(tick)
    for copy in own:
        copy.wait()

    for member, padded in enumerate((query, key, value)):

        def project(index):
            rows = rows_of(index, block)
            lines = normed[rows, :]
            inner = (dot_nt(lines, narrow[member]) * chosen).astype(BF16)
            small[member, rows, :] = inner
            attended[rows, :] = (
                dot_nn(lines, square[member]) + dot_nn(inner, narrow[3 + member])
            ).astype(BF16)

        repeat(0, blocks, project)
        for head in range(heads):
            padded[:, LANES * head : LANES * head + HEAD_DIM] = attended[
                :, HEAD_DIM * head : HEAD_DIM * (head + 1)
            ]
    advance(8)

    lane = lax.broadcasted_iota(jnp.int32, (block, LANES), 1)

    def attend(head):
        columns = rows_of(head, LANES)
        for part in range(blocks):
            rows = pl.ds(part * block, block)
            lines = query[rows, columns]
            scores = dot_nt(lines, key[:, columns])
            top = jnp.max(scores, axis=-1, keepdims=True)
            exponent = jnp.exp((scores - top) * scaling)
            total = jnp.sum(exponent, axis=-1, keepdims=True)
            probs = (exponent * (1.0 / total)).astype(BF16)
            mixed[rows, columns] = dot_nn(probs, value[:, columns]).astype(BF16)
            level = top + jnp.log(total) * (1.0 / scaling)
            high = level.astype(BF16).astype(F32)
            mid = (level - high).astype(BF16).astype(F32)
            low = level - high - mid
            kept = jnp.where(lane == HEAD_DIM, high, lines.astype(F32))
            kept = jnp.where(lane == HEAD_DIM + 1, mid, kept)
            kept = jnp.where(lane == HEAD_DIM + 2, low, kept)
            query[rows, columns] = kept.astype(BF16)

    repeat(0, heads // 2, attend)
    advance(9)
    repeat(heads // 2, heads, attend)
    for head in range(heads):
        attended[:, HEAD_DIM * head : HEAD_DIM * (head + 1)] = mixed[
            :, LANES * head : LANES * head + HEAD_DIM
        ]

    def branch_out(index):
        rows = rows_of(index, block)
        lines = attended[rows, :]
        inner = (dot_nt(lines, narrow[6]) * chosen).astype(BF16)
        small[3, rows, :] = inner
        total = tokens[rows, :].astype(F32) + (dot_nn(lines, square[3]) + dot_nn(inner, narrow[8]))
        middle[rows, :] = total
        normal, _ = layer_stats(total)
        lines = (normal * gain_two + shift_two).astype(BF16)
        normed_two[rows, :] = lines
        small[4, rows, :] = (dot_nt(lines, narrow[7]) * chosen).astype(BF16)
        small[5, rows, :] = (dot_nt(cotangent[rows, :], narrow[9]) * chosen).astype(BF16)
        after[rows, :] = jnp.zeros((block, width), F32)
        back[rows, :] = jnp.zeros((block, width), F32)
        sums[0, rows, :] = jnp.zeros((block, LANES), F32)
        sums[1, rows, :] = jnp.zeros((block, LANES), F32)

    repeat(0, blocks, branch_out)
    advance(10)
    sent(WIDE_GROUP)

    for cut, (start, count) in enumerate(CUTS):

        def piece(side):
            columns = pl.ds(pl.multiple_of(side * half + start, LANES), count)

            def lines_of(index):
                rows = rows_of(index, block)
                before = dot_nn(normed_two[rows, :], mlp[0, :, columns])
                before = before + dot_nn(small[4, rows, :], wide[0, :, columns])
                square_of = before * before
                tangent = jnp.tanh(GELU_SCALE * (before + GELU_CUBE * square_of * before))
                active = (0.5 * before * (1.0 + tangent)).astype(BF16)
                slope = 0.5 * (1.0 + tangent) + 0.5 * before * (1.0 - tangent * tangent) * (
                    GELU_SCALE * (1.0 + 3.0 * GELU_CUBE * square_of)
                )
                gradient = dot_nn(cotangent[rows, :], mlp[1, :, columns])
                gradient = gradient + dot_nn(small[5, rows, :], wide[1, :, columns])
                gradient = (gradient * slope).astype(BF16)
                hidden[0, rows, pl.ds(0, count)] = active
                hidden[1, rows, pl.ds(0, count)] = gradient
                after[rows, :] += dot_nt(active, mlp[1, :, columns])
                sums[0, rows, :] += dot_nt(active, wide[1, :, columns])
                back[rows, :] += dot_nt(gradient, mlp[0, :, columns])
                sums[1, rows, :] += dot_nt(gradient, wide[0, :, columns])

            repeat(0, blocks, lines_of)
            wide[1, :, columns] = dot_tn(small[5], hidden[0, :, pl.ds(0, count)]).astype(BF16)
            wide[0, :, columns] = dot_tn(small[4], hidden[1, :, pl.ds(0, count)]).astype(BF16)

        repeat(0, 2, piece)
        if cut < 3:
            advance(11 + cut)

    for at in range(len(GROUPS)):
        if at != WIDE_GROUP:
            sent(at)
    outgoing = []

    def emit(index, source, target):
        copy = pltpu.make_async_copy(source, target, local_sem.at[4 + index])
        copy.start()
        outgoing.append(copy)

    def place(index):
        if index < 3:
            return mlp.at[0, pl.ds(1024, LANES), pl.ds(width * index, width)]
        if index < 6:
            return mlp.at[1, pl.ds(1024, LANES), pl.ds(width * (index - 3), width)]
        return mlp.at[1, pl.ds(512 + LANES * (index - 6), LANES), pl.ds(2 * width, width)]

    def emit_narrow(index, left, right):
        spot = place(index)
        spot[...] = dot_tn(left, right).astype(BF16)
        emit(index, spot, narrow_grads.at[index])

    emit(10, wide, wide_grads)
    staged = mlp.at[1, pl.ds(512, seq_len), pl.ds(0, width)]

    def second_out(index):
        rows = rows_of(index, block)
        inner = (sums[0, rows, :] * chosen).astype(BF16)
        small[6, rows, :] = inner
        staged[rows, :] = (middle[rows, :] + (after[rows, :] + dot_nn(inner, narrow[9]))).astype(BF16)
        small[7, rows, :] = (sums[1, rows, :] * chosen).astype(BF16)

    repeat(0, blocks, second_out)
    emit(11, staged, output)
    emit_narrow(4, small[7], normed_two[...])
    emit_narrow(9, small[6], cotangent[...])

    def second_norm_back(index):
        rows = rows_of(index, block)
        gradient = back[rows, :] + dot_nn(small[7, rows, :], narrow[7])
        normal, inverse = layer_stats(middle[rows, :])
        total = cotangent[rows, :].astype(F32) + norm_back(gradient, normal, inverse, gain_two)
        middle[rows, :] = total
        normed_two[rows, :] = total.astype(BF16)

    repeat(0, blocks, second_norm_back)
    flat = [mlp.at[1, pl.ds(0, seq_len), pl.ds(width * member, width)] for member in range(3)]

    def branch_back(index):
        rows = rows_of(index, block)
        lines = normed_two[rows, :]
        inner = (dot_nt(lines, narrow[8]) * chosen).astype(BF16)
        small[4, rows, :] = inner
        flat[0][rows, :] = (dot_nt(lines, square[3]) + dot_nn(inner, narrow[6])).astype(BF16)

    repeat(0, blocks, branch_back)
    emit_narrow(3, small[4], attended[...])
    emit_narrow(8, small[3], normed_two[...])
    for head in range(heads):
        mixed[:, LANES * head : LANES * head + HEAD_DIM] = flat[0][
            :, HEAD_DIM * head : HEAD_DIM * (head + 1)
        ]
    spread = heads * LANES
    grads = [
        mlp.at[0, pl.ds(0, seq_len), pl.ds(0, spread)],
        mlp.at[0, pl.ds(0, seq_len), pl.ds(spread, spread)],
        mlp.at[0, pl.ds(512, seq_len), pl.ds(0, spread)],
    ]

    def attend_back(head):
        columns = rows_of(head, LANES)
        lines, keys = query[:, columns], key[:, columns]
        gradient = mixed[:, columns]
        probs = jnp.exp(dot_nt(keys, lines) * scaling)
        grad_probs = dot_nt(value[:, columns], gradient)
        level = jnp.sum(probs * grad_probs, axis=0, keepdims=True)
        grad_scores = (probs * (grad_probs - level)).astype(BF16)
        grads[2][:, columns] = dot_nn(probs.astype(BF16), gradient).astype(BF16)
        grads[1][:, columns] = (dot_nn(grad_scores, lines) * scaling).astype(BF16)
        grads[0][:, columns] = (dot_tn(grad_scores, keys) * scaling).astype(BF16)

    repeat(0, heads, attend_back)
    for member in range(3):
        for head in range(heads):
            flat[member][:, HEAD_DIM * head : HEAD_DIM * (head + 1)] = grads[member][
                :, LANES * head : LANES * head + HEAD_DIM
            ]

        def project_back(index):
            rows = rows_of(index, block)
            lines = flat[member][rows, :]
            inner = (dot_nt(lines, narrow[3 + member]) * chosen).astype(BF16)
            small[4 + member, rows, :] = inner
            total = dot_nt(lines, square[member]) + dot_nn(inner, narrow[member])
            back[rows, :] = total if member == 0 else back[rows, :] + total

        repeat(0, blocks, project_back)
        emit_narrow(member, small[4 + member], normed[...])
        emit_narrow(5 + member, small[member], flat[member][...])
    last = mlp.at[1, pl.ds(512, seq_len), pl.ds(width, width)]

    def first_norm_back(index):
        rows = rows_of(index, 64)
        normal, inverse = layer_stats(tokens[rows, :].astype(F32))
        total = middle[rows, :] + norm_back(back[rows, :], normal, inverse, gain_one)
        last[rows, :] = total.astype(BF16)

    repeat(0, seq_len // 64, first_norm_back)
    emit(12, last, input_grad)
    for copy in outgoing:
        copy.wait()


def layer(remote, tokens, cotangent, select, vectors, *sources):
    seq_len, width = tokens.shape
    spread = sources[2].shape[2]
    heads = width // HEAD_DIM
    anywhere = pl.BlockSpec(memory_space=pl.ANY)
    here = pl.BlockSpec(memory_space=pltpu.VMEM)
    shape = jax.ShapeDtypeStruct
    count = len(GROUPS)
    links = [pltpu.SemaphoreType.DMA((count, 28))] * 2 if remote else []
    return pl.pallas_call(
        functools.partial(layer_kernel, remote),
        out_shape=(
            shape((seq_len, width), BF16),
            shape((seq_len, width), BF16),
            shape((10, LANES, width), BF16),
            shape((2, LANES, spread), BF16),
        ),
        in_specs=[here] * 4 + [anywhere] * 4,
        out_specs=[anywhere] * 4,
        scratch_shapes=[
            pltpu.VMEM((12, LANES, width), BF16),
            pltpu.VMEM((4, width, width), BF16),
            pltpu.VMEM((2, width, spread), BF16),
            pltpu.VMEM((2, LANES, spread), BF16),
            pltpu.VMEM((seq_len, heads * LANES), BF16),
            pltpu.VMEM((seq_len, heads * LANES), BF16),
            pltpu.VMEM((seq_len, heads * LANES), BF16),
            pltpu.VMEM((seq_len, heads * LANES), BF16),
            pltpu.VMEM((seq_len, width), BF16),
            pltpu.VMEM((seq_len, width), BF16),
            pltpu.VMEM((seq_len, width), F32),
            pltpu.VMEM((seq_len, width), BF16),
            pltpu.VMEM((seq_len, width), F32),
            pltpu.VMEM((seq_len, width), F32),
            pltpu.VMEM((8, seq_len, LANES), BF16),
            pltpu.VMEM((2, seq_len, LANES), F32),
            pltpu.VMEM((2, seq_len, 512), BF16),
            pltpu.SemaphoreType.DMA((17,)),
            *links,
        ],
        compiler_params=pltpu.CompilerParams(
            has_side_effects=True,
            vmem_limit_bytes=64 * 1024 * 1024,
            collective_id=0 if remote else None,
        ),
        name="layer" if remote else "layer_alone",
    )(tokens, cotangent, select, vectors, *sources)


def per_device(
    tokens,
    cotangent,
    adapter_ids,
    gain_one,
    shift_one,
    gain_two,
    shift_two,
    qkv_weight,
    out_weight,
    mlp_first,
    mlp_second,
    down_narrow,
    down_wide,
    up_narrow,
    up_wide,
):
    width, features = tokens.shape[2], mlp_first.shape[1]
    shards = lax.axis_size("shard")
    ranks = down_narrow.shape[1] * shards
    select = (lax.broadcasted_iota(jnp.int32, (1, ranks), 1) // RANK == adapter_ids[0, 0]).astype(F32)
    vectors = jnp.stack([gain_one, shift_one, gain_two, shift_two])
    pad = ((0, 0), (0, 0), (0, -features % 256))
    sources = (
        jnp.concatenate([down_narrow[:3], up_narrow[:3], down_narrow[3:], up_narrow[3:], down_narrow[:2]]),
        jnp.concatenate([qkv_weight, out_weight[None]]),
        jnp.pad(jnp.stack([mlp_first, mlp_second.T]), pad),
        jnp.pad(jnp.stack([up_wide, down_wide]), pad),
    )
    remote = (lax.axis_size("rep"), shards) == (4, 8)
    if not remote:
        sources = [lax.all_gather(each, "shard", axis=1, tiled=True) for each in sources]
    output, input_grad, narrow_grads, wide_grads = layer(
        remote, tokens[0], cotangent[0], select, vectors, *sources
    )
    parts = [narrow_grads[index] for index in range(10)] + [wide_grads[0], wide_grads[1]]
    share = lax.psum_scatter(jnp.concatenate(parts, axis=1), "shard", scatter_dimension=0, tiled=True)
    total = lax.psum(share, "rep").astype(F32)
    narrows = total[:, : 10 * width].reshape(-1, 10, width).transpose(1, 0, 2)
    wides = total[:, 10 * width :].reshape(-1, 2, wide_grads.shape[2])[:, :, :features]
    return (output[None], input_grad[None], narrows[:5], wides[:, 1], narrows[5:], wides[:, 0])


def solution(mesh):
    return jax.shard_map(
        per_device,
        mesh=mesh,
        in_specs=(
            P(("rep", "shard"), None, None),
            P(("rep", "shard"), None, None),
            P(("rep", "shard"), None),
            P(),
            P(),
            P(),
            P(),
            P(None, "shard", None),
            P("shard", None),
            P("shard", None),
            P(None, "shard"),
            P(None, "shard", None),
            P("shard", None),
            P(None, "shard", None),
            P("shard", None),
        ),
        out_specs=(
            P(("rep", "shard"), None, None),
            P(("rep", "shard"), None, None),
            P(None, "shard", None),
            P("shard", None),
            P(None, "shard", None),
            P("shard", None),
        ),
        check_vma=False,
    )
```

```python
import functools

import jax
import jax.numpy as jnp
from jax import lax
from jax.experimental import pallas as pl
from jax.experimental.pallas import tpu as pltpu
from jax.sharding import PartitionSpec as P

HEAD_DIM = 72
RANK = 16
GELU_SCALE = 0.7978845608028654
GELU_CUBE = 0.044715
MESH = pl.DeviceIdType.MESH
LANES = 128
BF16 = jnp.bfloat16
F32 = jnp.float32
CUTS = [(0, 512), (512, 512), (1024, 512), (1536, 512), (2048, 128)]
GROUPS = [("narrow", 0), ("square", 0), ("square", 1), ("square", 2), ("wide", 0)] + [
    ("mlp", cut) for cut in range(len(CUTS))
]
WIDE_GROUP = 4


def dot_nn(left, right):
    return jnp.dot(left, right, preferred_element_type=F32)


def dot_nt(left, right):
    return lax.dot_general(left, right, (((1,), (1,)), ((), ())), preferred_element_type=F32)


def dot_tn(left, right):
    return lax.dot_general(left, right, (((0,), (0,)), ((), ())), preferred_element_type=F32)


def repeat(low, high, step):
    def body(index, carry):
        step(index)
        return carry

    lax.fori_loop(low, high, body, 0)


def rows_of(index, count):
    return pl.ds(pl.multiple_of(index * count, count), count)


def layer_stats(value):
    average = jnp.mean(value, axis=-1, keepdims=True)
    centred = value - average
    spread = jnp.mean(centred * centred, axis=-1, keepdims=True)
    inverse = lax.rsqrt(spread + 1e-06)
    return (centred * inverse, inverse)


def norm_back(gradient, normal_part, inverse, gain):
    scaled = gradient * gain
    return inverse * (
        scaled
        - jnp.mean(scaled, axis=-1, keepdims=True)
        - normal_part * jnp.mean(scaled * normal_part, axis=-1, keepdims=True)
    )


class Gather:
    def __init__(self, local, whole, send, receive):
        self.local, self.whole, self.send, self.receive = local, whole, send, receive
        rep, shard = lax.axis_index("rep"), lax.axis_index("shard")
        self.y, self.c = rep // 2, lax.rem(rep, 2)
        self.z, self.x = shard // 2, lax.rem(shard, 2)

    def piece(self, group, y, c, z, x, own=False):
        kind, part = group
        narrow, square, mlp, wide = self.local if own else self.whole
        shard, slot, quarter = 2 * z + x, 4 * x + z, 2 * y + c
        if kind == "narrow":
            three = pl.ds(3 * quarter, 3)
            return narrow.at[three] if own else narrow.at[three, rows_of(slot, 16)]
        if kind == "square":
            if own:
                return square.at[quarter, pl.ds(48 * part, 48)]
            return square.at[quarter, pl.ds(pl.multiple_of(144 * shard + 48 * part, 16), 48)]
        if kind == "mlp":
            start, width = CUTS[part]
            half = mlp.shape[2] // 2
            columns = pl.ds(pl.multiple_of(y * half + start, LANES), width)
            if own:
                return mlp.at[c, :, columns]
            return mlp.at[c, pl.ds(pl.multiple_of(144 * shard, 16), 144), columns]
        half = wide.shape[2] // 2
        columns = pl.ds(pl.multiple_of(y * half, LANES), half)
        return wide.at[c, :, columns] if own else wide.at[c, rows_of(slot, 16), columns]

    def device(self, y=None, c=None, z=None, x=None):
        y = self.y if y is None else y
        c = self.c if c is None else c
        z = self.z if z is None else z
        x = self.x if x is None else x
        return (2 * y + c, 2 * z + x)

    def source(self, hop):
        return lax.rem(self.z + 4 - hop, 4)

    def copy(self, at, slot, y, z, x, device, own=False):
        target = self.piece(GROUPS[at], y, self.c, z, x)
        start = self.piece(GROUPS[at], y, self.c, z, x, True) if own else target
        return pltpu.make_async_remote_copy(
            start,
            target,
            self.send.at[at, slot],
            self.receive.at[at, slot],
            device_id=device,
            device_id_type=MESH,
        )

    def along_z(self, at, hop):
        device = self.device(z=lax.rem(self.z + hop, 4))
        return self.copy(at, hop - 1, self.y, self.z, self.x, device, True)

    def over_x(self, at, hop, own=False):
        device = self.device(x=1 - self.x)
        return self.copy(at, 3 + hop, self.y, self.source(hop), self.x, device, own)

    def corner_here(self, at):
        return self.copy(at, 7, 1 - self.y, self.z, self.x, self.device(x=1 - self.x), True)

    def over_y(self, at, hop):
        device = self.device(y=1 - self.y)
        return self.copy(at, 7 + hop, self.y, self.source(hop), self.x, device)

    def corner_by_y(self, at, hop):
        device = self.device(y=1 - self.y)
        return self.copy(at, 10 + hop, self.y, self.source(hop), 1 - self.x, device)

    def corner_by_x(self, at, hop):
        device = self.device(x=1 - self.x)
        return self.copy(at, 10 + hop, 1 - self.y, self.source(hop), self.x, device)

    def to_core(self, at, slot, y, z, x):
        return self.copy(at, slot, y, z, x, self.device(c=1 - self.c))

    def core_z(self, at, hop):
        return self.to_core(at, 13 + hop, self.y, self.source(hop), self.x)

    def core_x(self, at, hop):
        return self.to_core(at, 17 + hop, self.y, self.source(hop), 1 - self.x)

    def core_here(self, at):
        return self.to_core(at, 21, 1 - self.y, self.z, 1 - self.x)

    def core_y(self, at, hop):
        return self.to_core(at, 21 + hop, 1 - self.y, self.source(hop), self.x)

    def core_corner(self, at, hop):
        return self.to_core(at, 24 + hop, 1 - self.y, self.source(hop), 1 - self.x)

    def barrier(self):
        ready = pltpu.get_barrier_semaphore()
        partners = [self.device(z=lax.rem(self.z + hop, 4)) for hop in (1, 2, 3)]
        partners += [self.device(x=1 - self.x), self.device(y=1 - self.y), self.device(c=1 - self.c)]
        partners.append(self.device(y=1 - self.y, c=1 - self.c))
        for partner in partners:
            pl.semaphore_signal(ready, 1, device_id=partner, device_id_type=MESH)
        pl.semaphore_wait(ready, len(partners))

    def stage_send(self, at):
        repeat(1, 4, lambda hop: self.along_z(at, hop).start())
        self.over_x(at, 0, True).start()
        self.corner_here(at).start()

    def stage_planes(self, at):
        def step(hop):
            self.along_z(at, hop).wait_recv()
            self.over_x(at, hop).start()
            self.over_y(at, hop).start()
            self.core_z(at, hop).start()

        repeat(1, 4, step)

    def stage_corners(self, at):
        by_x = at % 2
        self.over_x(at, 0, True).wait_recv()
        self.core_x(at, 0).start()
        self.corner_here(at).wait_recv()
        self.core_here(at).start()

        def step(hop, corner):
            self.over_y(at, hop).wait_recv()
            self.core_y(at, hop).start()
            self.over_x(at, hop).wait_recv()
            self.core_x(at, hop).start()
            corner(at, hop).start()

        if by_x:
            repeat(1, 1 + by_x, lambda hop: step(hop, self.corner_by_x))
        repeat(1 + by_x, 4, lambda hop: step(hop, self.corner_by_y))

    def stage_core(self, at):
        def step(hop):
            self.corner_by_y(at, hop).wait_recv()
            self.core_corner(at, hop).start()

        repeat(1, 4, step)

    def stage_arrived(self, at):
        self.core_x(at, 0).wait_recv()
        self.core_here(at).wait_recv()

        def step(hop):
            for copy in (self.core_z, self.core_x, self.core_y, self.core_corner):
                copy(at, hop).wait_recv()

        repeat(1, 4, step)

    def sent(self, at):
        def step(hop):
            for copy in (
                self.along_z,
                self.over_x,
                self.over_y,
                self.corner_by_y,
                self.core_z,
                self.core_x,
                self.core_y,
                self.core_corner,
            ):
                copy(at, hop).wait_send()

        repeat(1, 4, step)
        for copy in (self.over_x(at, 0), self.corner_here(at), self.core_x(at, 0), self.core_here(at)):
            copy.wait_send()

    def advance(self, tick):
        stages = (
            self.stage_arrived,
            self.stage_core,
            self.stage_corners,
            self.stage_planes,
            self.stage_send,
        )
        for lag, stage in zip((4, 3, 2, 1, 0), stages):
            if 0 <= tick - lag < len(GROUPS):
                stage(tick - lag)


class Reduce:
    def __init__(self, net, free, phases, send, receive):
        self.net, self.free, self.phases = net, free, phases
        self.send, self.receive = send, receive
        self.partners = [
            net.device(c=1 - net.c),
            net.device(y=1 - net.y),
            net.device(x=1 - net.x),
        ]
        self.partners += [net.device(z=lax.rem(net.z + hop, 4)) for hop in (1, 2, 3)]
        self.partners.append(net.device(y=1 - net.y, c=1 - net.c))
        self.open = [False] * len(self.partners)

    def offer(self):
        for index, partner in enumerate(self.partners):
            pl.semaphore_signal(self.free.at[(0, 1, 2, 5, 4, 3, 6)[index]], 1, device_id=partner, device_id_type=MESH)

    def accept(self, index):
        if not self.open[index]:
            self.open[index] = True
            pl.semaphore_wait(self.free.at[index], 1)

    def copy(self, at, slot, source, target, index):
        return pltpu.make_async_remote_copy(
            source,
            target,
            self.send.at[at, slot],
            self.receive.at[at, slot],
            device_id=self.partners[index],
            device_id_type=MESH,
        )

    def across_cores(self, at):
        phase = self.phases[at]
        return self.copy(at, 0, phase.both(1 - self.net.c), phase.from_core, 0)

    def across_y(self, at):
        phase, net = self.phases[at], self.net
        return self.copy(at, 1, phase.block(net.c, 1 - net.y), phase.from_y, 1)

    def across_x(self, at):
        phase, net = self.phases[at], self.net
        return self.copy(at, 2, phase.block(net.c, net.y).at[rows_of(1 - net.x, 64), :], phase.from_x, 2)

    def across_z(self, at, hop):
        phase, net = self.phases[at], self.net
        there = lax.rem(net.z + hop, 4)
        source = phase.block(net.c, net.y).at[pl.ds(pl.multiple_of(64 * net.x + 16 * there, 16), 16), :]
        return self.copy(at, 2 + hop, source, phase.from_z.at[pl.ds(16 * (hop - 1), 16), :], 2 + hop)

    def result(self, at, index):
        net = self.net
        mine = self.phases[at].result(2 * net.y + net.c)
        return self.copy(at, 6 + index, mine, mine, (0, 1, 6)[index])

    def start_cores(self, at):
        self.accept(0)
        self.across_cores(at).start()

    def start_y(self, at):
        phase, net = self.phases[at], self.net
        self.across_cores(at).wait_recv()
        for side in range(2):
            add_into(phase.block(net.c, side), phase.core_part(side))
        self.accept(1)
        self.across_y(at).start()

    def start_x(self, at):
        phase, net = self.phases[at], self.net
        self.across_y(at).wait_recv()
        add_into(phase.block(net.c, net.y), phase.from_y)
        self.accept(2)
        self.across_x(at).start()

    def start_z(self, at):
        phase, net = self.phases[at], self.net
        self.across_x(at).wait_recv()
        add_into(phase.block(net.c, net.y).at[rows_of(net.x, 64), :], phase.from_x)
        for hop in (1, 2, 3):
            self.accept(2 + hop)
            self.across_z(at, hop).start()

    def start_result(self, at):
        phase, net = self.phases[at], self.net
        for hop in (1, 2, 3):
            self.across_z(at, hop).wait_recv()
        mine = phase.block(net.c, net.y).at[pl.ds(pl.multiple_of(64 * net.x + 16 * net.z, 16), 16), :]
        total = mine[...].astype(F32)
        for hop in (0, 1, 2):
            total = total + phase.from_z[pl.ds(16 * hop, 16), :].astype(F32)
        phase.result(2 * net.y + net.c)[...] = total.astype(BF16)
        for index in range(3):
            self.accept((0, 1, 6)[index])
            self.result(at, index).start()

    def finish(self, at):
        for index in range(3):
            self.result(at, index).wait_recv()

    def sent(self, at):
        copies = [self.across_cores(at), self.across_y(at), self.across_x(at)]
        copies += [self.across_z(at, hop) for hop in (1, 2, 3)]
        copies += [self.result(at, index) for index in range(3)]
        for copy in copies:
            copy.wait_send()


class Phase:
    def __init__(self, both, block, from_core, core_part, from_y, from_x, from_z, result):
        self.both, self.block, self.from_core, self.core_part = both, block, from_core, core_part
        self.from_y, self.from_x, self.from_z, self.result = from_y, from_x, from_z, result


def add_into(target, other):
    def step(index):
        rows = rows_of(index, 32)
        target[rows, :] = (target[rows, :].astype(F32) + other[rows, :].astype(F32)).astype(BF16)

    repeat(0, target.shape[0] // 32, step)


def phases_of(mlp, wide, result_wide, result_narrow, result_square):
    width, half = result_narrow.shape[2], wide.shape[2] // 2
    part = result_square.shape[3]

    def stacked(which, row, column, count):
        def block(c, y):
            start = pl.multiple_of(row + 256 * c + 128 * y, LANES)
            return mlp.at[which, pl.ds(start, LANES), pl.ds(column, count)]

        def both(c):
            start = pl.multiple_of(row + 256 * c, LANES)
            return mlp.at[which, pl.ds(start, 256), pl.ds(column, count)]

        return both, block

    def spot(which, row, rows, column, count):
        return mlp.at[which, pl.ds(row, rows), pl.ds(column, count)]

    def sides(ref):
        return lambda side: ref.at[pl.ds(LANES * side, LANES), :]

    arrived = spot(0, 1024, LANES, 0, 2 * half)
    phases = [
        Phase(
            lambda c: wide.at[c],
            lambda c, y: wide.at[c, :, pl.ds(pl.multiple_of(y * half, LANES), half)],
            arrived,
            lambda side: arrived.at[:, pl.ds(half * side, half)],
            spot(1, 1024, LANES, 0, half),
            spot(1, 1024, 64, half, half),
            spot(1, 1088, 48, half, half),
            lambda quarter: result_wide.at[quarter],
        )
    ]
    both, block = stacked(1, 512, width, width)
    received = spot(1, 512, 256, 2 * width, width)
    phases.append(
        Phase(
            both,
            block,
            received,
            sides(received),
            spot(1, 768, LANES, 2 * width, width),
            spot(1, 896, 64, 2 * width, width),
            spot(1, 960, 48, 2 * width, width),
            lambda quarter: result_narrow.at[quarter],
        )
    )
    for member in range(2):
        both, block = stacked(0, 512, 2048 + part * member, part)
        received = spot(1, 256 * member, 256, 3 * width, part)
        phases.append(
            Phase(
                both,
                block,
                received,
                sides(received),
                spot(1, 512 + LANES * member, LANES, 3 * width, part),
                spot(1, 768 + 64 * member, 64, 3 * width, part),
                spot(1, 896 + 48 * member, 48, 3 * width, part),
                lambda quarter, member=member: result_square.at[member, quarter],
            )
        )
    return phases


def layer_kernel(
    remote,
    tokens,
    cotangent,
    select,
    vectors,
    narrow_from,
    square_from,
    mlp_from,
    wide_from,
    output,
    input_grad,
    grads_one,
    grads_two,
    grads_three,
    grads_four,
    narrow,
    square,
    mlp,
    wide,
    query,
    key,
    value,
    mixed,
    normed,
    attended,
    middle,
    normed_two,
    after,
    back,
    small,
    sums,
    hidden,
    result_wide,
    result_narrow,
    result_square,
    local_sem,
    *link_sems,
):
    sources = (narrow_from, square_from, mlp_from, wide_from)
    wholes = (narrow, square, mlp, wide)
    seq_len, width = tokens.shape
    heads = width // HEAD_DIM
    scaling = HEAD_DIM ** (-0.5)
    block = 256
    blocks = seq_len // block
    half = mlp.shape[2] // 2
    if remote:
        net = Gather(sources, wholes, *link_sems[:2])
        own = []
        slots = (4 * net.x + net.z, 2 * net.z + net.x)
        for index, (source, whole) in enumerate(zip(sources, wholes)):
            place = whole.at[:, rows_of(slots[index in (1, 2)], source.shape[1])]
            own.append(pltpu.make_async_copy(source, place, local_sem.at[index]))
        advance, sent = net.advance, net.sent
        net.barrier()
    else:
        own = [
            pltpu.make_async_copy(source, whole, local_sem.at[index])
            for index, (source, whole) in enumerate(zip(sources, wholes))
        ]
        advance = sent = lambda at: None
    gain_one, shift_one = vectors[0:1, :], vectors[1:2, :]
    gain_two, shift_two = vectors[2:3, :], vectors[3:4, :]
    chosen = select[...]

    advance(0)
    advance(1)
    for copy in own:
        copy.start()

    def first_norm(index):
        rows = rows_of(index, 64)
        normal, _ = layer_stats(tokens[rows, :].astype(F32))
        normed[rows, :] = (normal * gain_one + shift_one).astype(BF16)

    repeat(0, seq_len // 64, first_norm)
    lane = lax.rem(lax.broadcasted_iota(jnp.int32, (64, heads * LANES), 1), LANES)
    minus = jnp.where((lane >= HEAD_DIM) & (lane < HEAD_DIM + 3), -1.0, 0.0).astype(BF16)

    def clear(index):
        rows = rows_of(index, 64)
        query[rows, :] = jnp.zeros_like(minus)
        value[rows, :] = jnp.zeros_like(minus)
        key[rows, :] = minus

    repeat(0, seq_len // 64, clear)
    for tick in range(2, 8):
        advance(tick)
    for copy in own:
        copy.wait()

    for member, padded in enumerate((query, key, value)):

        def project(index):
            rows = rows_of(index, block)
            lines = normed[rows, :]
            inner = (dot_nt(lines, narrow[member]) * chosen).astype(BF16)
            small[member, rows, :] = inner
            attended[rows, :] = (
                dot_nn(lines, square[member]) + dot_nn(inner, narrow[3 + member])
            ).astype(BF16)

        repeat(0, blocks, project)
        for head in range(heads):
            padded[:, LANES * head : LANES * head + HEAD_DIM] = attended[
                :, HEAD_DIM * head : HEAD_DIM * (head + 1)
            ]
    advance(8)

    lane = lax.broadcasted_iota(jnp.int32, (block, LANES), 1)

    def attend(head):
        columns = rows_of(head, LANES)
        for part in range(blocks):
            rows = pl.ds(part * block, block)
            lines = query[rows, columns]
            scores = dot_nt(lines, key[:, columns])
            top = jnp.max(scores, axis=-1, keepdims=True)
            exponent = jnp.exp((scores - top) * scaling)
            total = jnp.sum(exponent, axis=-1, keepdims=True)
            probs = (exponent * (1.0 / total)).astype(BF16)
            mixed[rows, columns] = dot_nn(probs, value[:, columns]).astype(BF16)
            level = top + jnp.log(total) * (1.0 / scaling)
            high = level.astype(BF16).astype(F32)
            mid = (level - high).astype(BF16).astype(F32)
            low = level - high - mid
            kept = jnp.where(lane == HEAD_DIM, high, lines.astype(F32))
            kept = jnp.where(lane == HEAD_DIM + 1, mid, kept)
            kept = jnp.where(lane == HEAD_DIM + 2, low, kept)
            query[rows, columns] = kept.astype(BF16)

    repeat(0, heads // 2, attend)
    advance(9)
    repeat(heads // 2, heads, attend)
    for head in range(heads):
        attended[:, HEAD_DIM * head : HEAD_DIM * (head + 1)] = mixed[
            :, LANES * head : LANES * head + HEAD_DIM
        ]

    def branch_out(index):
        rows = rows_of(index, block)
        lines = attended[rows, :]
        inner = (dot_nt(lines, narrow[6]) * chosen).astype(BF16)
        small[3, rows, :] = inner
        total = tokens[rows, :].astype(F32) + (dot_nn(lines, square[3]) + dot_nn(inner, narrow[8]))
        middle[rows, :] = total
        normal, _ = layer_stats(total)
        lines = (normal * gain_two + shift_two).astype(BF16)
        normed_two[rows, :] = lines
        small[4, rows, :] = (dot_nt(lines, narrow[7]) * chosen).astype(BF16)
        small[5, rows, :] = (dot_nt(cotangent[rows, :], narrow[9]) * chosen).astype(BF16)
        after[rows, :] = jnp.zeros((block, width), F32)
        back[rows, :] = jnp.zeros((block, width), F32)
        sums[0, rows, :] = jnp.zeros((block, LANES), F32)
        sums[1, rows, :] = jnp.zeros((block, LANES), F32)

    repeat(0, blocks, branch_out)
    advance(10)
    sent(WIDE_GROUP)

    for cut, (start, count) in enumerate(CUTS):

        def piece(side):
            columns = pl.ds(pl.multiple_of(side * half + start, LANES), count)

            def lines_of(index):
                rows = rows_of(index, block)
                before = dot_nn(normed_two[rows, :], mlp[0, :, columns])
                before = before + dot_nn(small[4, rows, :], wide[0, :, columns])
                square_of = before * before
                tangent = jnp.tanh(GELU_SCALE * (before + GELU_CUBE * square_of * before))
                active = (0.5 * before * (1.0 + tangent)).astype(BF16)
                slope = 0.5 * (1.0 + tangent) + 0.5 * before * (1.0 - tangent * tangent) * (
                    GELU_SCALE * (1.0 + 3.0 * GELU_CUBE * square_of)
                )
                gradient = dot_nn(cotangent[rows, :], mlp[1, :, columns])
                gradient = gradient + dot_nn(small[5, rows, :], wide[1, :, columns])
                gradient = (gradient * slope).astype(BF16)
                hidden[0, rows, pl.ds(0, count)] = active
                hidden[1, rows, pl.ds(0, count)] = gradient
                after[rows, :] += dot_nt(active, mlp[1, :, columns])
                sums[0, rows, :] += dot_nt(active, wide[1, :, columns])
                back[rows, :] += dot_nt(gradient, mlp[0, :, columns])
                sums[1, rows, :] += dot_nt(gradient, wide[0, :, columns])

            repeat(0, blocks, lines_of)
            wide[1, :, columns] = dot_tn(small[5], hidden[0, :, pl.ds(0, count)]).astype(BF16)
            wide[0, :, columns] = dot_tn(small[4], hidden[1, :, pl.ds(0, count)]).astype(BF16)

        repeat(0, 2, piece)
        if cut < 3:
            advance(11 + cut)

    for at in range(len(GROUPS)):
        if at != WIDE_GROUP:
            sent(at)
    outgoing = []

    def emit(index, source, target):
        copy = pltpu.make_async_copy(source, target, local_sem.at[4 + index])
        copy.start()
        outgoing.append(copy)

    phases = phases_of(mlp, wide, result_wide, result_narrow, result_square)
    if remote:
        reduce = Reduce(net, link_sems[2], phases, *link_sems[3:])
        reduce.offer()
        reduce.start_cores(0)

    def act(stage, at):
        if remote:
            getattr(reduce, stage)(at)

    staged = mlp.at[1, pl.ds(512, seq_len), pl.ds(0, width)]

    def second_out(index):
        rows = rows_of(index, block)
        inner = (sums[0, rows, :] * chosen).astype(BF16)
        small[6, rows, :] = inner
        staged[rows, :] = (middle[rows, :] + (after[rows, :] + dot_nn(inner, narrow[9]))).astype(BF16)
        small[7, rows, :] = (sums[1, rows, :] * chosen).astype(BF16)

    repeat(0, blocks, second_out)
    emit(11, staged, output)
    phases[1].block(0, 0)[...] = dot_tn(small[7], normed_two[...]).astype(BF16)
    phases[1].block(0, 1)[...] = dot_tn(small[6], cotangent[...]).astype(BF16)
    act("start_y", 0)

    def second_norm_back(index):
        rows = rows_of(index, block)
        gradient = back[rows, :] + dot_nn(small[7, rows, :], narrow[7])
        normal, inverse = layer_stats(middle[rows, :])
        total = cotangent[rows, :].astype(F32) + norm_back(gradient, normal, inverse, gain_two)
        middle[rows, :] = total
        normed_two[rows, :] = total.astype(BF16)

    repeat(0, blocks, second_norm_back)
    flat = [mlp.at[1, pl.ds(0, seq_len), pl.ds(width * member, width)] for member in range(3)]

    def branch_back(index):
        rows = rows_of(index, block)
        lines = normed_two[rows, :]
        inner = (dot_nt(lines, narrow[8]) * chosen).astype(BF16)
        small[4, rows, :] = inner
        flat[0][rows, :] = (dot_nt(lines, square[3]) + dot_nn(inner, narrow[6])).astype(BF16)

    repeat(0, blocks, branch_back)
    phases[1].block(1, 0)[...] = dot_tn(small[4], attended[...]).astype(BF16)
    phases[1].block(1, 1)[...] = dot_tn(small[3], normed_two[...]).astype(BF16)
    act("start_cores", 1)
    for head in range(heads):
        mixed[:, LANES * head : LANES * head + HEAD_DIM] = flat[0][
            :, HEAD_DIM * head : HEAD_DIM * (head + 1)
        ]
    spread = heads * LANES
    grads = [
        mlp.at[0, pl.ds(0, seq_len), pl.ds(0, spread)],
        mlp.at[0, pl.ds(0, seq_len), pl.ds(spread, spread)],
        mlp.at[0, pl.ds(512, seq_len), pl.ds(0, spread)],
    ]

    def attend_back(head):
        columns = rows_of(head, LANES)
        lines, keys = query[:, columns], key[:, columns]
        gradient = mixed[:, columns]
        probs = jnp.exp(dot_nt(keys, lines) * scaling)
        grad_probs = dot_nt(value[:, columns], gradient)
        level = jnp.sum(probs * grad_probs, axis=0, keepdims=True)
        grad_scores = (probs * (grad_probs - level)).astype(BF16)
        grads[2][:, columns] = dot_nn(probs.astype(BF16), gradient).astype(BF16)
        grads[1][:, columns] = (dot_nn(grad_scores, lines) * scaling).astype(BF16)
        grads[0][:, columns] = (dot_tn(grad_scores, keys) * scaling).astype(BF16)

    quarter = heads // 4
    repeat(0, quarter, attend_back)
    act("start_x", 0)
    act("start_y", 1)
    repeat(quarter, 2 * quarter, attend_back)
    act("start_z", 0)
    act("start_x", 1)
    repeat(2 * quarter, 3 * quarter, attend_back)
    act("start_result", 0)
    act("start_z", 1)
    repeat(3 * quarter, heads, attend_back)
    act("start_result", 1)
    part = result_square.shape[3]

    def put_square(side, member, value):
        for index in range(4):
            low, high = max(index * part, member * width), min((index + 1) * part, (member + 1) * width)
            if low < high:
                block = phases[2 + index % 2].block(index // 2, side)
                block[:, low - index * part : high - index * part] = value[
                    :, low - member * width : high - member * width
                ]

    for side in range(2):
        phases[3].block(1, side)[:, 3 * width - 3 * part :] = jnp.zeros((LANES, 4 * part - 3 * width), BF16)
    for member in range(3):
        for head in range(heads):
            flat[member][:, HEAD_DIM * head : HEAD_DIM * (head + 1)] = grads[member][
                :, LANES * head : LANES * head + HEAD_DIM
            ]

        def inner_back(index):
            rows = rows_of(index, block)
            inner = (dot_nt(flat[member][rows, :], narrow[3 + member]) * chosen).astype(BF16)
            small[4 + member, rows, :] = inner

        repeat(0, blocks, inner_back)
        put_square(0, member, dot_tn(small[4 + member], normed[...]).astype(BF16))
        put_square(1, member, dot_tn(small[member], flat[member][...]).astype(BF16))
    act("start_cores", 2)
    act("start_cores", 3)
    act("finish", 0)
    act("finish", 1)
    for member in range(3):

        def project_back(index):
            rows = rows_of(index, block)
            total = dot_nt(flat[member][rows, :], square[member])
            total = total + dot_nn(small[4 + member, rows, :], narrow[member])
            back[rows, :] = total if member == 0 else back[rows, :] + total

        repeat(0, blocks, project_back)
        for at in (2, 3):
            act(("start_y", "start_x", "start_z")[member], at)
    last = normed_two

    def first_norm_back(index):
        rows = rows_of(index, 64)
        normal, inverse = layer_stats(tokens[rows, :].astype(F32))
        total = middle[rows, :] + norm_back(back[rows, :], normal, inverse, gain_one)
        last[rows, :] = total.astype(BF16)

    repeat(0, seq_len // 64, first_norm_back)
    emit(12, last, input_grad)
    if remote:
        for at in (2, 3):
            reduce.start_result(at)
        far = grads_two.shape[1] - half
        for which, grad in ((1, grads_two), (0, grads_four)):
            grad[:, :half] = result_wide[which].astype(F32)
            grad[:, half:] = result_wide[2 + which, :, :far].astype(F32)
        for side, grad in ((0, grads_one), (1, grads_three)):
            grad[4] = result_narrow[2 * side].astype(F32)
            grad[3] = result_narrow[2 * side + 1].astype(F32)
        for at in (2, 3):
            reduce.finish(at)
        for side, grad in ((0, grads_one), (1, grads_three)):
            for member in range(3):
                for index in range(4):
                    low, high = max(index * part, member * width), min((index + 1) * part, (member + 1) * width)
                    if low < high:
                        grad[member, :, low - member * width : high - member * width] = result_square[
                            index % 2, 2 * side + index // 2, :, low - index * part : high - index * part
                        ].astype(F32)
        for at in range(4):
            reduce.sent(at)
    else:
        emit(0, wide, grads_one)
        for index in range(4):
            c, y = index // 2, index % 2
            emit(1 + index, phases[1].block(c, y), grads_two.at[c, y])
            emit(5 + index, phases[2].block(c, y), grads_three.at[c, y])
            emit(13 + index, phases[3].block(c, y), grads_four.at[c, y])
    for copy in outgoing:
        copy.wait()


def layer(remote, features, tokens, cotangent, select, vectors, *sources):
    seq_len, width = tokens.shape
    spread = sources[2].shape[2]
    heads = width // HEAD_DIM
    anywhere = pl.BlockSpec(memory_space=pl.ANY)
    here = pl.BlockSpec(memory_space=pltpu.VMEM)
    shape = jax.ShapeDtypeStruct
    count = len(GROUPS)
    part = 896
    links = []
    if remote:
        links = [pltpu.SemaphoreType.DMA((count, 28))] * 2 + [pltpu.SemaphoreType.REGULAR((7,))]
        links += [pltpu.SemaphoreType.DMA((4, 9))] * 2
        grads = (
            shape((5, 16, width), F32),
            shape((16, features), F32),
            shape((5, 16, width), F32),
            shape((16, features), F32),
        )
    else:
        grads = (
            shape((2, LANES, spread), BF16),
            shape((2, 2, LANES, width), BF16),
            shape((2, 2, LANES, part), BF16),
            shape((2, 2, LANES, part), BF16),
        )
    return pl.pallas_call(
        functools.partial(layer_kernel, remote),
        out_shape=(
            shape((seq_len, width), BF16),
            shape((seq_len, width), BF16),
            *grads,
        ),
        in_specs=[here] * 4 + [anywhere] * 4,
        out_specs=[anywhere] * 2 + [here if remote else anywhere] * 4,
        scratch_shapes=[
            pltpu.VMEM((12, LANES, width), BF16),
            pltpu.VMEM((4, width, width), BF16),
            pltpu.VMEM((2, width, spread), BF16),
            pltpu.VMEM((2, LANES, spread), BF16),
            pltpu.VMEM((seq_len, heads * LANES), BF16),
            pltpu.VMEM((seq_len, heads * LANES), BF16),
            pltpu.VMEM((seq_len, heads * LANES), BF16),
            pltpu.VMEM((seq_len, heads * LANES), BF16),
            pltpu.VMEM((seq_len, width), BF16),
            pltpu.VMEM((seq_len, width), BF16),
            pltpu.VMEM((seq_len, width), F32),
            pltpu.VMEM((seq_len, width), BF16),
            pltpu.VMEM((seq_len, width), F32),
            pltpu.VMEM((seq_len, width), F32),
            pltpu.VMEM((8, seq_len, LANES), BF16),
            pltpu.VMEM((2, seq_len, LANES), F32),
            pltpu.VMEM((2, seq_len, 512), BF16),
            pltpu.VMEM((4, 16, spread // 2), BF16),
            pltpu.VMEM((4, 16, width), BF16),
            pltpu.VMEM((2, 4, 16, part), BF16),
            pltpu.SemaphoreType.DMA((21,)),
            *links,
        ],
        compiler_params=pltpu.CompilerParams(
            has_side_effects=True,
            vmem_limit_bytes=64 * 1024 * 1024,
            collective_id=0 if remote else None,
        ),
        name="layer" if remote else "layer_alone",
    )(tokens, cotangent, select, vectors, *sources)


def per_device(
    tokens,
    cotangent,
    adapter_ids,
    gain_one,
    shift_one,
    gain_two,
    shift_two,
    qkv_weight,
    out_weight,
    mlp_first,
    mlp_second,
    down_narrow,
    down_wide,
    up_narrow,
    up_wide,
):
    width, features = tokens.shape[2], mlp_first.shape[1]
    shards = lax.axis_size("shard")
    ranks = down_narrow.shape[1] * shards
    remote = (lax.axis_size("rep"), shards) == (4, 8)
    adapter = adapter_ids[0, 0]
    slot = 4 * (adapter % 2) + adapter // 2 if remote else adapter
    select = (lax.broadcasted_iota(jnp.int32, (1, ranks), 1) // RANK == slot).astype(F32)
    vectors = jnp.stack([gain_one, shift_one, gain_two, shift_two])
    pad = ((0, 0), (0, 0), (0, -features % 256))
    sources = (
        jnp.concatenate([down_narrow[:3], up_narrow[:3], down_narrow[3:], up_narrow[3:], down_narrow[:2]]),
        jnp.concatenate([qkv_weight, out_weight[None]]),
        jnp.pad(jnp.stack([mlp_first, mlp_second.T]), pad),
        jnp.pad(jnp.stack([up_wide, down_wide]), pad),
    )
    if not remote:
        sources = [lax.all_gather(each, "shard", axis=1, tiled=True) for each in sources]
    output, input_grad, *grads = layer(
        remote, features, tokens[0], cotangent[0], select, vectors, *sources
    )
    if not remote:
        grads = reduced(features, *grads)
    return (output[None], input_grad[None], *grads)


def reduced(features, wide, narrow, square, square_more):
    width = narrow.shape[3]
    downs, ups = [
        jnp.concatenate([square[0, side], square_more[0, side], square[1, side], square_more[1, side]], axis=1)
        for side in range(2)
    ]
    parts = [downs[:, : 3 * width], narrow[1, 0], narrow[0, 0], ups[:, : 3 * width], narrow[1, 1], narrow[0, 1]]
    parts = parts + [wide[1, :, :features], wide[0, :, :features]]
    share = lax.psum_scatter(jnp.concatenate(parts, axis=1), "shard", scatter_dimension=0, tiled=True)
    total = lax.psum(share, "rep").astype(F32)
    narrows = total[:, : 10 * width].reshape(-1, 10, width).transpose(1, 0, 2)
    wides = total[:, 10 * width :].reshape(-1, 2, features)
    return (narrows[:5], wides[:, 0], narrows[5:], wides[:, 1])


def solution(mesh):
    return jax.shard_map(
        per_device,
        mesh=mesh,
        in_specs=(
            P(("rep", "shard"), None, None),
            P(("rep", "shard"), None, None),
            P(("rep", "shard"), None),
            P(),
            P(),
            P(),
            P(),
            P(None, "shard", None),
            P("shard", None),
            P("shard", None),
            P(None, "shard"),
            P(None, "shard", None),
            P("shard", None),
            P(None, "shard", None),
            P("shard", None),
        ),
        out_specs=(
            P(("rep", "shard"), None, None),
            P(("rep", "shard"), None, None),
            P(None, "shard", None),
            P("shard", None),
            P(None, "shard", None),
            P("shard", None),
        ),
        check_vma=False,
    )
```

```python
import functools

import jax
import jax.numpy as jnp
from jax import lax
from jax.experimental import pallas as pl
from jax.experimental.pallas import tpu as pltpu
from jax.sharding import PartitionSpec as P

HEAD_DIM = 72
RANK = 16
GELU_SCALE = 0.7978845608028654
GELU_CUBE = 0.044715
MESH = pl.DeviceIdType.MESH
LANES = 128
BF16 = jnp.bfloat16
F32 = jnp.float32
CUTS = [(0, 1024), (1024, 1024), (2048, 1024), (3072, 1024), (4096, 256)]
CROSSED, PLAIN = 768, 256
GROUPS = [("down", 0, False), ("up", 0, False)]
GROUPS += [("square", part, True) for part in range(3)]
GROUPS += [("wide", 0, False)]
BATCHES = [[2, 0], [3, 1], [4, 5]]
for each in range(len(CUTS)):
    BATCHES.append([])
    if CUTS[each][1] > PLAIN:
        BATCHES[-1].append(len(GROUPS))
        GROUPS.append(("mlp", each, True))
    BATCHES[-1].append(len(GROUPS))
    GROUPS.append(("mlp", each, False))
FIRST_CUT = 3
WIDE_PARTS, NARROW_PARTS = (1152, 1024), (640, 512)
SQUARE_PHASE = 4
LAG = 3
AHEAD = 1


def dot_nn(left, right):
    return jnp.dot(left, right, preferred_element_type=F32)


def dot_nt(left, right):
    return lax.dot_general(left, right, (((1,), (1,)), ((), ())), preferred_element_type=F32)


def dot_tn(left, right):
    return lax.dot_general(left, right, (((0,), (0,)), ((), ())), preferred_element_type=F32)


def repeat(low, high, step):
    def body(index, carry):
        step(index)
        return carry

    lax.fori_loop(low, high, body, 0)


def rows_of(index, count):
    return pl.ds(pl.multiple_of(index * count, count), count)


def layer_stats(value):
    average = jnp.mean(value, axis=-1, keepdims=True)
    centred = value - average
    spread = jnp.mean(centred * centred, axis=-1, keepdims=True)
    inverse = lax.rsqrt(spread + 1e-06)
    return (centred * inverse, inverse)


def norm_back(gradient, normal_part, inverse, gain):
    scaled = gradient * gain
    return inverse * (
        scaled
        - jnp.mean(scaled, axis=-1, keepdims=True)
        - normal_part * jnp.mean(scaled * normal_part, axis=-1, keepdims=True)
    )


class Gather:
    def __init__(self, whole, send, receive):
        self.whole, self.send, self.receive = whole, send, receive
        rep, shard = lax.axis_index("rep"), lax.axis_index("shard")
        self.y, self.c = rep // 2, lax.rem(rep, 2)
        self.z, self.x = shard // 2, lax.rem(shard, 2)

    def piece(self, at, y, c, z, x):
        kind, part, _ = GROUPS[at]
        square, down, mlp = self.whole
        width, depth = down.shape[2], down.shape[2]
        shard, slot = 2 * z + x, 4 * x + z
        extra = pl.ds(pl.multiple_of(depth + 16 * slot, 16), 16)
        if kind == "down":
            return down.at[pl.ds(3 * c, 3), rows_of(slot, 16)]
        if kind == "up":
            return square.at[extra, pl.ds(pl.multiple_of(2 * width * c, LANES), 2 * width)]
        if kind == "square":
            rows = pl.ds(pl.multiple_of(144 * shard + 48 * part, 16), 48)
            return square.at[rows, pl.ds(pl.multiple_of(width * (2 * y + c), LANES), width)]
        if kind == "wide":
            return mlp.at[c, extra, :]
        start, count = CUTS[part]
        rows = pl.ds(pl.multiple_of(144 * shard, 16), 144)
        if not GROUPS[at][2]:
            return mlp.at[c, rows, pl.ds(start + count - PLAIN, PLAIN)]
        return mlp.at[c, rows, pl.ds(pl.multiple_of(start + (CROSSED // 2) * y, LANES), CROSSED // 2)]

    def device(self, y=None, c=None, z=None, x=None):
        y = self.y if y is None else y
        c = self.c if c is None else c
        z = self.z if z is None else z
        x = self.x if x is None else x
        return (2 * y + c, 2 * z + x)

    def source(self, hop):
        return lax.rem(self.z + 4 - hop, 4)

    def copy(self, at, slot, y, z, x, device):
        piece = self.piece(at, y, self.c, z, x)
        return pltpu.make_async_remote_copy(
            piece,
            piece,
            self.send.at[at, slot],
            self.receive.at[at, slot],
            device_id=device,
            device_id_type=MESH,
        )

    def along_z(self, at, hop):
        return self.copy(at, hop - 1, self.y, self.z, self.x, self.device(z=lax.rem(self.z + hop, 4)))

    def over_x(self, at, hop):
        return self.copy(at, 3 + hop, self.y, self.source(hop), self.x, self.device(x=1 - self.x))

    def over_y(self, at, hop):
        return self.copy(at, 6 + hop, self.y, self.source(hop), self.x, self.device(y=1 - self.y))

    def corner(self, at, hop):
        return self.copy(at, 10 + hop, self.y, self.source(hop), 1 - self.x, self.device(y=1 - self.y))

    def to_core(self, at, slot, y, hop, x):
        return self.copy(at, slot, y, self.source(hop), x, self.device(c=1 - self.c))

    def core_z(self, at, hop):
        return self.to_core(at, 13 + hop, self.y, hop, self.x)

    def core_x(self, at, hop):
        return self.to_core(at, 17 + hop, self.y, hop, 1 - self.x)

    def core_y(self, at, hop):
        return self.to_core(at, 20 + hop, 1 - self.y, hop, self.x)

    def core_corner(self, at, hop):
        return self.to_core(at, 24 + hop, 1 - self.y, hop, 1 - self.x)

    def greet(self):
        ready = pltpu.get_barrier_semaphore()
        partners = [self.device(z=lax.rem(self.z + hop, 4)) for hop in (1, 2, 3)]
        partners += [self.device(x=1 - self.x), self.device(y=1 - self.y), self.device(c=1 - self.c)]
        partners.append(self.device(y=1 - self.y, c=1 - self.c))
        for partner in partners:
            pl.semaphore_signal(ready, 1, device_id=partner, device_id_type=MESH)
        pl.semaphore_wait(ready, len(partners))

    def stage_send(self, at):
        repeat(1, 4, lambda hop: self.along_z(at, hop).start())
        self.over_x(at, 0).start()

    def stage_planes(self, at):
        def step(hop):
            self.along_z(at, hop).wait_recv()
            self.over_x(at, hop).start()
            if GROUPS[at][2]:
                self.over_y(at, hop).start()
            self.core_z(at, hop).start()

        repeat(1, 4, step)

    def stage_corners(self, at):
        def step(hop):
            self.over_x(at, hop).wait_recv()
            if GROUPS[at][2]:
                self.corner(at, hop).start()
            self.core_x(at, hop).start()

        repeat(0, 4, step)

    def stage_core(self, at):
        def step(hop):
            self.over_y(at, hop).wait_recv()
            self.core_y(at, hop).start()

        def corner_step(hop):
            self.corner(at, hop).wait_recv()
            self.core_corner(at, hop).start()

        if GROUPS[at][2]:
            repeat(1, 4, step)
            repeat(0, 4, corner_step)

    def copies_of(self, at):
        links, cores = [(self.along_z, 1), (self.over_x, 0)], [(self.core_z, 1), (self.core_x, 0)]
        if GROUPS[at][2]:
            links += [(self.over_y, 1), (self.corner, 0)]
            cores += [(self.core_y, 1), (self.core_corner, 0)]
        return links, cores

    def arrived(self, at):
        for copy, first in self.copies_of(at)[1]:
            repeat(first, 4, lambda hop: copy(at, hop).wait_recv())

    def sent(self, at):
        links, cores = self.copies_of(at)
        for copy, first in links + cores:
            repeat(first, 4, lambda hop: copy(at, hop).wait_send())

    def advance(self, tick):
        stages = (
            self.stage_core,
            self.stage_corners,
            self.stage_planes,
            self.stage_send,
        )
        for lag, stage in zip((3, 2, 1, 0), stages):
            if 0 <= tick - lag < len(BATCHES):
                for at in BATCHES[tick - lag]:
                    stage(at)


class Reduce:
    def __init__(self, net, free, phases, send, receive):
        self.net, self.free, self.phases = net, free, phases
        self.send, self.receive = send, receive
        self.partners = [
            net.device(c=1 - net.c),
            net.device(y=1 - net.y),
            net.device(x=1 - net.x),
        ]
        self.partners += [net.device(z=lax.rem(net.z + hop, 4)) for hop in (1, 2, 3)]
        self.partners.append(net.device(y=1 - net.y, c=1 - net.c))
        self.open = [False] * len(self.partners)

    def offer(self):
        for index, partner in enumerate(self.partners):
            pl.semaphore_signal(self.free.at[(0, 1, 2, 5, 4, 3, 6)[index]], 1, device_id=partner, device_id_type=MESH)

    def accept(self, index):
        if not self.open[index]:
            self.open[index] = True
            pl.semaphore_wait(self.free.at[index], 1)

    def copy(self, at, slot, source, target, index):
        return pltpu.make_async_remote_copy(
            source,
            target,
            self.send.at[at, slot],
            self.receive.at[at, slot],
            device_id=self.partners[index],
            device_id_type=MESH,
        )

    def across_cores(self, at):
        phase = self.phases[at]
        return self.copy(at, 0, phase.both(1 - self.net.c), phase.from_core, 0)

    def first_copies(self, at):
        phase, net = self.phases[at], self.net
        if not phase.by_x:
            return [self.copy(at, 1, phase.block(net.c, 1 - net.y), phase.from_first, 1)]
        return [
            self.copy(
                at,
                1 + side,
                phase.block(net.c, side).at[rows_of(1 - net.x, 64), :],
                phase.from_first.at[pl.ds(64 * side, 64), :],
                2,
            )
            for side in range(2)
        ]

    def second_copy(self, at):
        phase, net = self.phases[at], self.net
        if phase.by_x:
            source = phase.block(net.c, 1 - net.y).at[rows_of(net.x, 64), :]
        else:
            source = phase.block(net.c, net.y).at[rows_of(1 - net.x, 64), :]
        return self.copy(at, 3, source, phase.from_second, 1 if phase.by_x else 2)

    def across_z(self, at, hop):
        phase, net = self.phases[at], self.net
        there = lax.rem(net.z + hop, 4)
        source = phase.block(net.c, net.y).at[pl.ds(pl.multiple_of(64 * net.x + 16 * there, 16), 16), :]
        return self.copy(at, 3 + hop, source, phase.from_z.at[pl.ds(16 * (hop - 1), 16), :], 2 + hop)

    def result(self, at, index):
        net = self.net
        mine = self.phases[at].result(2 * net.y + net.c)
        return self.copy(at, 7 + index, mine, mine, (0, 1, 6)[index])

    def start_cores(self, at):
        self.accept(0)
        self.across_cores(at).start()

    def start_first(self, at):
        phase, net = self.phases[at], self.net
        self.across_cores(at).wait_recv()
        for side in range(2):
            add_into(phase.block(net.c, side), phase.core_part(side))
        self.accept(2 if phase.by_x else 1)
        for copy in self.first_copies(at):
            copy.start()

    def start_second(self, at):
        phase, net = self.phases[at], self.net
        for copy in self.first_copies(at):
            copy.wait_recv()
        if phase.by_x:
            for side in range(2):
                rows = rows_of(net.x, 64)
                add_into(phase.block(net.c, side).at[rows, :], phase.from_first.at[pl.ds(64 * side, 64), :])
        else:
            add_into(phase.block(net.c, net.y), phase.from_first)
        self.accept(1 if phase.by_x else 2)
        self.second_copy(at).start()

    def start_z(self, at):
        phase, net = self.phases[at], self.net
        self.second_copy(at).wait_recv()
        add_into(phase.block(net.c, net.y).at[rows_of(net.x, 64), :], phase.from_second)
        for hop in (1, 2, 3):
            self.accept(2 + hop)
            self.across_z(at, hop).start()

    def start_result(self, at):
        phase, net = self.phases[at], self.net
        for hop in (1, 2, 3):
            self.across_z(at, hop).wait_recv()
        mine = phase.block(net.c, net.y).at[pl.ds(pl.multiple_of(64 * net.x + 16 * net.z, 16), 16), :]
        total = mine[...].astype(F32)
        for hop in (0, 1, 2):
            total = total + phase.from_z[pl.ds(16 * hop, 16), :].astype(F32)
        phase.result(2 * net.y + net.c)[...] = total.astype(BF16)
        for index in range(3):
            self.accept((0, 1, 6)[index])
            self.result(at, index).start()

    def finish(self, at):
        for index in range(3):
            self.result(at, index).wait_recv()

    def sent(self, at):
        copies = [self.across_cores(at), *self.first_copies(at), self.second_copy(at)]
        copies += [self.across_z(at, hop) for hop in (1, 2, 3)]
        copies += [self.result(at, index) for index in range(3)]
        for copy in copies:
            copy.wait_send()


class Phase:
    def __init__(self, by_x, both, block, from_core, core_part, from_first, from_second, from_z, result):
        self.by_x, self.both, self.block = by_x, both, block
        self.from_core, self.core_part, self.result = from_core, core_part, result
        self.from_first, self.from_second, self.from_z = from_first, from_second, from_z


def add_into(target, other):
    def step(index):
        rows = rows_of(index, 32)
        target[rows, :] = (target[rows, :].astype(F32) + other[rows, :].astype(F32)).astype(BF16)

    repeat(0, target.shape[0] // 32, step)


def phases_of(mlp, result_wide, result_narrow, result_square):
    width = mlp.shape[1] - LANES
    part = result_square.shape[3]
    phases = []

    def spot(which, row, rows, column, count):
        return mlp.at[which, pl.ds(row, rows), pl.ds(column, count)]

    def wide_phase(by_x, first, count, column, result):
        def block(c, y):
            columns = pl.ds(pl.multiple_of(first + y * count, LANES), count)
            return mlp.at[c, pl.ds(width, LANES), columns]

        arrived = spot(0, 1024, LANES, first, 2 * count)
        phases.append(
            Phase(
                by_x,
                lambda c: mlp.at[c, pl.ds(width, LANES), pl.ds(first, 2 * count)],
                block,
                arrived,
                lambda side: arrived.at[:, pl.ds(count * side, count)],
                spot(1, 1024, LANES, column, count),
                spot(1, 1024, 64, 2176 + column, count),
                spot(1, 1088, 48, 2176 + column, count),
                result,
            )
        )

    def stacked_phase(by_x, which, row, column, count, land, places, result):
        def block(c, y):
            start = pl.multiple_of(row + 256 * c + LANES * y, LANES)
            return mlp.at[which, pl.ds(start, LANES), pl.ds(column, count)]

        def both(c):
            start = pl.multiple_of(row + 256 * c, LANES)
            return mlp.at[which, pl.ds(start, 256), pl.ds(column, count)]

        arrived = spot(1, places[0], 256, land, count)
        phases.append(
            Phase(
                by_x,
                both,
                block,
                arrived,
                lambda side: arrived.at[pl.ds(LANES * side, LANES), :],
                spot(1, places[1], LANES, land, count),
                spot(1, places[2], 64, land, count),
                spot(1, places[3], 48, land, count),
                result,
            )
        )

    wide_first = WIDE_PARTS[0]
    wide_phase(False, 0, wide_first, 0, lambda quarter: result_wide.at[quarter, :, pl.ds(0, wide_first)])
    wide_phase(
        True,
        2 * wide_first,
        WIDE_PARTS[1],
        wide_first,
        lambda quarter: result_wide.at[quarter, :, pl.ds(wide_first, WIDE_PARTS[1])],
    )
    start = 0
    for by_x, count in enumerate(NARROW_PARTS):
        stacked_phase(
            bool(by_x),
            1,
            512,
            width + start,
            count,
            2 * width + start,
            (512, 768, 896, 960),
            lambda quarter, columns=pl.ds(start, count): result_narrow.at[quarter, :, columns],
        )
        start += count
    for member in range(2):
        stacked_phase(
            bool(member),
            0,
            512,
            2048 + part * member,
            part,
            3 * width,
            (256 * member, 512 + LANES * member, 768 + 64 * member, 896 + 48 * member),
            lambda quarter, member=member: result_square.at[member, quarter],
        )
    return phases


def layer_kernel(
    remote,
    tokens,
    cotangent_from,
    adapter,
    gain_one_from,
    shift_one_from,
    gain_two_from,
    shift_two_from,
    qkv_from,
    out_from,
    down_from,
    up_from,
    mlp_from,
    output,
    input_grad,
    grads_one,
    grads_two,
    grads_three,
    grads_four,
    square,
    down,
    mlp,
    query,
    key,
    value,
    mixed,
    normed,
    attended,
    normed_two,
    cotangent,
    middle,
    after,
    back,
    inner,
    inner_back,
    hidden,
    result_wide,
    result_narrow,
    result_square,
    local_sem,
    *link_sems,
):
    seq_len, width = tokens.shape
    heads = width // HEAD_DIM
    scaling = HEAD_DIM ** (-0.5)
    block = 256
    blocks = seq_len // block
    side_columns = pl.ds(width, LANES)
    main = pl.ds(0, width)

    if remote:
        net = Gather((square, down, mlp), *link_sems[:2])
        shard, slot = 2 * net.z + net.x, 4 * net.x + net.z
        advance, arrived, sent = net.advance, net.arrived, net.sent
        number = 4 * lax.rem(adapter[0, 0], 2) + adapter[0, 0] // 2
    else:
        shard = slot = 0
        advance = arrived = sent = lambda at: None
        number = adapter[0, 0]
    ranks = lax.broadcasted_iota(jnp.int32, (1, LANES), 1)
    chosen = jnp.where((ranks >= number * RANK) & (ranks < (number + 1) * RANK), 1.0, 0.0)

    own = []

    def bring(source, target):
        copy = pltpu.make_async_copy(source, target, local_sem.at[len(own)])
        copy.start()
        own.append(copy)

    rank_rows = rows_of(slot, down_from.shape[1])
    extra_rows = pl.ds(pl.multiple_of(width + down_from.shape[1] * slot, 16), down_from.shape[1])
    depth_rows = rows_of(shard, out_from.shape[0])
    bring(down_from, down.at[pl.ds(0, 5), rank_rows])
    bring(up_from.at[4], down.at[5, rank_rows])
    for member in range(4):
        bring(up_from.at[member], square.at[extra_rows, pl.ds(member * width, width)])
    for member in range(3):
        bring(qkv_from.at[member], square.at[depth_rows, pl.ds(member * width, width)])
    bring(out_from, square.at[depth_rows, pl.ds(3 * width, width)])
    bring(mlp_from.at[:, pl.ds(out_from.shape[0], down_from.shape[1]), :], mlp.at[:, extra_rows, :])
    bring(mlp_from.at[:, pl.ds(0, out_from.shape[0]), :], mlp.at[:, depth_rows, :])
    bring(cotangent_from, cotangent.at[:, main])
    if remote:
        net.greet()
    for copy in own:
        copy.wait()
    advance(0)

    gain_one, shift_one, gain_two, shift_two = [
        each[...].reshape(1, width) for each in (gain_one_from, shift_one_from, gain_two_from, shift_two_from)
    ]

    def first_norm(index):
        rows = rows_of(index, 64)
        normal, _ = layer_stats(tokens[rows, :].astype(F32))
        normed[rows, main] = (normal * gain_one + shift_one).astype(BF16)

    repeat(0, seq_len // 64, first_norm)
    advance(1)
    lane = lax.rem(lax.broadcasted_iota(jnp.int32, (64, heads * LANES), 1), LANES)
    minus = jnp.where((lane >= HEAD_DIM) & (lane < HEAD_DIM + 3), -1.0, 0.0).astype(BF16)

    def clear(index):
        rows = rows_of(index, 64)
        query[rows, :] = jnp.zeros_like(minus)
        value[rows, :] = jnp.zeros_like(minus)
        key[rows, :] = minus

    repeat(0, seq_len // 64, clear)
    advance(2)
    arrived(0)

    def inner_of(index):
        rows = rows_of(index, block)
        three = dot_nt(normed[rows, main], down[0:3].reshape(3 * LANES, width))
        inner[rows, :] = (three * jnp.concatenate([chosen] * 3, axis=1)).astype(BF16)

        lines = dot_nt(cotangent[rows, main], down[5])
        cotangent[rows, side_columns] = (lines * chosen).astype(BF16)

    repeat(0, blocks, inner_of)
    for tick in range(3, FIRST_CUT + LAG):
        advance(tick)
    for at in range(1, BATCHES[FIRST_CUT][0]):
        arrived(at)

    for member, padded in enumerate((query, key, value)):

        def project(index):
            rows = rows_of(index, block)
            normed[rows, side_columns] = inner[rows, pl.ds(member * LANES, LANES)]
            lines = dot_nn(normed[rows, :], square[:, pl.ds(member * width, width)])
            attended[rows, main] = lines.astype(BF16)

        repeat(0, blocks, project)
        for head in range(heads):
            padded[:, LANES * head : LANES * head + HEAD_DIM] = attended[
                :, HEAD_DIM * head : HEAD_DIM * (head + 1)
            ]
    tick = FIRST_CUT + LAG
    advance(tick)

    lane = lax.broadcasted_iota(jnp.int32, (block, LANES), 1)

    def attend(head):
        columns = rows_of(head, LANES)
        for part in range(blocks):
            rows = pl.ds(part * block, block)
            lines = query[rows, columns]
            scores = dot_nt(lines, key[:, columns])
            top = jnp.max(scores, axis=-1, keepdims=True)
            exponent = jnp.exp((scores - top) * scaling)
            total = jnp.sum(exponent, axis=-1, keepdims=True)
            probs = (exponent * (1.0 / total)).astype(BF16)
            mixed[rows, columns] = dot_nn(probs, value[:, columns]).astype(BF16)
            level = top + jnp.log(total) * (1.0 / scaling)
            high = level.astype(BF16).astype(F32)
            mid = (level - high).astype(BF16).astype(F32)
            low = level - high - mid
            kept = jnp.where(lane == HEAD_DIM, high, lines.astype(F32))
            kept = jnp.where(lane == HEAD_DIM + 1, mid, kept)
            kept = jnp.where(lane == HEAD_DIM + 2, low, kept)
            query[rows, columns] = kept.astype(BF16)

    repeat(0, heads // 2, attend)
    tick += 1
    advance(tick)
    repeat(heads // 2, heads, attend)
    for head in range(heads):
        attended[:, HEAD_DIM * head : HEAD_DIM * (head + 1)] = mixed[
            :, LANES * head : LANES * head + HEAD_DIM
        ]

    def branch_out(index):
        rows = rows_of(index, block)
        attended[rows, side_columns] = (dot_nt(attended[rows, main], down[3]) * chosen).astype(BF16)
        total = tokens[rows, :].astype(F32) + dot_nn(attended[rows, :], square[:, pl.ds(3 * width, width)])
        middle[rows, :] = total
        normal, _ = layer_stats(total)
        lines = (normal * gain_two + shift_two).astype(BF16)
        normed_two[rows, main] = lines
        normed_two[rows, side_columns] = (dot_nt(lines, down[4]) * chosen).astype(BF16)

    repeat(0, blocks, branch_out)
    for at in range(BATCHES[FIRST_CUT][0]):
        sent(at)

    for cut, (start, count) in enumerate(CUTS):
        columns = pl.ds(start, count)
        while tick < min(FIRST_CUT + LAG + cut + AHEAD, len(BATCHES) + LAG - 1):
            tick += 1
            advance(tick)
        for at in BATCHES[FIRST_CUT + cut]:
            arrived(at)

        def lines_of(index):
            rows = rows_of(index, block)
            before = dot_nn(normed_two[rows, :], mlp[0, :, columns])
            square_of = before * before
            tangent = jnp.tanh(GELU_SCALE * (before + GELU_CUBE * square_of * before))
            active = (0.5 * before * (1.0 + tangent)).astype(BF16)
            slope = 0.5 * (1.0 + tangent) + 0.5 * before * (1.0 - tangent * tangent) * (
                GELU_SCALE * (1.0 + 3.0 * GELU_CUBE * square_of)
            )
            gradient = dot_nn(cotangent[rows, :], mlp[1, :, columns])
            gradient = (gradient * slope).astype(BF16)
            hidden[0, rows, pl.ds(0, count)] = active
            hidden[1, rows, pl.ds(0, count)] = gradient
            forward = dot_nt(active, mlp[1, :, columns])
            backward = dot_nt(gradient, mlp[0, :, columns])
            after[rows, :] = forward if cut == 0 else after[rows, :] + forward
            back[rows, :] = backward if cut == 0 else back[rows, :] + backward

        repeat(0, blocks, lines_of)
        for which, lines in ((1, cotangent), (0, normed_two)):
            mlp[which, pl.ds(width, LANES), columns] = dot_tn(
                lines[:, side_columns], hidden[1 - which, :, pl.ds(0, count)]
            ).astype(BF16)
        if cut == len(CUTS) - 2:
            for at in range(BATCHES[FIRST_CUT][0], BATCHES[-1][0]):
                sent(at)
    sent(len(GROUPS) - 1)

    outgoing = []

    def emit(source, target):
        copy = pltpu.make_async_copy(source, target, local_sem.at[len(own) + len(outgoing)])
        copy.start()
        outgoing.append(copy)

    phases = phases_of(mlp, result_wide, result_narrow, result_square)
    if remote:
        reduce = Reduce(net, link_sems[2], phases, *link_sems[3:])
        reduce.offer()
        reduce.start_cores(0)
        reduce.start_cores(1)

    def act(stage, at):
        if remote:
            getattr(reduce, stage)(at)

    staged = mlp.at[1, pl.ds(512, seq_len), main]
    branch = mlp.at[0, pl.ds(0, seq_len), main]
    flat = [mlp.at[1, pl.ds(0, seq_len), pl.ds(width * member, width)] for member in range(3)]
    flats = mlp.at[1, pl.ds(0, seq_len), pl.ds(0, 3 * width)]

    def second_norm_back(index):
        rows = rows_of(index, block)
        lines = (after[rows, side_columns] * chosen).astype(BF16)
        inner_back[rows, pl.ds(0, LANES)] = lines
        residual = middle[rows, :]
        staged[rows, :] = (residual + (after[rows, main] + dot_nn(lines, down[5]))).astype(BF16)
        lines = (back[rows, side_columns] * chosen).astype(BF16)
        inner_back[rows, pl.ds(LANES, LANES)] = lines
        gradient = back[rows, main] + dot_nn(lines, down[4])
        normal, inverse = layer_stats(residual)
        total = cotangent[rows, main].astype(F32) + norm_back(gradient, normal, inverse, gain_two)
        middle[rows, :] = total
        lines = total.astype(BF16)
        branch[rows, :] = lines
        both = dot_nt(lines, square[:, pl.ds(3 * width, width)])
        lines = (both[:, width:] * chosen).astype(BF16)
        inner_back[rows, pl.ds(2 * LANES, LANES)] = lines
        flat[0][rows, :] = (both[:, :width] + dot_nn(lines, down[3])).astype(BF16)

    repeat(0, blocks, second_norm_back)
    emit(staged, output)
    act("start_first", 0)
    act("start_first", 1)
    for head in range(heads):
        mixed[:, LANES * head : LANES * head + HEAD_DIM] = flat[0][
            :, HEAD_DIM * head : HEAD_DIM * (head + 1)
        ]
    narrow_blocks = mlp.at[1, pl.ds(512, 4 * LANES), pl.ds(width, width)]
    for index, (left, right) in enumerate(
        (
            (inner_back[:, pl.ds(LANES, LANES)], normed_two[:, main]),
            (inner_back[:, pl.ds(0, LANES)], cotangent[:, main]),
            (inner_back[:, pl.ds(2 * LANES, LANES)], attended[:, main]),
            (attended[:, side_columns], branch[...]),
        )
    ):
        narrow_blocks[pl.ds(LANES * index, LANES), :] = dot_tn(left, right).astype(BF16)
    act("start_cores", 2)
    act("start_cores", 3)
    spread = heads * LANES
    grads = [
        mlp.at[0, pl.ds(0, seq_len), pl.ds(0, spread)],
        mlp.at[0, pl.ds(0, seq_len), pl.ds(spread, spread)],
        mlp.at[0, pl.ds(512, seq_len), pl.ds(0, spread)],
    ]

    def attend_back(pair):
        for head in (2 * pair, 2 * pair + 1):
            columns = rows_of(head, LANES)
            lines, keys = query[:, columns], key[:, columns]
            gradient = mixed[:, columns]
            probs = jnp.exp(dot_nt(keys, lines) * scaling)
            grad_probs = dot_nt(value[:, columns], gradient)
            level = jnp.sum(probs * grad_probs, axis=0, keepdims=True)
            grad_scores = (probs * (grad_probs - level)).astype(BF16)
            grads[2][:, columns] = dot_nn(probs.astype(BF16), gradient).astype(BF16)
            grads[1][:, columns] = (dot_nn(grad_scores, lines) * scaling).astype(BF16)
            grads[0][:, columns] = (dot_tn(grad_scores, keys) * scaling).astype(BF16)

    repeat(0, 3, attend_back)
    for at in (0, 1):
        act("start_second", at)
    for at in (2, 3):
        act("start_first", at)
    repeat(3, 5, attend_back)
    for at in (0, 1):
        act("start_z", at)
    for at in (2, 3):
        act("start_second", at)
    repeat(5, heads // 2, attend_back)
    for at in (0, 1):
        act("start_result", at)
    for at in (2, 3):
        act("start_z", at)
    part = result_square.shape[3]

    def put_square(side, member, value):
        for index in range(4):
            low, high = max(index * part, member * width), min((index + 1) * part, (member + 1) * width)
            if low < high:
                place = phases[SQUARE_PHASE + index % 2].block(index // 2, side)
                place[:, low - index * part : high - index * part] = value[
                    :, low - member * width : high - member * width
                ]

    for side in range(2):
        phases[SQUARE_PHASE + 1].block(1, side)[:, 3 * width - 3 * part :] = jnp.zeros((LANES, 4 * part - 3 * width), BF16)
    for member in range(3):
        for head in range(heads):
            flat[member][:, HEAD_DIM * head : HEAD_DIM * (head + 1)] = grads[member][
                :, LANES * head : LANES * head + HEAD_DIM
            ]
        lines = dot_nt(flat[member][...], square[pl.ds(width, LANES), pl.ds(member * width, width)])
        inner_back[:, pl.ds(member * LANES, LANES)] = (lines * chosen).astype(BF16)
        put_square(1, member, dot_tn(inner[:, pl.ds(member * LANES, LANES)], flat[member][...]).astype(BF16))
    downs = dot_tn(inner_back[...], normed[:, main]).astype(BF16)
    for member in range(3):
        put_square(0, member, downs[member * LANES : (member + 1) * LANES])
    last_phases = (SQUARE_PHASE, SQUARE_PHASE + 1)
    for at in last_phases:
        act("start_cores", at)
    for at in (2, 3):
        act("start_result", at)
    for index in range(blocks):
        rows = pl.ds(index * block, block)
        total = dot_nt(flats[rows, :], square[pl.ds(0, width), pl.ds(0, 3 * width)])
        back[rows, main] = total + dot_nn(inner_back[rows, :], down[0:3].reshape(3 * LANES, width))
        if index == 0:
            for at in last_phases:
                act("start_first", at)

    def first_norm_back(index):
        rows = rows_of(index, 64)
        normal, inverse = layer_stats(tokens[rows, :].astype(F32))
        total = middle[rows, :] + norm_back(back[rows, main], normal, inverse, gain_one)
        normed_two[rows, main] = total.astype(BF16)

    repeat(0, seq_len // 64, first_norm_back)
    emit(normed_two.at[:, main], input_grad)
    if remote:
        for at in last_phases:
            reduce.start_second(at)
        for at in range(SQUARE_PHASE):
            reduce.finish(at)
        one, two = WIDE_PARTS
        for which, grad in ((1, grads_two), (0, grads_four)):
            for side in range(2):
                quarter = result_wide.at[2 * side + which]
                grad[:, side * one : (side + 1) * one] = quarter[:, :one].astype(F32)
                low = 2 * one + side * two
                high = min(low + two, grad.shape[1])
                grad[:, low:high] = quarter[:, one : one + high - low].astype(F32)
        for at in last_phases:
            reduce.start_z(at)
        for side, grad in ((0, grads_one), (1, grads_three)):
            grad[4] = result_narrow[2 * side].astype(F32)
            grad[3] = result_narrow[2 * side + 1].astype(F32)
        for at in last_phases:
            reduce.start_result(at)
        for at in last_phases:
            reduce.finish(at)
        for side, grad in ((0, grads_one), (1, grads_three)):
            for member in range(3):
                for index in range(4):
                    low, high = max(index * part, member * width), min((index + 1) * part, (member + 1) * width)
                    if low < high:
                        grad[member, :, low - member * width : high - member * width] = result_square[
                            index % 2, 2 * side + index // 2, :, low - index * part : high - index * part
                        ].astype(F32)
        for at in range(len(phases)):
            reduce.sent(at)
    else:
        emit(mlp.at[:, pl.ds(width, LANES), :], grads_one)
        for index in range(4):
            c, y = index // 2, index % 2
            emit(narrow_blocks.at[pl.ds(LANES * index, LANES), :], grads_two.at[c, y])
            emit(phases[SQUARE_PHASE].block(c, y), grads_three.at[c, y])
            emit(phases[SQUARE_PHASE + 1].block(c, y), grads_four.at[c, y])
    for copy in outgoing:
        copy.wait()


def layer(remote, features, tokens, cotangent, adapter, *rest):
    seq_len, width = tokens.shape
    spread = rest[-1].shape[2]
    heads = width // HEAD_DIM
    anywhere = pl.BlockSpec(memory_space=pl.ANY)
    here = pl.BlockSpec(memory_space=pltpu.VMEM)
    shape = jax.ShapeDtypeStruct
    count = len(GROUPS)
    part = 896
    links = []
    if remote:
        links = [pltpu.SemaphoreType.DMA((count, 28))] * 2 + [pltpu.SemaphoreType.REGULAR((7,))]
        links += [pltpu.SemaphoreType.DMA((SQUARE_PHASE + 2, 10))] * 2
        grads = (
            shape((5, 16, width), F32),
            shape((16, features), F32),
            shape((5, 16, width), F32),
            shape((16, features), F32),
        )
    else:
        grads = (
            shape((2, LANES, spread), BF16),
            shape((2, 2, LANES, width), BF16),
            shape((2, 2, LANES, part), BF16),
            shape((2, 2, LANES, part), BF16),
        )
    deep = width + LANES
    return pl.pallas_call(
        functools.partial(layer_kernel, remote),
        out_shape=(shape((seq_len, width), BF16), shape((seq_len, width), BF16), *grads),
        in_specs=[here, anywhere, pl.BlockSpec(memory_space=pltpu.SMEM)] + [here] * 4 + [anywhere] * 5,
        out_specs=[anywhere] * 2 + [here if remote else anywhere] * 4,
        scratch_shapes=[
            pltpu.VMEM((deep, 4 * width), BF16),
            pltpu.VMEM((6, LANES, width), BF16),
            pltpu.VMEM((2, deep, spread), BF16),
            pltpu.VMEM((seq_len, heads * LANES), BF16),
            pltpu.VMEM((seq_len, heads * LANES), BF16),
            pltpu.VMEM((seq_len, heads * LANES), BF16),
            pltpu.VMEM((seq_len, heads * LANES), BF16),
            pltpu.VMEM((seq_len, deep), BF16),
            pltpu.VMEM((seq_len, deep), BF16),
            pltpu.VMEM((seq_len, deep), BF16),
            pltpu.VMEM((seq_len, deep), BF16),
            pltpu.VMEM((seq_len, width), F32),
            pltpu.VMEM((seq_len, deep), F32),
            pltpu.VMEM((seq_len, deep), F32),
            pltpu.VMEM((seq_len, 3 * LANES), BF16),
            pltpu.VMEM((seq_len, 3 * LANES), BF16),
            pltpu.VMEM((2, seq_len, 1024), BF16),
            pltpu.VMEM((4, 16, spread // 2), BF16),
            pltpu.VMEM((4, 16, width), BF16),
            pltpu.VMEM((2, 4, 16, part), BF16),
            pltpu.SemaphoreType.DMA((32,)),
            *links,
        ],
        compiler_params=pltpu.CompilerParams(
            has_side_effects=True,
            vmem_limit_bytes=64 * 1024 * 1024,
            collective_id=0 if remote else None,
        ),
        name="layer" if remote else "layer_alone",
    )(tokens, cotangent, adapter, *rest)


def per_device(
    tokens,
    cotangent,
    adapter_ids,
    gain_one,
    shift_one,
    gain_two,
    shift_two,
    qkv_weight,
    out_weight,
    mlp_first,
    mlp_second,
    down_narrow,
    down_wide,
    up_narrow,
    up_wide,
):
    features = mlp_first.shape[1]
    depth = mlp_first.shape[0]
    mlp = jnp.stack(
        [
            jnp.concatenate([mlp_first, up_wide], axis=0),
            jnp.concatenate([mlp_second.T, down_wide], axis=0),
        ]
    )
    mlp = jnp.pad(mlp, ((0, 0), (0, 0), (0, -features % 256)))
    vectors = (gain_one, shift_one, gain_two, shift_two)
    weights = [qkv_weight, out_weight, down_narrow, up_narrow, mlp]
    remote = (lax.axis_size("rep"), lax.axis_size("shard")) == (4, 8)
    if not remote:
        parts = (qkv_weight, out_weight, down_narrow, up_narrow, mlp[:, :depth], mlp[:, depth:])
        parts = [
            lax.all_gather(each, "shard", axis=each.ndim - 2, tiled=True) for each in parts
        ]
        weights = parts[:4] + [jnp.concatenate(parts[4:], axis=1)]
    output, input_grad, *grads = layer(
        remote, features, tokens[0], cotangent[0], adapter_ids, *vectors, *weights
    )
    if not remote:
        grads = reduced(features, *grads)
    return (output[None], input_grad[None], *grads)


def reduced(features, wide, narrow, square, square_more):
    width = narrow.shape[3]
    downs, ups = [
        jnp.concatenate([square[0, side], square_more[0, side], square[1, side], square_more[1, side]], axis=1)
        for side in range(2)
    ]
    parts = [downs[:, : 3 * width], narrow[1, 0], narrow[0, 0], ups[:, : 3 * width], narrow[1, 1], narrow[0, 1]]
    parts = parts + [wide[1, :, :features], wide[0, :, :features]]
    share = lax.psum_scatter(jnp.concatenate(parts, axis=1), "shard", scatter_dimension=0, tiled=True)
    total = lax.psum(share, "rep").astype(F32)
    narrows = total[:, : 10 * width].reshape(-1, 10, width).transpose(1, 0, 2)
    wides = total[:, 10 * width :].reshape(-1, 2, features)
    return (narrows[:5], wides[:, 0], narrows[5:], wides[:, 1])


def solution(mesh):
    return jax.shard_map(
        per_device,
        mesh=mesh,
        in_specs=(
            P(("rep", "shard"), None, None),
            P(("rep", "shard"), None, None),
            P(("rep", "shard"), None),
            P(),
            P(),
            P(),
            P(),
            P(None, "shard", None),
            P("shard", None),
            P("shard", None),
            P(None, "shard"),
            P(None, "shard", None),
            P("shard", None),
            P(None, "shard", None),
            P("shard", None),
        ),
        out_specs=(
            P(("rep", "shard"), None, None),
            P(("rep", "shard"), None, None),
            P(None, "shard", None),
            P("shard", None),
            P(None, "shard", None),
            P("shard", None),
        ),
        check_vma=False,
    )
```

```python
import functools

import jax
import jax.numpy as jnp
from jax import lax
from jax.experimental import pallas as pl
from jax.experimental.pallas import tpu as pltpu
from jax.sharding import PartitionSpec as P

HEAD_DIM = 72
RANK = 16
GELU_SCALE = 0.7978845608028654
GELU_CUBE = 0.044715
MESH = pl.DeviceIdType.MESH
LANES = 128
BF16 = jnp.bfloat16
F32 = jnp.float32
CUTS = [(0, 1024), (1024, 1024), (2048, 1024), (3072, 1024), (4096, 256)]
CROSSED, PLAIN = 768, 256
GROUPS = [("down", 0, False), ("up", 0, False)]
GROUPS += [("square", part, True) for part in range(3)]
GROUPS += [("wide", 0, False)]
BATCHES = [[2, 0], [3, 1], [4, 5]]
for each in range(len(CUTS)):
    BATCHES.append([])
    if CUTS[each][1] > PLAIN:
        BATCHES[-1].append(len(GROUPS))
        GROUPS.append(("mlp", each, True))
    BATCHES[-1].append(len(GROUPS))
    GROUPS.append(("mlp", each, False))
FIRST_CUT = 3
WIDE_PARTS, NARROW_PARTS = (1152, 1024), (640, 512)
SQUARE_PHASE = 4
SEND, OWN, PLANE, ACROSS, BESIDE, CORNER, COMPUTE = range(7)
ORDER = (
    (0, 0, 0), (1, 0, 0), (1, 4, 0), (1, 3, 0), (1, 2, 0), (6, 0, 0), (1, 1, 0), (0, 2, 0),
    (3, 2, 0), (3, 3, 0), (3, 1, 0), (2, 0, 0), (5, 3, 0), (2, 0, 1), (0, 1, 0), (2, 2, 1),
    (3, 4, 0), (2, 2, 0), (0, 3, 0), (3, 0, 1), (2, 0, 2), (2, 2, 2), (1, 9, 0), (2, 1, 0),
    (3, 0, 2), (3, 2, 2), (1, 5, 0), (2, 3, 0), (0, 4, 0), (2, 1, 2), (2, 3, 2), (3, 2, 3),
    (1, 7, 0), (3, 2, 1), (0, 5, 0), (2, 3, 1), (3, 3, 1), (5, 2, 2), (2, 1, 1), (3, 7, 0),
    (4, 2, 2), (4, 3, 0), (1, 10, 0), (1, 6, 0), (5, 2, 1), (5, 2, 3), (3, 3, 2), (3, 0, 0),
    (2, 4, 0), (2, 4, 1), (0, 7, 0), (3, 1, 2), (3, 0, 3), (0, 6, 0), (2, 4, 2), (2, 5, 0),
    (4, 2, 0), (3, 3, 3), (6, 1, 0), (4, 3, 2), (3, 4, 2), (3, 4, 3), (1, 8, 0), (4, 3, 1),
    (2, 5, 2), (3, 5, 1), (1, 13, 0), (5, 2, 0), (3, 4, 1), (4, 4, 1), (2, 7, 1), (4, 4, 0),
    (3, 1, 3), (3, 1, 1), (5, 4, 3), (2, 5, 1), (5, 4, 0), (4, 2, 1), (4, 4, 2), (3, 6, 0),
    (5, 3, 3), (5, 3, 2), (5, 3, 1), (3, 5, 0), (0, 9, 0), (2, 7, 0), (2, 7, 2), (5, 4, 2),
    (3, 8, 0), (0, 8, 0), (2, 6, 1), (5, 4, 1), (2, 6, 0), (2, 6, 2), (6, 2, 0), (3, 7, 2),
    (6, 3, 0), (6, 4, 0), (6, 5, 0), (3, 9, 0), (6, 6, 0), (6, 7, 0), (6, 8, 0), (6, 9, 0),
    (3, 6, 2), (3, 7, 1), (1, 11, 0), (1, 12, 0), (0, 11, 0), (6, 10, 0), (0, 10, 0), (2, 8, 2),
    (2, 8, 0), (6, 11, 0), (6, 12, 0), (6, 13, 0), (3, 6, 1), (5, 8, 0), (2, 9, 2), (3, 7, 3),
    (5, 6, 0), (3, 6, 3), (2, 9, 0), (2, 9, 1), (3, 12, 0), (3, 13, 0), (6, 14, 0), (6, 15, 0),
    (6, 16, 0), (4, 6, 1), (6, 17, 0), (6, 18, 0), (1, 14, 0), (3, 10, 0), (3, 9, 3), (4, 6, 2),
    (3, 8, 1), (3, 9, 1), (0, 12, 0), (6, 19, 0), (4, 6, 0), (3, 5, 2), (2, 8, 1), (5, 6, 3),
    (5, 12, 0), (4, 8, 2), (6, 20, 0), (6, 21, 0), (6, 22, 0), (2, 10, 1), (3, 5, 3), (4, 8, 0),
    (2, 10, 2), (6, 23, 0), (2, 10, 0), (5, 8, 1), (3, 8, 2), (2, 11, 0), (3, 11, 0), (6, 24, 0),
    (0, 13, 0), (5, 6, 2), (2, 11, 2), (5, 6, 1), (6, 25, 0), (6, 26, 0), (4, 8, 1), (2, 12, 0),
    (0, 14, 0), (3, 8, 3), (4, 10, 1), (3, 11, 1), (6, 27, 0), (2, 13, 1), (5, 10, 0), (3, 14, 0),
    (3, 9, 2), (2, 13, 2), (5, 8, 2), (3, 10, 1), (2, 12, 1), (3, 10, 2), (5, 8, 3), (2, 11, 1),
    (3, 11, 3), (3, 10, 3), (2, 13, 0), (2, 12, 2), (4, 10, 0), (6, 28, 0), (3, 13, 2), (4, 10, 2),
    (6, 29, 0), (2, 14, 0), (2, 14, 2), (3, 11, 2), (4, 12, 0), (3, 12, 1), (3, 13, 3), (3, 12, 3),
    (2, 14, 1), (5, 10, 1), (6, 30, 0), (5, 10, 2), (4, 12, 1), (5, 10, 3), (4, 12, 2), (3, 14, 3),
    (3, 12, 2), (3, 14, 2), (6, 31, 0), (5, 12, 2), (5, 12, 1), (3, 14, 1), (5, 12, 3), (3, 13, 1),
    (6, 32, 0), (6, 33, 0), (6, 34, 0), (6, 35, 0), (6, 36, 0),
)


def dot_nn(left, right):
    return jnp.dot(left, right, preferred_element_type=F32)


def dot_nt(left, right):
    return lax.dot_general(left, right, (((1,), (1,)), ((), ())), preferred_element_type=F32)


def dot_tn(left, right):
    return lax.dot_general(left, right, (((0,), (0,)), ((), ())), preferred_element_type=F32)


def repeat(low, high, step):
    def body(index, carry):
        step(index)
        return carry

    lax.fori_loop(low, high, body, 0)


def rows_of(index, count):
    return pl.ds(pl.multiple_of(index * count, count), count)


def layer_stats(value):
    average = jnp.mean(value, axis=-1, keepdims=True)
    centred = value - average
    spread = jnp.mean(centred * centred, axis=-1, keepdims=True)
    inverse = lax.rsqrt(spread + 1e-06)
    return (centred * inverse, inverse)


def norm_back(gradient, normal_part, inverse, gain):
    scaled = gradient * gain
    return inverse * (
        scaled
        - jnp.mean(scaled, axis=-1, keepdims=True)
        - normal_part * jnp.mean(scaled * normal_part, axis=-1, keepdims=True)
    )


class Gather:
    def __init__(self, whole, send, receive):
        self.whole, self.send, self.receive = whole, send, receive
        rep, shard = lax.axis_index("rep"), lax.axis_index("shard")
        self.y, self.c = rep // 2, lax.rem(rep, 2)
        self.z, self.x = shard // 2, lax.rem(shard, 2)

    def piece(self, at, y, c, z, x):
        kind, part, _ = GROUPS[at]
        square, down, mlp = self.whole
        width, depth = down.shape[2], down.shape[2]
        shard, slot = 2 * z + x, 4 * x + z
        extra = pl.ds(pl.multiple_of(depth + 16 * slot, 16), 16)
        if kind == "down":
            return down.at[pl.ds(3 * c, 3), rows_of(slot, 16)]
        if kind == "up":
            return square.at[extra, pl.ds(pl.multiple_of(2 * width * c, LANES), 2 * width)]
        if kind == "square":
            rows = pl.ds(pl.multiple_of(144 * shard + 48 * part, 16), 48)
            return square.at[rows, pl.ds(pl.multiple_of(width * (2 * y + c), LANES), width)]
        if kind == "wide":
            return mlp.at[c, extra, :]
        start, count = CUTS[part]
        rows = pl.ds(pl.multiple_of(144 * shard, 16), 144)
        if not GROUPS[at][2]:
            return mlp.at[c, rows, pl.ds(start + count - PLAIN, PLAIN)]
        return mlp.at[c, rows, pl.ds(pl.multiple_of(start + (CROSSED // 2) * y, LANES), CROSSED // 2)]

    def device(self, y=None, c=None, z=None, x=None):
        y = self.y if y is None else y
        c = self.c if c is None else c
        z = self.z if z is None else z
        x = self.x if x is None else x
        return (2 * y + c, 2 * z + x)

    def source(self, hop):
        return lax.rem(self.z + 4 - hop, 4)

    def copy(self, at, slot, y, z, x, device):
        piece = self.piece(at, y, self.c, z, x)
        return pltpu.make_async_remote_copy(
            piece,
            piece,
            self.send.at[at, slot],
            self.receive.at[at, slot],
            device_id=device,
            device_id_type=MESH,
        )

    def along_z(self, at, hop):
        return self.copy(at, hop - 1, self.y, self.z, self.x, self.device(z=lax.rem(self.z + hop, 4)))

    def over_x(self, at, hop):
        return self.copy(at, 3 + hop, self.y, self.source(hop), self.x, self.device(x=1 - self.x))

    def over_y(self, at, hop):
        return self.copy(at, 6 + hop, self.y, self.source(hop), self.x, self.device(y=1 - self.y))

    def corner(self, at, hop):
        return self.copy(at, 10 + hop, self.y, self.source(hop), 1 - self.x, self.device(y=1 - self.y))

    def to_core(self, at, slot, y, hop, x):
        return self.copy(at, slot, y, self.source(hop), x, self.device(c=1 - self.c))

    def core_z(self, at, hop):
        return self.to_core(at, 13 + hop, self.y, hop, self.x)

    def core_x(self, at, hop):
        return self.to_core(at, 17 + hop, self.y, hop, 1 - self.x)

    def core_y(self, at, hop):
        return self.to_core(at, 20 + hop, 1 - self.y, hop, self.x)

    def core_corner(self, at, hop):
        return self.to_core(at, 24 + hop, 1 - self.y, hop, 1 - self.x)

    def greet(self):
        ready = pltpu.get_barrier_semaphore()
        partners = [self.device(z=lax.rem(self.z + hop, 4)) for hop in (1, 2, 3)]
        partners += [self.device(x=1 - self.x), self.device(y=1 - self.y), self.device(c=1 - self.c)]
        partners.append(self.device(y=1 - self.y, c=1 - self.c))
        for partner in partners:
            pl.semaphore_signal(ready, 1, device_id=partner, device_id_type=MESH)
        pl.semaphore_wait(ready, len(partners))

    def hop_of(self, index):
        near = 1 + 2 * ((3 - self.z) // 3)
        middle = 2 + lax.rem((self.z + 1) // 2, 2)
        return (near, middle, 6 - near - middle)[index]

    def step(self, what, at, index):
        crossed = GROUPS[at][2]
        if what == SEND:
            repeat(1, 4, lambda hop: self.along_z(at, hop).start())
        elif what == OWN:
            self.over_x(at, 0).start()
        elif what == PLANE:
            hop = self.hop_of(index)
            self.along_z(at, hop).wait_recv()
            if crossed:
                self.over_y(at, hop).start()
            self.over_x(at, hop).start()
            self.core_z(at, hop).start()
        elif what == ACROSS:
            hop = self.hop_of(index - 1) if index else 0
            self.over_x(at, hop).wait_recv()
            if crossed:
                self.corner(at, hop).start()
            self.core_x(at, hop).start()
        elif what == BESIDE:
            hop = self.hop_of(index)
            self.over_y(at, hop).wait_recv()
            self.core_y(at, hop).start()
        else:
            hop = self.hop_of(index - 1) if index else 0
            self.corner(at, hop).wait_recv()
            self.core_corner(at, hop).start()

    def copies_of(self, at):
        links, cores = [(self.along_z, 1), (self.over_x, 0)], [(self.core_z, 1), (self.core_x, 0)]
        if GROUPS[at][2]:
            links += [(self.over_y, 1), (self.corner, 0)]
            cores += [(self.core_y, 1), (self.core_corner, 0)]
        return links, cores

    def arrived(self, at):
        for copy, first in self.copies_of(at)[1]:
            repeat(first, 4, lambda hop: copy(at, hop).wait_recv())

    def sent(self, at):
        links, cores = self.copies_of(at)
        for copy, first in links + cores:
            repeat(first, 4, lambda hop: copy(at, hop).wait_send())


class Reduce:
    def __init__(self, net, free, phases, send, receive):
        self.net, self.free, self.phases = net, free, phases
        self.send, self.receive = send, receive
        self.partners = [
            net.device(c=1 - net.c),
            net.device(y=1 - net.y),
            net.device(x=1 - net.x),
        ]
        self.partners += [net.device(z=lax.rem(net.z + hop, 4)) for hop in (1, 2, 3)]
        self.partners.append(net.device(y=1 - net.y, c=1 - net.c))
        self.open = [False] * len(self.partners)

    def offer(self):
        for index, partner in enumerate(self.partners):
            pl.semaphore_signal(self.free.at[(0, 1, 2, 5, 4, 3, 6)[index]], 1, device_id=partner, device_id_type=MESH)

    def accept(self, index):
        if not self.open[index]:
            self.open[index] = True
            pl.semaphore_wait(self.free.at[index], 1)

    def copy(self, at, slot, source, target, index):
        return pltpu.make_async_remote_copy(
            source,
            target,
            self.send.at[at, slot],
            self.receive.at[at, slot],
            device_id=self.partners[index],
            device_id_type=MESH,
        )

    def across_cores(self, at):
        phase = self.phases[at]
        return self.copy(at, 0, phase.both(1 - self.net.c), phase.from_core, 0)

    def first_copies(self, at):
        phase, net = self.phases[at], self.net
        if not phase.by_x:
            return [self.copy(at, 1, phase.block(net.c, 1 - net.y), phase.from_first, 1)]
        return [
            self.copy(
                at,
                1 + side,
                phase.block(net.c, side).at[rows_of(1 - net.x, 64), :],
                phase.from_first.at[pl.ds(64 * side, 64), :],
                2,
            )
            for side in range(2)
        ]

    def second_copy(self, at):
        phase, net = self.phases[at], self.net
        if phase.by_x:
            source = phase.block(net.c, 1 - net.y).at[rows_of(net.x, 64), :]
        else:
            source = phase.block(net.c, net.y).at[rows_of(1 - net.x, 64), :]
        return self.copy(at, 3, source, phase.from_second, 1 if phase.by_x else 2)

    def across_z(self, at, hop):
        phase, net = self.phases[at], self.net
        there = lax.rem(net.z + hop, 4)
        source = phase.block(net.c, net.y).at[pl.ds(pl.multiple_of(64 * net.x + 16 * there, 16), 16), :]
        return self.copy(at, 3 + hop, source, phase.from_z.at[pl.ds(16 * (hop - 1), 16), :], 2 + hop)

    def result(self, at, index):
        net = self.net
        mine = self.phases[at].result(2 * net.y + net.c)
        return self.copy(at, 7 + index, mine, mine, (0, 1, 6)[index])

    def start_cores(self, at):
        self.accept(0)
        self.across_cores(at).start()

    def start_first(self, at):
        phase, net = self.phases[at], self.net
        self.across_cores(at).wait_recv()
        for side in range(2):
            add_into(phase.block(net.c, side), phase.core_part(side))
        self.accept(2 if phase.by_x else 1)
        for copy in self.first_copies(at):
            copy.start()

    def start_second(self, at):
        phase, net = self.phases[at], self.net
        for copy in self.first_copies(at):
            copy.wait_recv()
        if phase.by_x:
            for side in range(2):
                rows = rows_of(net.x, 64)
                add_into(phase.block(net.c, side).at[rows, :], phase.from_first.at[pl.ds(64 * side, 64), :])
        else:
            add_into(phase.block(net.c, net.y), phase.from_first)
        self.accept(1 if phase.by_x else 2)
        self.second_copy(at).start()

    def start_z(self, at):
        phase, net = self.phases[at], self.net
        self.second_copy(at).wait_recv()
        add_into(phase.block(net.c, net.y).at[rows_of(net.x, 64), :], phase.from_second)
        for hop in (1, 2, 3):
            self.accept(2 + hop)
            self.across_z(at, hop).start()

    def start_result(self, at):
        phase, net = self.phases[at], self.net
        for hop in (1, 2, 3):
            self.across_z(at, hop).wait_recv()
        mine = phase.block(net.c, net.y).at[pl.ds(pl.multiple_of(64 * net.x + 16 * net.z, 16), 16), :]
        total = mine[...].astype(F32)
        for hop in (0, 1, 2):
            total = total + phase.from_z[pl.ds(16 * hop, 16), :].astype(F32)
        phase.result(2 * net.y + net.c)[...] = total.astype(BF16)
        for index in range(3):
            self.accept((0, 1, 6)[index])
            self.result(at, index).start()

    def finish(self, at):
        for index in range(3):
            self.result(at, index).wait_recv()

    def sent(self, at):
        copies = [self.across_cores(at), *self.first_copies(at), self.second_copy(at)]
        copies += [self.across_z(at, hop) for hop in (1, 2, 3)]
        copies += [self.result(at, index) for index in range(3)]
        for copy in copies:
            copy.wait_send()


class Phase:
    def __init__(self, by_x, both, block, from_core, core_part, from_first, from_second, from_z, result):
        self.by_x, self.both, self.block = by_x, both, block
        self.from_core, self.core_part, self.result = from_core, core_part, result
        self.from_first, self.from_second, self.from_z = from_first, from_second, from_z


def add_into(target, other):
    def step(index):
        rows = rows_of(index, 32)
        target[rows, :] = (target[rows, :].astype(F32) + other[rows, :].astype(F32)).astype(BF16)

    repeat(0, target.shape[0] // 32, step)


def phases_of(mlp, result_wide, result_narrow, result_square):
    width = mlp.shape[1] - LANES
    part = result_square.shape[3]
    phases = []

    def spot(which, row, rows, column, count):
        return mlp.at[which, pl.ds(row, rows), pl.ds(column, count)]

    def wide_phase(by_x, first, count, column, result):
        def block(c, y):
            columns = pl.ds(pl.multiple_of(first + y * count, LANES), count)
            return mlp.at[c, pl.ds(width, LANES), columns]

        arrived = spot(0, 1024, LANES, first, 2 * count)
        phases.append(
            Phase(
                by_x,
                lambda c: mlp.at[c, pl.ds(width, LANES), pl.ds(first, 2 * count)],
                block,
                arrived,
                lambda side: arrived.at[:, pl.ds(count * side, count)],
                spot(1, 1024, LANES, column, count),
                spot(1, 1024, 64, 2176 + column, count),
                spot(1, 1088, 48, 2176 + column, count),
                result,
            )
        )

    def stacked_phase(by_x, which, row, column, count, land, places, result):
        def block(c, y):
            start = pl.multiple_of(row + 256 * c + LANES * y, LANES)
            return mlp.at[which, pl.ds(start, LANES), pl.ds(column, count)]

        def both(c):
            start = pl.multiple_of(row + 256 * c, LANES)
            return mlp.at[which, pl.ds(start, 256), pl.ds(column, count)]

        arrived = spot(1, places[0], 256, land, count)
        phases.append(
            Phase(
                by_x,
                both,
                block,
                arrived,
                lambda side: arrived.at[pl.ds(LANES * side, LANES), :],
                spot(1, places[1], LANES, land, count),
                spot(1, places[2], 64, land, count),
                spot(1, places[3], 48, land, count),
                result,
            )
        )

    wide_first = WIDE_PARTS[0]
    wide_phase(False, 0, wide_first, 0, lambda quarter: result_wide.at[quarter, :, pl.ds(0, wide_first)])
    wide_phase(
        True,
        2 * wide_first,
        WIDE_PARTS[1],
        wide_first,
        lambda quarter: result_wide.at[quarter, :, pl.ds(wide_first, WIDE_PARTS[1])],
    )
    start = 0
    for by_x, count in enumerate(NARROW_PARTS):
        stacked_phase(
            bool(by_x),
            1,
            512,
            width + start,
            count,
            2 * width + start,
            (512, 768, 896, 960),
            lambda quarter, columns=pl.ds(start, count): result_narrow.at[quarter, :, columns],
        )
        start += count
    for member in range(2):
        stacked_phase(
            bool(member),
            0,
            512,
            2048 + part * member,
            part,
            3 * width,
            (256 * member, 512 + LANES * member, 768 + 64 * member, 896 + 48 * member),
            lambda quarter, member=member: result_square.at[member, quarter],
        )
    return phases


def layer_kernel(
    remote,
    tokens,
    cotangent_from,
    adapter,
    gain_one_from,
    shift_one_from,
    gain_two_from,
    shift_two_from,
    qkv_from,
    out_from,
    down_from,
    up_from,
    mlp_from,
    output,
    input_grad,
    grads_one,
    grads_two,
    grads_three,
    grads_four,
    square,
    down,
    mlp,
    query,
    key,
    value,
    mixed,
    normed,
    attended,
    normed_two,
    cotangent,
    middle,
    after,
    back,
    inner,
    inner_back,
    result_wide,
    result_narrow,
    result_square,
    local_sem,
    *link_sems,
):
    seq_len, width = tokens.shape
    heads = width // HEAD_DIM
    scaling = HEAD_DIM ** (-0.5)
    block = 256
    blocks = seq_len // block
    side_columns = pl.ds(width, LANES)
    main = pl.ds(0, width)

    if remote:
        net = Gather((square, down, mlp), *link_sems[:2])
        shard, slot = 2 * net.z + net.x, 4 * net.x + net.z
        step, arrived, sent = net.step, net.arrived, net.sent
        number = 4 * lax.rem(adapter[0, 0], 2) + adapter[0, 0] // 2
    else:
        shard = slot = 0
        step = arrived = sent = lambda *at: None
        number = adapter[0, 0]
    ranks = lax.broadcasted_iota(jnp.int32, (1, LANES), 1)
    chosen = jnp.where((ranks >= number * RANK) & (ranks < (number + 1) * RANK), 1.0, 0.0)

    own = []

    def bring(source, target):
        copy = pltpu.make_async_copy(source, target, local_sem.at[len(own)])
        copy.start()
        own.append(copy)

    rank_rows = rows_of(slot, down_from.shape[1])
    extra_rows = pl.ds(pl.multiple_of(width + down_from.shape[1] * slot, 16), down_from.shape[1])
    depth_rows = rows_of(shard, out_from.shape[0])
    bring(down_from, down.at[pl.ds(0, 5), rank_rows])
    bring(up_from.at[4], down.at[5, rank_rows])
    for member in range(4):
        bring(up_from.at[member], square.at[extra_rows, pl.ds(member * width, width)])
    for member in range(3):
        bring(qkv_from.at[member], square.at[depth_rows, pl.ds(member * width, width)])
    bring(out_from, square.at[depth_rows, pl.ds(3 * width, width)])
    bring(mlp_from.at[:, pl.ds(out_from.shape[0], down_from.shape[1]), :], mlp.at[:, extra_rows, :])
    bring(mlp_from.at[:, pl.ds(0, out_from.shape[0]), :], mlp.at[:, depth_rows, :])
    bring(cotangent_from, cotangent.at[:, main])
    if remote:
        net.greet()
    for copy in own:
        copy.wait()
    gain_one, shift_one, gain_two, shift_two = [
        each[...].reshape(1, width) for each in (gain_one_from, shift_one_from, gain_two_from, shift_two_from)
    ]

    def first_norm(index):
        rows = rows_of(index, 64)
        normal, _ = layer_stats(tokens[rows, :].astype(F32))
        normed[rows, main] = (normal * gain_one + shift_one).astype(BF16)

    lane = lax.rem(lax.broadcasted_iota(jnp.int32, (64, heads * LANES), 1), LANES)
    minus = jnp.where((lane >= HEAD_DIM) & (lane < HEAD_DIM + 3), -1.0, 0.0).astype(BF16)

    def clear(index):
        rows = rows_of(index, 64)
        query[rows, :] = jnp.zeros_like(minus)
        value[rows, :] = jnp.zeros_like(minus)
        key[rows, :] = minus

    def start_block():
        repeat(0, seq_len // 64, first_norm)
        repeat(0, seq_len // 64, clear)

    def inner_of(index):
        rows = rows_of(index, block)
        three = dot_nt(normed[rows, main], down[0:3].reshape(3 * LANES, width))
        inner[rows, :] = (three * jnp.concatenate([chosen] * 3, axis=1)).astype(BF16)

        lines = dot_nt(cotangent[rows, main], down[5])
        cotangent[rows, side_columns] = (lines * chosen).astype(BF16)

    def inner_block():
        arrived(0)
        repeat(0, blocks, inner_of)

    def project(member, index):
        rows = rows_of(index, block)
        normed[rows, side_columns] = inner[rows, pl.ds(member * LANES, LANES)]
        lines = dot_nn(normed[rows, :], square[:, pl.ds(member * width, width)])
        attended[rows, main] = lines.astype(BF16)
        padded = (query, key, value)[member]
        for head in range(heads):
            padded[rows, LANES * head : LANES * head + HEAD_DIM] = attended[
                rows, HEAD_DIM * head : HEAD_DIM * (head + 1)
            ]

    lane = lax.broadcasted_iota(jnp.int32, (block, LANES), 1)

    def attend(head):
        columns = rows_of(head, LANES)
        for part in range(blocks):
            rows = pl.ds(part * block, block)
            lines = query[rows, columns]
            scores = dot_nt(lines, key[:, columns])
            top = jnp.max(scores, axis=-1, keepdims=True)
            exponent = jnp.exp((scores - top) * scaling)
            total = jnp.sum(exponent, axis=-1, keepdims=True)
            probs = (exponent * (1.0 / total)).astype(BF16)
            mixed[rows, columns] = dot_nn(probs, value[:, columns]).astype(BF16)
            level = top + jnp.log(total) * (1.0 / scaling)
            high = level.astype(BF16).astype(F32)
            mid = (level - high).astype(BF16).astype(F32)
            low = level - high - mid
            kept = jnp.where(lane == HEAD_DIM, high, lines.astype(F32))
            kept = jnp.where(lane == HEAD_DIM + 1, mid, kept)
            kept = jnp.where(lane == HEAD_DIM + 2, low, kept)
            query[rows, columns] = kept.astype(BF16)

    def join_heads():
        for head in range(heads):
            attended[:, HEAD_DIM * head : HEAD_DIM * (head + 1)] = mixed[
                :, LANES * head : LANES * head + HEAD_DIM
            ]

    def branch_out(index):
        rows = rows_of(index, block)
        attended[rows, side_columns] = (dot_nt(attended[rows, main], down[3]) * chosen).astype(BF16)
        total = tokens[rows, :].astype(F32) + dot_nn(attended[rows, :], square[:, pl.ds(3 * width, width)])
        middle[rows, :] = total
        normal, _ = layer_stats(total)
        lines = (normal * gain_two + shift_two).astype(BF16)
        normed_two[rows, main] = lines
        normed_two[rows, side_columns] = (dot_nt(lines, down[4]) * chosen).astype(BF16)

    def feed(cut, index):
        start, count = CUTS[cut]
        columns = pl.ds(start, count)
        rows = rows_of(index, block)
        before = dot_nn(normed_two[rows, :], mlp[0, :, columns])
        square_of = before * before
        tangent = jnp.tanh(GELU_SCALE * (before + GELU_CUBE * square_of * before))
        active = (0.5 * before * (1.0 + tangent)).astype(BF16)
        slope = 0.5 * (1.0 + tangent) + 0.5 * before * (1.0 - tangent * tangent) * (
            GELU_SCALE * (1.0 + 3.0 * GELU_CUBE * square_of)
        )
        gradient = dot_nn(cotangent[rows, :], mlp[1, :, columns])
        gradient = (gradient * slope).astype(BF16)
        mixed[rows, pl.ds(0, count)] = active
        mixed[rows, pl.ds(1024, count)] = gradient
        forward = dot_nt(active, mlp[1, :, columns])
        backward = dot_nt(gradient, mlp[0, :, columns])
        after[rows, :] = forward if cut == 0 else after[rows, :] + forward
        back[rows, :] = backward if cut == 0 else back[rows, :] + backward

    def feed_grads(cut):
        start, count = CUTS[cut]
        for which, lines in ((1, cotangent), (0, normed_two)):
            mlp[which, pl.ds(width, LANES), pl.ds(start, count)] = dot_tn(
                lines[:, side_columns], mixed[:, pl.ds(1024 * (1 - which), count)]
            ).astype(BF16)

    table = [((), start_block), ((), inner_block)]
    table += [
        ((1, 2, 3, 4) if (member, index) == (0, 0) else (), functools.partial(project, member, index))
        for member in range(3)
        for index in range(blocks)
    ]
    table += [((), functools.partial(attend, head)) for head in range(heads)]
    table += [((), join_heads)]
    table += [((5,) if index == 0 else (), functools.partial(branch_out, index)) for index in range(blocks)]
    for cut in range(len(CUTS)):
        for index in range(blocks):
            groups = BATCHES[FIRST_CUT + cut] if index == 0 else ()
            table.append((groups, functools.partial(feed, cut, index)))
    first_head = table.index(next(each for each in table if getattr(each[1], "func", None) is attend))
    place = 0 if remote else len(ORDER)
    if not remote:
        start_block()
        inner_block()
        for member in range(3):
            repeat(0, blocks, functools.partial(project, member))
        repeat(0, heads, attend)
        join_heads()
        repeat(0, blocks, branch_out)
        for cut in range(len(CUTS)):
            repeat(0, blocks, functools.partial(feed, cut))
            feed_grads(cut)
    while place < len(ORDER):
        what, at, index = ORDER[place]
        place += 1
        if what != COMPUTE:
            step(what, at, index)
            continue
        head = at - first_head
        if 0 <= head < heads:
            last = head + 1
            while ORDER[place][0] == COMPUTE and ORDER[place][1] - first_head < heads:
                last, place = last + 1, place + 1
            repeat(head, last, attend)
            continue
        groups, run = table[at]
        for group in groups:
            arrived(group)
        if groups and groups[0] == BATCHES[FIRST_CUT][0]:
            for group in range(groups[0]):
                sent(group)
        run()
        if getattr(run, "func", None) is feed and run.args[1] == blocks - 1:
            feed_grads(run.args[0])
    for at in range(BATCHES[FIRST_CUT][0], len(GROUPS)):
        sent(at)

    outgoing = []

    def emit(source, target):
        copy = pltpu.make_async_copy(source, target, local_sem.at[len(own) + len(outgoing)])
        copy.start()
        outgoing.append(copy)

    phases = phases_of(mlp, result_wide, result_narrow, result_square)
    if remote:
        reduce = Reduce(net, link_sems[2], phases, *link_sems[3:])
        reduce.offer()
        reduce.start_cores(0)
        reduce.start_cores(1)

    def act(stage, at):
        if remote:
            getattr(reduce, stage)(at)

    staged = mlp.at[1, pl.ds(512, seq_len), main]
    branch = mlp.at[0, pl.ds(0, seq_len), main]
    flat = [mlp.at[1, pl.ds(0, seq_len), pl.ds(width * member, width)] for member in range(3)]
    flats = mlp.at[1, pl.ds(0, seq_len), pl.ds(0, 3 * width)]

    def second_norm_back(index):
        rows = rows_of(index, block)
        lines = (after[rows, side_columns] * chosen).astype(BF16)
        inner_back[rows, pl.ds(0, LANES)] = lines
        residual = middle[rows, :]
        staged[rows, :] = (residual + (after[rows, main] + dot_nn(lines, down[5]))).astype(BF16)
        lines = (back[rows, side_columns] * chosen).astype(BF16)
        inner_back[rows, pl.ds(LANES, LANES)] = lines
        gradient = back[rows, main] + dot_nn(lines, down[4])
        normal, inverse = layer_stats(residual)
        total = cotangent[rows, main].astype(F32) + norm_back(gradient, normal, inverse, gain_two)
        middle[rows, :] = total
        lines = total.astype(BF16)
        branch[rows, :] = lines
        both = dot_nt(lines, square[:, pl.ds(3 * width, width)])
        lines = (both[:, width:] * chosen).astype(BF16)
        inner_back[rows, pl.ds(2 * LANES, LANES)] = lines
        flat[0][rows, :] = (both[:, :width] + dot_nn(lines, down[3])).astype(BF16)

    repeat(0, blocks, second_norm_back)
    emit(staged, output)
    act("start_first", 0)
    act("start_first", 1)
    for head in range(heads):
        mixed[:, LANES * head : LANES * head + HEAD_DIM] = flat[0][
            :, HEAD_DIM * head : HEAD_DIM * (head + 1)
        ]
    narrow_blocks = mlp.at[1, pl.ds(512, 4 * LANES), pl.ds(width, width)]
    for index, (left, right) in enumerate(
        (
            (inner_back[:, pl.ds(LANES, LANES)], normed_two[:, main]),
            (inner_back[:, pl.ds(0, LANES)], cotangent[:, main]),
            (inner_back[:, pl.ds(2 * LANES, LANES)], attended[:, main]),
            (attended[:, side_columns], branch[...]),
        )
    ):
        narrow_blocks[pl.ds(LANES * index, LANES), :] = dot_tn(left, right).astype(BF16)
    act("start_cores", 2)
    act("start_cores", 3)
    spread = heads * LANES
    grads = [
        mlp.at[0, pl.ds(0, seq_len), pl.ds(0, spread)],
        mlp.at[0, pl.ds(0, seq_len), pl.ds(spread, spread)],
        mlp.at[0, pl.ds(512, seq_len), pl.ds(0, spread)],
    ]

    def attend_back(pair):
        for head in (2 * pair, 2 * pair + 1):
            columns = rows_of(head, LANES)
            lines, keys = query[:, columns], key[:, columns]
            gradient = mixed[:, columns]
            probs = jnp.exp(dot_nt(keys, lines) * scaling)
            grad_probs = dot_nt(value[:, columns], gradient)
            level = jnp.sum(probs * grad_probs, axis=0, keepdims=True)
            grad_scores = (probs * (grad_probs - level)).astype(BF16)
            grads[2][:, columns] = dot_nn(probs.astype(BF16), gradient).astype(BF16)
            grads[1][:, columns] = (dot_nn(grad_scores, lines) * scaling).astype(BF16)
            grads[0][:, columns] = (dot_tn(grad_scores, keys) * scaling).astype(BF16)

    repeat(0, 3, attend_back)
    for at in (0, 1):
        act("start_second", at)
    for at in (2, 3):
        act("start_first", at)
    repeat(3, 6, attend_back)
    for at in (0, 1):
        act("start_z", at)
    for at in (2, 3):
        act("start_second", at)
    repeat(6, heads // 2, attend_back)
    for at in (2, 3):
        act("start_z", at)
    part = result_square.shape[3]

    def put_square(side, member, value):
        for index in range(4):
            low, high = max(index * part, member * width), min((index + 1) * part, (member + 1) * width)
            if low < high:
                place = phases[SQUARE_PHASE + index % 2].block(index // 2, side)
                place[:, low - index * part : high - index * part] = value[
                    :, low - member * width : high - member * width
                ]

    for side in range(2):
        phases[SQUARE_PHASE + 1].block(1, side)[:, 3 * width - 3 * part :] = jnp.zeros((LANES, 4 * part - 3 * width), BF16)
    for member in range(3):
        for head in range(heads):
            flat[member][:, HEAD_DIM * head : HEAD_DIM * (head + 1)] = grads[member][
                :, LANES * head : LANES * head + HEAD_DIM
            ]
        lines = dot_nt(flat[member][...], square[pl.ds(width, LANES), pl.ds(member * width, width)])
        inner_back[:, pl.ds(member * LANES, LANES)] = (lines * chosen).astype(BF16)
        put_square(1, member, dot_tn(inner[:, pl.ds(member * LANES, LANES)], flat[member][...]).astype(BF16))
    downs = dot_tn(inner_back[...], normed[:, main]).astype(BF16)
    for member in range(3):
        put_square(0, member, downs[member * LANES : (member + 1) * LANES])
    last_phases = (SQUARE_PHASE, SQUARE_PHASE + 1)
    for at in last_phases:
        act("start_cores", at)
    for at in range(SQUARE_PHASE):
        act("start_result", at)
    small = block // 2

    def project_back(index):
        rows = rows_of(index, small)
        total = dot_nt(flats[rows, :], square[pl.ds(0, width), pl.ds(0, 3 * width)])
        back[rows, main] = total + dot_nn(inner_back[rows, :], down[0:3].reshape(3 * LANES, width))

    repeat(0, 1, project_back)
    for at in last_phases:
        act("start_first", at)
    repeat(1, seq_len // small, project_back)
    for at in last_phases:
        act("start_second", at)

    def first_norm_back(index):
        rows = rows_of(index, 64)
        normal, inverse = layer_stats(tokens[rows, :].astype(F32))
        total = middle[rows, :] + norm_back(back[rows, main], normal, inverse, gain_one)
        normed_two[rows, main] = total.astype(BF16)

    repeat(0, seq_len // 64, first_norm_back)
    emit(normed_two.at[:, main], input_grad)
    if remote:
        for at in last_phases:
            reduce.start_z(at)
        for at in range(SQUARE_PHASE):
            reduce.finish(at)
        one, two = WIDE_PARTS
        for which, grad in ((1, grads_two), (0, grads_four)):
            for side in range(2):
                quarter = result_wide.at[2 * side + which]
                grad[:, side * one : (side + 1) * one] = quarter[:, :one].astype(F32)
                low = 2 * one + side * two
                high = min(low + two, grad.shape[1])
                grad[:, low:high] = quarter[:, one : one + high - low].astype(F32)
        for side, grad in ((0, grads_one), (1, grads_three)):
            grad[4] = result_narrow[2 * side].astype(F32)
            grad[3] = result_narrow[2 * side + 1].astype(F32)
        for at in last_phases:
            reduce.start_result(at)
        for at in last_phases:
            reduce.finish(at)
        for side, grad in ((0, grads_one), (1, grads_three)):
            for member in range(3):
                for index in range(4):
                    low, high = max(index * part, member * width), min((index + 1) * part, (member + 1) * width)
                    if low < high:
                        grad[member, :, low - member * width : high - member * width] = result_square[
                            index % 2, 2 * side + index // 2, :, low - index * part : high - index * part
                        ].astype(F32)
        for at in range(len(phases)):
            reduce.sent(at)
    else:
        emit(mlp.at[:, pl.ds(width, LANES), :], grads_one)
        for index in range(4):
            c, y = index // 2, index % 2
            emit(narrow_blocks.at[pl.ds(LANES * index, LANES), :], grads_two.at[c, y])
            emit(phases[SQUARE_PHASE].block(c, y), grads_three.at[c, y])
            emit(phases[SQUARE_PHASE + 1].block(c, y), grads_four.at[c, y])
    for copy in outgoing:
        copy.wait()


def layer(remote, features, tokens, cotangent, adapter, *rest):
    seq_len, width = tokens.shape
    spread = rest[-1].shape[2]
    heads = width // HEAD_DIM
    anywhere = pl.BlockSpec(memory_space=pl.ANY)
    here = pl.BlockSpec(memory_space=pltpu.VMEM)
    shape = jax.ShapeDtypeStruct
    count = len(GROUPS)
    part = 896
    links = []
    if remote:
        links = [pltpu.SemaphoreType.DMA((count, 28))] * 2 + [pltpu.SemaphoreType.REGULAR((7,))]
        links += [pltpu.SemaphoreType.DMA((SQUARE_PHASE + 2, 10))] * 2
        grads = (
            shape((5, 16, width), F32),
            shape((16, features), F32),
            shape((5, 16, width), F32),
            shape((16, features), F32),
        )
    else:
        grads = (
            shape((2, LANES, spread), BF16),
            shape((2, 2, LANES, width), BF16),
            shape((2, 2, LANES, part), BF16),
            shape((2, 2, LANES, part), BF16),
        )
    deep = width + LANES
    return pl.pallas_call(
        functools.partial(layer_kernel, remote),
        out_shape=(shape((seq_len, width), BF16), shape((seq_len, width), BF16), *grads),
        in_specs=[here, anywhere, pl.BlockSpec(memory_space=pltpu.SMEM)] + [here] * 4 + [anywhere] * 5,
        out_specs=[anywhere] * 2 + [here if remote else anywhere] * 4,
        scratch_shapes=[
            pltpu.VMEM((deep, 4 * width), BF16),
            pltpu.VMEM((6, LANES, width), BF16),
            pltpu.VMEM((2, deep, spread), BF16),
            pltpu.VMEM((seq_len, heads * LANES), BF16),
            pltpu.VMEM((seq_len, heads * LANES), BF16),
            pltpu.VMEM((seq_len, heads * LANES), BF16),
            pltpu.VMEM((seq_len, heads * LANES), BF16),
            pltpu.VMEM((seq_len, deep), BF16),
            pltpu.VMEM((seq_len, deep), BF16),
            pltpu.VMEM((seq_len, deep), BF16),
            pltpu.VMEM((seq_len, deep), BF16),
            pltpu.VMEM((seq_len, width), F32),
            pltpu.VMEM((seq_len, deep), F32),
            pltpu.VMEM((seq_len, deep), F32),
            pltpu.VMEM((seq_len, 3 * LANES), BF16),
            pltpu.VMEM((seq_len, 3 * LANES), BF16),
            pltpu.VMEM((4, 16, spread // 2), BF16),
            pltpu.VMEM((4, 16, width), BF16),
            pltpu.VMEM((2, 4, 16, part), BF16),
            pltpu.SemaphoreType.DMA((32,)),
            *links,
        ],
        compiler_params=pltpu.CompilerParams(
            has_side_effects=True,
            vmem_limit_bytes=64 * 1024 * 1024,
            collective_id=0 if remote else None,
        ),
        name="layer" if remote else "layer_alone",
    )(tokens, cotangent, adapter, *rest)


def per_device(
    tokens,
    cotangent,
    adapter_ids,
    gain_one,
    shift_one,
    gain_two,
    shift_two,
    qkv_weight,
    out_weight,
    mlp_first,
    mlp_second,
    down_narrow,
    down_wide,
    up_narrow,
    up_wide,
):
    features = mlp_first.shape[1]
    depth = mlp_first.shape[0]
    mlp = jnp.stack(
        [
            jnp.concatenate([mlp_first, up_wide], axis=0),
            jnp.concatenate([mlp_second.T, down_wide], axis=0),
        ]
    )
    mlp = jnp.pad(mlp, ((0, 0), (0, 0), (0, -features % 256)))
    vectors = (gain_one, shift_one, gain_two, shift_two)
    weights = [qkv_weight, out_weight, down_narrow, up_narrow, mlp]
    remote = (lax.axis_size("rep"), lax.axis_size("shard")) == (4, 8)
    if not remote:
        parts = (qkv_weight, out_weight, down_narrow, up_narrow, mlp[:, :depth], mlp[:, depth:])
        parts = [
            lax.all_gather(each, "shard", axis=each.ndim - 2, tiled=True) for each in parts
        ]
        weights = parts[:4] + [jnp.concatenate(parts[4:], axis=1)]
    output, input_grad, *grads = layer(
        remote, features, tokens[0], cotangent[0], adapter_ids, *vectors, *weights
    )
    if not remote:
        grads = reduced(features, *grads)
    return (output[None], input_grad[None], *grads)


def reduced(features, wide, narrow, square, square_more):
    width = narrow.shape[3]
    downs, ups = [
        jnp.concatenate([square[0, side], square_more[0, side], square[1, side], square_more[1, side]], axis=1)
        for side in range(2)
    ]
    parts = [downs[:, : 3 * width], narrow[1, 0], narrow[0, 0], ups[:, : 3 * width], narrow[1, 1], narrow[0, 1]]
    parts = parts + [wide[1, :, :features], wide[0, :, :features]]
    share = lax.psum_scatter(jnp.concatenate(parts, axis=1), "shard", scatter_dimension=0, tiled=True)
    total = lax.psum(share, "rep").astype(F32)
    narrows = total[:, : 10 * width].reshape(-1, 10, width).transpose(1, 0, 2)
    wides = total[:, 10 * width :].reshape(-1, 2, features)
    return (narrows[:5], wides[:, 0], narrows[5:], wides[:, 1])


def solution(mesh):
    return jax.shard_map(
        per_device,
        mesh=mesh,
        in_specs=(
            P(("rep", "shard"), None, None),
            P(("rep", "shard"), None, None),
            P(("rep", "shard"), None),
            P(),
            P(),
            P(),
            P(),
            P(None, "shard", None),
            P("shard", None),
            P("shard", None),
            P(None, "shard"),
            P(None, "shard", None),
            P("shard", None),
            P(None, "shard", None),
            P("shard", None),
        ),
        out_specs=(
            P(("rep", "shard"), None, None),
            P(("rep", "shard"), None, None),
            P(None, "shard", None),
            P("shard", None),
            P(None, "shard", None),
            P("shard", None),
        ),
        check_vma=False,
    )
```

```python
import functools

import jax
import jax.numpy as jnp
from jax import lax
from jax.experimental import pallas as pl
from jax.experimental.pallas import tpu as pltpu
from jax.sharding import PartitionSpec as P

HEAD_DIM = 72
RANK = 16
GELU_SCALE = 0.7978845608028654
GELU_CUBE = 0.044715
MESH = pl.DeviceIdType.MESH
LANES = 128
BF16 = jnp.bfloat16
F32 = jnp.float32
CUTS = [(0, 1024), (1024, 1024), (2048, 1024), (3072, 1024), (4096, 256)]
CROSSED, PLAIN = 768, 256
GROUPS = [("down", 0, False), ("up", 0, False)]
GROUPS += [("square", part, True) for part in range(3)]
GROUPS += [("wide", 0, False)]
BATCHES = [[2, 0], [3, 1], [4, 5]]
for each in range(len(CUTS)):
    BATCHES.append([])
    if CUTS[each][1] > PLAIN:
        BATCHES[-1].append(len(GROUPS))
        GROUPS.append(("mlp", each, True))
    BATCHES[-1].append(len(GROUPS))
    GROUPS.append(("mlp", each, False))
FIRST_CUT = 3
SETTLE = 40
WIDE_PARTS, NARROW_PARTS = (1152, 1024), (640, 512)
SQUARE_PHASE = 4
SEND, OWN, PLANE, ACROSS, BESIDE, CORNER, COMPUTE = range(7)
ORDER = (
    (0, 0, 0), (1, 1, 0), (1, 0, 0), (1, 3, 0), (0, 2, 0), (3, 0, 0), (1, 2, 0), (3, 2, 0),
    (6, 0, 0), (2, 0, 0), (2, 2, 0), (3, 1, 0), (2, 0, 1), (3, 0, 1), (2, 0, 2), (3, 3, 0),
    (0, 1, 0), (1, 4, 0), (2, 2, 1), (0, 3, 0), (3, 2, 1), (3, 0, 2), (4, 2, 0), (2, 2, 2),
    (5, 2, 0), (5, 2, 1), (4, 2, 1), (1, 5, 0), (3, 0, 3), (4, 2, 2), (6, 1, 0), (2, 1, 0),
    (3, 4, 0), (3, 2, 2), (0, 4, 0), (5, 3, 0), (0, 5, 0), (2, 3, 0), (2, 3, 2), (2, 1, 1),
    (3, 1, 2), (1, 7, 0), (2, 1, 2), (3, 2, 3), (2, 3, 1), (3, 7, 0), (3, 3, 1), (1, 6, 0),
    (3, 1, 3), (3, 3, 3), (5, 4, 0), (4, 3, 0), (5, 2, 3), (3, 3, 2), (1, 8, 0), (2, 4, 0),
    (4, 3, 2), (2, 4, 1), (2, 5, 0), (5, 3, 1), (0, 7, 0), (2, 4, 2), (0, 6, 0), (5, 3, 3),
    (5, 2, 2), (2, 5, 1), (5, 3, 2), (4, 3, 1), (2, 5, 2), (3, 6, 0), (1, 9, 0), (4, 4, 1),
    (3, 1, 1), (3, 4, 1), (4, 4, 0), (3, 4, 2), (3, 4, 3), (5, 6, 0), (2, 7, 1), (2, 7, 2),
    (1, 11, 0), (3, 9, 0), (4, 4, 2), (5, 4, 2), (3, 5, 0), (2, 7, 0), (3, 5, 2), (3, 5, 1),
    (5, 4, 1), (3, 8, 0), (0, 9, 0), (2, 6, 0), (0, 8, 0), (5, 4, 3), (2, 6, 1), (6, 2, 0),
    (6, 3, 0), (2, 6, 2), (6, 4, 0), (6, 5, 0), (6, 6, 0), (3, 7, 2), (1, 10, 0), (6, 7, 0),
    (3, 6, 1), (6, 8, 0), (3, 7, 3), (3, 6, 2), (1, 12, 0), (1, 13, 0), (3, 11, 0), (0, 11, 0),
    (3, 5, 3), (3, 6, 3), (3, 10, 0), (2, 9, 2), (6, 9, 0), (6, 10, 0), (2, 9, 0), (3, 7, 1),
    (5, 6, 1), (6, 11, 0), (0, 10, 0), (6, 12, 0), (2, 8, 0), (6, 13, 0), (5, 8, 0), (5, 6, 2),
    (3, 13, 0), (2, 9, 1), (2, 8, 2), (6, 14, 0), (6, 15, 0), (6, 16, 0), (6, 17, 0), (3, 8, 1),
    (4, 8, 0), (1, 14, 0), (2, 11, 0), (2, 8, 1), (3, 12, 0), (6, 18, 0), (3, 9, 3), (4, 6, 2),
    (6, 19, 0), (3, 9, 2), (3, 9, 1), (5, 6, 3), (5, 10, 0), (4, 6, 1), (4, 8, 2), (6, 20, 0),
    (0, 13, 0), (6, 21, 0), (4, 6, 0), (3, 8, 2), (6, 22, 0), (6, 23, 0), (2, 10, 2), (3, 11, 1),
    (6, 24, 0), (2, 10, 0), (5, 8, 1), (2, 11, 2), (3, 8, 3), (0, 12, 0), (2, 10, 1), (6, 25, 0),
    (6, 26, 0), (4, 8, 1), (6, 27, 0), (2, 11, 1), (3, 11, 3), (3, 10, 2), (4, 10, 1), (0, 14, 0),
    (5, 8, 3), (3, 10, 1), (3, 10, 3), (2, 13, 0), (2, 12, 0), (2, 13, 2), (2, 12, 1), (4, 10, 2),
    (2, 12, 2), (5, 12, 0), (5, 8, 2), (4, 10, 0), (6, 28, 0), (2, 13, 1), (6, 29, 0), (6, 30, 0),
    (5, 10, 3), (5, 10, 1), (4, 12, 0), (3, 12, 1), (3, 12, 2), (3, 11, 2), (4, 12, 2), (5, 10, 2),
    (2, 14, 2), (3, 12, 3), (2, 14, 1), (3, 13, 1), (2, 14, 0), (6, 31, 0), (6, 32, 0), (4, 12, 1),
    (5, 12, 1), (5, 12, 3), (5, 12, 2), (3, 13, 3), (3, 13, 2), (3, 14, 1), (3, 14, 2), (3, 14, 3),
    (3, 14, 0), (6, 33, 0), (6, 34, 0), (6, 35, 0), (6, 36, 0),
)


def dot_nn(left, right):
    return jnp.dot(left, right, preferred_element_type=F32)


def dot_nt(left, right):
    return lax.dot_general(left, right, (((1,), (1,)), ((), ())), preferred_element_type=F32)


def dot_tn(left, right):
    return lax.dot_general(left, right, (((0,), (0,)), ((), ())), preferred_element_type=F32)


def repeat(low, high, step):
    def body(index, carry):
        step(index)
        return carry

    lax.fori_loop(low, high, body, 0)


def rows_of(index, count):
    return pl.ds(pl.multiple_of(index * count, count), count)


def layer_stats(value):
    average = jnp.mean(value, axis=-1, keepdims=True)
    centred = value - average
    spread = jnp.mean(centred * centred, axis=-1, keepdims=True)
    inverse = lax.rsqrt(spread + 1e-06)
    return (centred * inverse, inverse)


def norm_back(gradient, normal_part, inverse, gain):
    scaled = gradient * gain
    return inverse * (
        scaled
        - jnp.mean(scaled, axis=-1, keepdims=True)
        - normal_part * jnp.mean(scaled * normal_part, axis=-1, keepdims=True)
    )


class Gather:
    def __init__(self, whole, send, receive):
        self.whole, self.send, self.receive = whole, send, receive
        rep, shard = lax.axis_index("rep"), lax.axis_index("shard")
        self.y, self.c = rep // 2, lax.rem(rep, 2)
        self.z, self.x = shard // 2, lax.rem(shard, 2)

    def piece(self, at, y, c, z, x):
        kind, part, _ = GROUPS[at]
        square, down, mlp = self.whole
        width, depth = down.shape[2], down.shape[2]
        shard, slot = 2 * z + x, 4 * x + z
        extra = pl.ds(pl.multiple_of(depth + 16 * slot, 16), 16)
        if kind == "down":
            return down.at[pl.ds(3 * c, 3), rows_of(slot, 16)]
        if kind == "up":
            return square.at[extra, pl.ds(pl.multiple_of(2 * width * c, LANES), 2 * width)]
        if kind == "square":
            rows = pl.ds(pl.multiple_of(144 * shard + 48 * part, 16), 48)
            return square.at[rows, pl.ds(pl.multiple_of(width * (2 * y + c), LANES), width)]
        if kind == "wide":
            return mlp.at[c, extra, :]
        start, count = CUTS[part]
        rows = pl.ds(pl.multiple_of(144 * shard, 16), 144)
        if not GROUPS[at][2]:
            return mlp.at[c, rows, pl.ds(start + count - PLAIN, PLAIN)]
        return mlp.at[c, rows, pl.ds(pl.multiple_of(start + (CROSSED // 2) * y, LANES), CROSSED // 2)]

    def device(self, y=None, c=None, z=None, x=None):
        y = self.y if y is None else y
        c = self.c if c is None else c
        z = self.z if z is None else z
        x = self.x if x is None else x
        return (2 * y + c, 2 * z + x)

    def source(self, hop):
        return lax.rem(self.z + 4 - hop, 4)

    def copy(self, at, slot, y, z, x, device):
        piece = self.piece(at, y, self.c, z, x)
        return pltpu.make_async_remote_copy(
            piece,
            piece,
            self.send.at[at, slot],
            self.receive.at[at, slot],
            device_id=device,
            device_id_type=MESH,
        )

    def along_z(self, at, hop):
        return self.copy(at, hop - 1, self.y, self.z, self.x, self.device(z=lax.rem(self.z + hop, 4)))

    def over_x(self, at, hop):
        return self.copy(at, 3 + hop, self.y, self.source(hop), self.x, self.device(x=1 - self.x))

    def over_y(self, at, hop):
        return self.copy(at, 6 + hop, self.y, self.source(hop), self.x, self.device(y=1 - self.y))

    def corner(self, at, hop):
        return self.copy(at, 10 + hop, self.y, self.source(hop), 1 - self.x, self.device(y=1 - self.y))

    def to_core(self, at, slot, y, hop, x):
        return self.copy(at, slot, y, self.source(hop), x, self.device(c=1 - self.c))

    def core_z(self, at, hop):
        return self.to_core(at, 13 + hop, self.y, hop, self.x)

    def core_x(self, at, hop):
        return self.to_core(at, 17 + hop, self.y, hop, 1 - self.x)

    def core_y(self, at, hop):
        return self.to_core(at, 20 + hop, 1 - self.y, hop, self.x)

    def core_corner(self, at, hop):
        return self.to_core(at, 24 + hop, 1 - self.y, hop, 1 - self.x)

    def greet(self):
        ready = pltpu.get_barrier_semaphore()
        partners = [self.device(z=lax.rem(self.z + hop, 4)) for hop in (1, 2, 3)]
        partners += [self.device(x=1 - self.x), self.device(y=1 - self.y), self.device(c=1 - self.c)]
        partners.append(self.device(y=1 - self.y, c=1 - self.c))
        for partner in partners:
            pl.semaphore_signal(ready, 1, device_id=partner, device_id_type=MESH)
        return lambda: pl.semaphore_wait(ready, len(partners))

    def hop_of(self, index):
        near = 1 + 2 * ((3 - self.z) // 3)
        middle = 2 + lax.rem((self.z + 1) // 2, 2)
        return (near, middle, 6 - near - middle)[index]

    def step(self, what, at, index):
        crossed = GROUPS[at][2]
        if what == SEND:
            repeat(1, 4, lambda hop: self.along_z(at, hop).start())
        elif what == OWN:
            self.over_x(at, 0).start()
        elif what == PLANE:
            hop = self.hop_of(index)
            self.along_z(at, hop).wait_recv()
            if crossed:
                self.over_y(at, hop).start()
            self.over_x(at, hop).start()
            self.core_z(at, hop).start()
        elif what == ACROSS:
            hop = self.hop_of(index - 1) if index else 0
            self.over_x(at, hop).wait_recv()
            if crossed:
                self.corner(at, hop).start()
            self.core_x(at, hop).start()
        elif what == BESIDE:
            hop = self.hop_of(index)
            self.over_y(at, hop).wait_recv()
            self.core_y(at, hop).start()
        else:
            hop = self.hop_of(index - 1) if index else 0
            self.corner(at, hop).wait_recv()
            self.core_corner(at, hop).start()

    def copies_of(self, at):
        links, cores = [(self.along_z, 1), (self.over_x, 0)], [(self.core_z, 1), (self.core_x, 0)]
        if GROUPS[at][2]:
            links += [(self.over_y, 1), (self.corner, 0)]
            cores += [(self.core_y, 1), (self.core_corner, 0)]
        return links, cores

    def arrived(self, at):
        for copy, first in self.copies_of(at)[1]:
            repeat(first, 4, lambda hop: copy(at, hop).wait_recv())

    def sent(self, at):
        links, cores = self.copies_of(at)
        for copy, first in links + cores:
            repeat(first, 4, lambda hop: copy(at, hop).wait_send())


class Reduce:
    def __init__(self, net, free, phases, send, receive):
        self.net, self.free, self.phases = net, free, phases
        self.send, self.receive = send, receive
        self.partners = [
            net.device(c=1 - net.c),
            net.device(y=1 - net.y),
            net.device(x=1 - net.x),
        ]
        self.partners += [net.device(z=lax.rem(net.z + hop, 4)) for hop in (1, 2, 3)]
        self.partners.append(net.device(y=1 - net.y, c=1 - net.c))
        self.open = [False] * len(self.partners)

    def offer(self):
        for index, partner in enumerate(self.partners):
            pl.semaphore_signal(self.free.at[(0, 1, 2, 5, 4, 3, 6)[index]], 1, device_id=partner, device_id_type=MESH)

    def accept(self, index):
        if not self.open[index]:
            self.open[index] = True
            pl.semaphore_wait(self.free.at[index], 1)

    def copy(self, at, slot, source, target, index):
        return pltpu.make_async_remote_copy(
            source,
            target,
            self.send.at[at, slot],
            self.receive.at[at, slot],
            device_id=self.partners[index],
            device_id_type=MESH,
        )

    def across_cores(self, at):
        phase = self.phases[at]
        return self.copy(at, 0, phase.both(1 - self.net.c), phase.from_core, 0)

    def first_copies(self, at):
        phase, net = self.phases[at], self.net
        if not phase.by_x:
            return [self.copy(at, 1, phase.block(net.c, 1 - net.y), phase.from_first, 1)]
        return [
            self.copy(
                at,
                1 + side,
                phase.block(net.c, side).at[rows_of(1 - net.x, 64), :],
                phase.from_first.at[pl.ds(64 * side, 64), :],
                2,
            )
            for side in range(2)
        ]

    def second_copy(self, at):
        phase, net = self.phases[at], self.net
        if phase.by_x:
            source = phase.block(net.c, 1 - net.y).at[rows_of(net.x, 64), :]
        else:
            source = phase.block(net.c, net.y).at[rows_of(1 - net.x, 64), :]
        return self.copy(at, 3, source, phase.from_second, 1 if phase.by_x else 2)

    def across_z(self, at, hop):
        phase, net = self.phases[at], self.net
        there = lax.rem(net.z + hop, 4)
        source = phase.block(net.c, net.y).at[pl.ds(pl.multiple_of(64 * net.x + 16 * there, 16), 16), :]
        return self.copy(at, 3 + hop, source, phase.from_z.at[pl.ds(16 * (hop - 1), 16), :], 2 + hop)

    def result(self, at, index):
        net = self.net
        mine = self.phases[at].result(2 * net.y + net.c)
        return self.copy(at, 7 + index, mine, mine, (0, 1, 6)[index])

    def start_cores(self, at):
        self.accept(0)
        self.across_cores(at).start()

    def start_first(self, at):
        phase, net = self.phases[at], self.net
        self.across_cores(at).wait_recv()
        for side in range(2):
            add_into(phase.block(net.c, side), phase.core_part(side))
        self.accept(2 if phase.by_x else 1)
        for copy in self.first_copies(at):
            copy.start()

    def start_second(self, at):
        phase, net = self.phases[at], self.net
        for copy in self.first_copies(at):
            copy.wait_recv()
        if phase.by_x:
            for side in range(2):
                rows = rows_of(net.x, 64)
                add_into(phase.block(net.c, side).at[rows, :], phase.from_first.at[pl.ds(64 * side, 64), :])
        else:
            add_into(phase.block(net.c, net.y), phase.from_first)
        self.accept(1 if phase.by_x else 2)
        self.second_copy(at).start()

    def start_z(self, at):
        phase, net = self.phases[at], self.net
        self.second_copy(at).wait_recv()
        add_into(phase.block(net.c, net.y).at[rows_of(net.x, 64), :], phase.from_second)
        for hop in (1, 2, 3):
            self.accept(2 + hop)
            self.across_z(at, hop).start()

    def start_result(self, at):
        phase, net = self.phases[at], self.net
        for hop in (1, 2, 3):
            self.across_z(at, hop).wait_recv()
        mine = phase.block(net.c, net.y).at[pl.ds(pl.multiple_of(64 * net.x + 16 * net.z, 16), 16), :]
        total = mine[...].astype(F32)
        for hop in (0, 1, 2):
            total = total + phase.from_z[pl.ds(16 * hop, 16), :].astype(F32)
        phase.result(2 * net.y + net.c)[...] = total.astype(BF16)
        for index in range(3):
            self.accept((0, 1, 6)[index])
            self.result(at, index).start()

    def finish(self, at):
        for index in range(3):
            self.result(at, index).wait_recv()

    def sent(self, at):
        copies = [self.across_cores(at), *self.first_copies(at), self.second_copy(at)]
        copies += [self.across_z(at, hop) for hop in (1, 2, 3)]
        copies += [self.result(at, index) for index in range(3)]
        for copy in copies:
            copy.wait_send()


class Phase:
    def __init__(self, by_x, both, block, from_core, core_part, from_first, from_second, from_z, result):
        self.by_x, self.both, self.block = by_x, both, block
        self.from_core, self.core_part, self.result = from_core, core_part, result
        self.from_first, self.from_second, self.from_z = from_first, from_second, from_z


def add_into(target, other):
    def step(index):
        rows = rows_of(index, 32)
        target[rows, :] = (target[rows, :].astype(F32) + other[rows, :].astype(F32)).astype(BF16)

    repeat(0, target.shape[0] // 32, step)


def phases_of(mlp, result_wide, result_narrow, result_square):
    width = mlp.shape[1] - LANES
    part = result_square.shape[3]
    phases = []

    def spot(which, row, rows, column, count):
        return mlp.at[which, pl.ds(row, rows), pl.ds(column, count)]

    def wide_phase(by_x, first, count, column, result):
        def block(c, y):
            columns = pl.ds(pl.multiple_of(first + y * count, LANES), count)
            return mlp.at[c, pl.ds(width, LANES), columns]

        arrived = spot(0, 1024, LANES, first, 2 * count)
        phases.append(
            Phase(
                by_x,
                lambda c: mlp.at[c, pl.ds(width, LANES), pl.ds(first, 2 * count)],
                block,
                arrived,
                lambda side: arrived.at[:, pl.ds(count * side, count)],
                spot(1, 1024, LANES, column, count),
                spot(1, 1024, 64, 2176 + column, count),
                spot(1, 1088, 48, 2176 + column, count),
                result,
            )
        )

    def stacked_phase(by_x, which, row, column, count, land, places, result):
        def block(c, y):
            start = pl.multiple_of(row + 256 * c + LANES * y, LANES)
            return mlp.at[which, pl.ds(start, LANES), pl.ds(column, count)]

        def both(c):
            start = pl.multiple_of(row + 256 * c, LANES)
            return mlp.at[which, pl.ds(start, 256), pl.ds(column, count)]

        arrived = spot(1, places[0], 256, land, count)
        phases.append(
            Phase(
                by_x,
                both,
                block,
                arrived,
                lambda side: arrived.at[pl.ds(LANES * side, LANES), :],
                spot(1, places[1], LANES, land, count),
                spot(1, places[2], 64, land, count),
                spot(1, places[3], 48, land, count),
                result,
            )
        )

    wide_first = WIDE_PARTS[0]
    wide_phase(False, 0, wide_first, 0, lambda quarter: result_wide.at[quarter, :, pl.ds(0, wide_first)])
    wide_phase(
        True,
        2 * wide_first,
        WIDE_PARTS[1],
        wide_first,
        lambda quarter: result_wide.at[quarter, :, pl.ds(wide_first, WIDE_PARTS[1])],
    )
    start = 0
    for by_x, count in enumerate(NARROW_PARTS):
        stacked_phase(
            bool(by_x),
            1,
            512,
            width + start,
            count,
            2 * width + start,
            (512, 768, 896, 960),
            lambda quarter, columns=pl.ds(start, count): result_narrow.at[quarter, :, columns],
        )
        start += count
    for member in range(2):
        stacked_phase(
            bool(member),
            0,
            512,
            2048 + part * member,
            part,
            3 * width,
            (256 * member, 512 + LANES * member, 768 + 64 * member, 896 + 48 * member),
            lambda quarter, member=member: result_square.at[member, quarter],
        )
    return phases


def layer_kernel(
    remote,
    tokens,
    cotangent_from,
    adapter,
    gain_one_from,
    shift_one_from,
    gain_two_from,
    shift_two_from,
    qkv_from,
    out_from,
    down_from,
    up_from,
    mlp_from,
    output,
    input_grad,
    grads_one,
    grads_two,
    grads_three,
    grads_four,
    square,
    down,
    mlp,
    query,
    key,
    value,
    mixed,
    normed,
    attended,
    normed_two,
    cotangent,
    middle,
    after,
    back,
    inner,
    inner_back,
    result_wide,
    result_narrow,
    result_square,
    local_sem,
    *link_sems,
):
    seq_len, width = tokens.shape
    heads = width // HEAD_DIM
    scaling = HEAD_DIM ** (-0.5)
    block = 256
    blocks = seq_len // block
    side_columns = pl.ds(width, LANES)
    main = pl.ds(0, width)

    if remote:
        net = Gather((square, down, mlp), *link_sems[:2])
        shard, slot = 2 * net.z + net.x, 4 * net.x + net.z
        step, arrived, sent = net.step, net.arrived, net.sent
        all_here = net.greet()
        number = 4 * lax.rem(adapter[0, 0], 2) + adapter[0, 0] // 2
    else:
        shard = slot = 0
        step = arrived = sent = lambda *at: None
        number = adapter[0, 0]
    ranks = lax.broadcasted_iota(jnp.int32, (1, LANES), 1)
    chosen = jnp.where((ranks >= number * RANK) & (ranks < (number + 1) * RANK), 1.0, 0.0)

    own = []

    def bring(source, target):
        copy = pltpu.make_async_copy(source, target, local_sem.at[len(own)])
        copy.start()
        own.append(copy)

    rank_rows = rows_of(slot, down_from.shape[1])
    extra_rows = pl.ds(pl.multiple_of(width + down_from.shape[1] * slot, 16), down_from.shape[1])
    depth_rows = rows_of(shard, out_from.shape[0])
    bring(down_from, down.at[pl.ds(0, 5), rank_rows])
    bring(up_from.at[4], down.at[5, rank_rows])
    for member in range(4):
        bring(up_from.at[member], square.at[extra_rows, pl.ds(member * width, width)])
    for member in range(3):
        bring(qkv_from.at[member], square.at[depth_rows, pl.ds(member * width, width)])
    bring(out_from, square.at[depth_rows, pl.ds(3 * width, width)])
    bring(mlp_from.at[:, pl.ds(out_from.shape[0], down_from.shape[1]), :], mlp.at[:, extra_rows, :])
    bring(mlp_from.at[:, pl.ds(0, out_from.shape[0]), :], mlp.at[:, depth_rows, :])
    bring(cotangent_from, cotangent.at[:, main])
    gain_one, shift_one, gain_two, shift_two = [
        each[...].reshape(1, width) for each in (gain_one_from, shift_one_from, gain_two_from, shift_two_from)
    ]

    def first_norm(index):
        rows = rows_of(index, 64)
        normal, _ = layer_stats(tokens[rows, :].astype(F32))
        normed[rows, main] = (normal * gain_one + shift_one).astype(BF16)

    lane = lax.rem(lax.broadcasted_iota(jnp.int32, (64, heads * LANES), 1), LANES)
    minus = jnp.where((lane >= HEAD_DIM) & (lane < HEAD_DIM + 3), -1.0, 0.0).astype(BF16)

    def clear(index):
        rows = rows_of(index, 64)
        query[rows, :] = jnp.zeros_like(minus)
        value[rows, :] = jnp.zeros_like(minus)
        key[rows, :] = minus

    def start_block():
        repeat(0, seq_len // 64, first_norm)
        repeat(0, seq_len // 64, clear)

    def inner_of(index):
        rows = rows_of(index, block)
        three = dot_nt(normed[rows, main], down[0:3].reshape(3 * LANES, width))
        inner[rows, :] = (three * jnp.concatenate([chosen] * 3, axis=1)).astype(BF16)

        lines = dot_nt(cotangent[rows, main], down[5])
        cotangent[rows, side_columns] = (lines * chosen).astype(BF16)

    def inner_block():
        arrived(0)
        repeat(0, blocks, inner_of)

    def project(member, index):
        rows = rows_of(index, block)
        normed[rows, side_columns] = inner[rows, pl.ds(member * LANES, LANES)]
        lines = dot_nn(normed[rows, :], square[:, pl.ds(member * width, width)])
        attended[rows, main] = lines.astype(BF16)
        padded = (query, key, value)[member]
        for head in range(heads):
            padded[rows, LANES * head : LANES * head + HEAD_DIM] = attended[
                rows, HEAD_DIM * head : HEAD_DIM * (head + 1)
            ]

    lane = lax.broadcasted_iota(jnp.int32, (block, LANES), 1)

    def attend(head):
        columns = rows_of(head, LANES)
        for part in range(blocks):
            rows = pl.ds(part * block, block)
            lines = query[rows, columns]
            scores = dot_nt(lines, key[:, columns])
            top = jnp.max(scores, axis=-1, keepdims=True)
            exponent = jnp.exp((scores - top) * scaling)
            total = jnp.sum(exponent, axis=-1, keepdims=True)
            probs = (exponent * (1.0 / total)).astype(BF16)
            mixed[rows, columns] = dot_nn(probs, value[:, columns]).astype(BF16)
            level = top + jnp.log(total) * (1.0 / scaling)
            high = level.astype(BF16).astype(F32)
            mid = (level - high).astype(BF16).astype(F32)
            low = level - high - mid
            kept = jnp.where(lane == HEAD_DIM, high, lines.astype(F32))
            kept = jnp.where(lane == HEAD_DIM + 1, mid, kept)
            kept = jnp.where(lane == HEAD_DIM + 2, low, kept)
            query[rows, columns] = kept.astype(BF16)

    def join_heads():
        for head in range(heads):
            attended[:, HEAD_DIM * head : HEAD_DIM * (head + 1)] = mixed[
                :, LANES * head : LANES * head + HEAD_DIM
            ]

    def branch_out(index):
        rows = rows_of(index, block)
        attended[rows, side_columns] = (dot_nt(attended[rows, main], down[3]) * chosen).astype(BF16)
        total = tokens[rows, :].astype(F32) + dot_nn(attended[rows, :], square[:, pl.ds(3 * width, width)])
        middle[rows, :] = total
        normal, _ = layer_stats(total)
        lines = (normal * gain_two + shift_two).astype(BF16)
        normed_two[rows, main] = lines
        normed_two[rows, side_columns] = (dot_nt(lines, down[4]) * chosen).astype(BF16)

    def feed(cut, index):
        start, count = CUTS[cut]
        columns = pl.ds(start, count)
        rows = rows_of(index, block)
        before = dot_nn(normed_two[rows, :], mlp[0, :, columns])
        square_of = before * before
        tangent = jnp.tanh(GELU_SCALE * (before + GELU_CUBE * square_of * before))
        active = (0.5 * before * (1.0 + tangent)).astype(BF16)
        slope = 0.5 * (1.0 + tangent) + 0.5 * before * (1.0 - tangent * tangent) * (
            GELU_SCALE * (1.0 + 3.0 * GELU_CUBE * square_of)
        )
        gradient = dot_nn(cotangent[rows, :], mlp[1, :, columns])
        gradient = (gradient * slope).astype(BF16)
        mixed[rows, pl.ds(0, count)] = active
        mixed[rows, pl.ds(1024, count)] = gradient
        forward = dot_nt(active, mlp[1, :, columns])
        backward = dot_nt(gradient, mlp[0, :, columns])
        after[rows, :] = forward if cut == 0 else after[rows, :] + forward
        back[rows, :] = backward if cut == 0 else back[rows, :] + backward

    def feed_grads(cut):
        start, count = CUTS[cut]
        for which, lines in ((1, cotangent), (0, normed_two)):
            mlp[which, pl.ds(width, LANES), pl.ds(start, count)] = dot_tn(
                lines[:, side_columns], mixed[:, pl.ds(1024 * (1 - which), count)]
            ).astype(BF16)

    start_block()
    if remote:
        all_here()
    for copy in own:
        copy.wait()

    table = [((), lambda: None), ((), inner_block)]
    table += [
        ((1, 2, 3, 4) if (member, index) == (0, 0) else (), functools.partial(project, member, index))
        for member in range(3)
        for index in range(blocks)
    ]
    table += [((), functools.partial(attend, head)) for head in range(heads)]
    table += [((), join_heads)]
    table += [((5,) if index == 0 else (), functools.partial(branch_out, index)) for index in range(blocks)]
    for cut in range(len(CUTS)):
        for index in range(blocks):
            groups = BATCHES[FIRST_CUT + cut] if index == 0 else ()
            table.append((groups, functools.partial(feed, cut, index)))
    first_head = table.index(next(each for each in table if getattr(each[1], "func", None) is attend))
    place = 0 if remote else len(ORDER)
    waited = []
    if not remote:
        inner_block()
        for member in range(3):
            repeat(0, blocks, functools.partial(project, member))
        repeat(0, heads, attend)
        join_heads()
        repeat(0, blocks, branch_out)
        for cut in range(len(CUTS)):
            repeat(0, blocks, functools.partial(feed, cut))
            feed_grads(cut)
    while place < len(ORDER):
        what, at, index = ORDER[place]
        place += 1
        if what != COMPUTE:
            step(what, at, index)
            continue
        head = at - first_head
        if 0 <= head < heads:
            last = head + 1
            while ORDER[place][0] == COMPUTE and ORDER[place][1] - first_head < heads:
                last, place = last + 1, place + 1
            repeat(head, last, attend)
            continue
        groups, run = table[at]
        if groups and groups[0] >= BATCHES[FIRST_CUT][0]:
            later = {group for kind, group, _ in ORDER[max(place - SETTLE, 0) :] if kind != COMPUTE}
            later -= set(range(groups[0] if groups[0] == BATCHES[FIRST_CUT][0] else 0))
            for group in range(len(GROUPS)):
                if group not in later and group not in waited:
                    waited.append(group)
                    sent(group)
        for group in groups:
            arrived(group)
        run()
        if getattr(run, "func", None) is feed and run.args[1] == blocks - 1:
            feed_grads(run.args[0])
    for group in range(len(GROUPS)):
        if group not in waited:
            sent(group)

    outgoing = []

    def emit(source, target):
        copy = pltpu.make_async_copy(source, target, local_sem.at[len(own) + len(outgoing)])
        copy.start()
        outgoing.append(copy)

    phases = phases_of(mlp, result_wide, result_narrow, result_square)
    if remote:
        reduce = Reduce(net, link_sems[2], phases, *link_sems[3:])
        reduce.offer()
        reduce.start_cores(0)
        reduce.start_cores(1)

    def act(stage, at):
        if remote:
            getattr(reduce, stage)(at)

    staged = mlp.at[1, pl.ds(512, seq_len), main]
    branch = mlp.at[0, pl.ds(0, seq_len), main]
    flat = [mlp.at[1, pl.ds(0, seq_len), pl.ds(width * member, width)] for member in range(3)]
    flats = mlp.at[1, pl.ds(0, seq_len), pl.ds(0, 3 * width)]

    def second_norm_back(index):
        rows = rows_of(index, block)
        lines = (after[rows, side_columns] * chosen).astype(BF16)
        inner_back[rows, pl.ds(0, LANES)] = lines
        residual = middle[rows, :]
        staged[rows, :] = (residual + (after[rows, main] + dot_nn(lines, down[5]))).astype(BF16)
        lines = (back[rows, side_columns] * chosen).astype(BF16)
        inner_back[rows, pl.ds(LANES, LANES)] = lines
        gradient = back[rows, main] + dot_nn(lines, down[4])
        normal, inverse = layer_stats(residual)
        total = cotangent[rows, main].astype(F32) + norm_back(gradient, normal, inverse, gain_two)
        middle[rows, :] = total
        lines = total.astype(BF16)
        branch[rows, :] = lines
        both = dot_nt(lines, square[:, pl.ds(3 * width, width)])
        lines = (both[:, width:] * chosen).astype(BF16)
        inner_back[rows, pl.ds(2 * LANES, LANES)] = lines
        flat[0][rows, :] = (both[:, :width] + dot_nn(lines, down[3])).astype(BF16)

    repeat(0, blocks, second_norm_back)
    emit(staged, output)
    act("start_first", 0)
    act("start_first", 1)
    for head in range(heads):
        mixed[:, LANES * head : LANES * head + HEAD_DIM] = flat[0][
            :, HEAD_DIM * head : HEAD_DIM * (head + 1)
        ]
    narrow_blocks = mlp.at[1, pl.ds(512, 4 * LANES), pl.ds(width, width)]
    for index, (left, right) in enumerate(
        (
            (inner_back[:, pl.ds(LANES, LANES)], normed_two[:, main]),
            (inner_back[:, pl.ds(0, LANES)], cotangent[:, main]),
            (inner_back[:, pl.ds(2 * LANES, LANES)], attended[:, main]),
            (attended[:, side_columns], branch[...]),
        )
    ):
        narrow_blocks[pl.ds(LANES * index, LANES), :] = dot_tn(left, right).astype(BF16)
    act("start_cores", 2)
    act("start_cores", 3)
    spread = heads * LANES
    grads = [
        mlp.at[0, pl.ds(0, seq_len), pl.ds(0, spread)],
        mlp.at[0, pl.ds(0, seq_len), pl.ds(spread, spread)],
        mlp.at[0, pl.ds(512, seq_len), pl.ds(0, spread)],
    ]

    def attend_back(pair):
        for head in (2 * pair, 2 * pair + 1):
            columns = rows_of(head, LANES)
            lines, keys = query[:, columns], key[:, columns]
            gradient = mixed[:, columns]
            probs = jnp.exp(dot_nt(keys, lines) * scaling)
            grad_probs = dot_nt(value[:, columns], gradient)
            level = jnp.sum(probs * grad_probs, axis=0, keepdims=True)
            grad_scores = (probs * (grad_probs - level)).astype(BF16)
            grads[2][:, columns] = dot_nn(probs.astype(BF16), gradient).astype(BF16)
            grads[1][:, columns] = (dot_nn(grad_scores, lines) * scaling).astype(BF16)
            grads[0][:, columns] = (dot_tn(grad_scores, keys) * scaling).astype(BF16)

    repeat(0, 3, attend_back)
    for at in (0, 1):
        act("start_second", at)
    for at in (2, 3):
        act("start_first", at)
    repeat(3, 6, attend_back)
    for at in (0, 1):
        act("start_z", at)
    for at in (2, 3):
        act("start_second", at)
    repeat(6, heads // 2, attend_back)
    for at in (2, 3):
        act("start_z", at)
    part = result_square.shape[3]

    def put_square(side, member, value):
        for index in range(4):
            low, high = max(index * part, member * width), min((index + 1) * part, (member + 1) * width)
            if low < high:
                place = phases[SQUARE_PHASE + index % 2].block(index // 2, side)
                place[:, low - index * part : high - index * part] = value[
                    :, low - member * width : high - member * width
                ]

    for side in range(2):
        phases[SQUARE_PHASE + 1].block(1, side)[:, 3 * width - 3 * part :] = jnp.zeros((LANES, 4 * part - 3 * width), BF16)
    for member in range(3):
        for head in range(heads):
            flat[member][:, HEAD_DIM * head : HEAD_DIM * (head + 1)] = grads[member][
                :, LANES * head : LANES * head + HEAD_DIM
            ]
        lines = dot_nt(flat[member][...], square[pl.ds(width, LANES), pl.ds(member * width, width)])
        inner_back[:, pl.ds(member * LANES, LANES)] = (lines * chosen).astype(BF16)
        put_square(1, member, dot_tn(inner[:, pl.ds(member * LANES, LANES)], flat[member][...]).astype(BF16))
    downs = dot_tn(inner_back[...], normed[:, main]).astype(BF16)
    for member in range(3):
        put_square(0, member, downs[member * LANES : (member + 1) * LANES])
    last_phases = (SQUARE_PHASE, SQUARE_PHASE + 1)
    for at in last_phases:
        act("start_cores", at)
    for at in range(SQUARE_PHASE):
        act("start_result", at)
    small = block // 2

    def project_back(index):
        rows = rows_of(index, small)
        total = dot_nt(flats[rows, :], square[pl.ds(0, width), pl.ds(0, 3 * width)])
        back[rows, main] = total + dot_nn(inner_back[rows, :], down[0:3].reshape(3 * LANES, width))

    repeat(0, 1, project_back)
    for at in last_phases:
        act("start_first", at)
    repeat(1, seq_len // small, project_back)
    for at in last_phases:
        act("start_second", at)

    def first_norm_back(index):
        rows = rows_of(index, 64)
        normal, inverse = layer_stats(tokens[rows, :].astype(F32))
        total = middle[rows, :] + norm_back(back[rows, main], normal, inverse, gain_one)
        normed_two[rows, main] = total.astype(BF16)

    repeat(0, seq_len // 64, first_norm_back)
    emit(normed_two.at[:, main], input_grad)
    if remote:
        for at in last_phases:
            reduce.start_z(at)
        for at in range(SQUARE_PHASE):
            reduce.finish(at)
        one, two = WIDE_PARTS
        for which, grad in ((1, grads_two), (0, grads_four)):
            for side in range(2):
                quarter = result_wide.at[2 * side + which]
                grad[:, side * one : (side + 1) * one] = quarter[:, :one].astype(F32)
                low = 2 * one + side * two
                high = min(low + two, grad.shape[1])
                grad[:, low:high] = quarter[:, one : one + high - low].astype(F32)
        for side, grad in ((0, grads_one), (1, grads_three)):
            grad[4] = result_narrow[2 * side].astype(F32)
            grad[3] = result_narrow[2 * side + 1].astype(F32)
        for at in last_phases:
            reduce.start_result(at)
        for at in range(SQUARE_PHASE):
            reduce.sent(at)
        for at in last_phases:
            reduce.finish(at)
        for side, grad in ((0, grads_one), (1, grads_three)):
            for member in range(3):
                for index in range(4):
                    low, high = max(index * part, member * width), min((index + 1) * part, (member + 1) * width)
                    if low < high:
                        grad[member, :, low - member * width : high - member * width] = result_square[
                            index % 2, 2 * side + index // 2, :, low - index * part : high - index * part
                        ].astype(F32)
        for at in last_phases:
            reduce.sent(at)
    else:
        emit(mlp.at[:, pl.ds(width, LANES), :], grads_one)
        for index in range(4):
            c, y = index // 2, index % 2
            emit(narrow_blocks.at[pl.ds(LANES * index, LANES), :], grads_two.at[c, y])
            emit(phases[SQUARE_PHASE].block(c, y), grads_three.at[c, y])
            emit(phases[SQUARE_PHASE + 1].block(c, y), grads_four.at[c, y])
    for copy in outgoing:
        copy.wait()


def copy_kernel(count, *refs):
    sources, targets, buffers = refs[:count], refs[count : 2 * count], refs[2 * count : 3 * count]
    sems = refs[3 * count]
    arrive = [pltpu.make_async_copy(sources[at], buffers[at], sems.at[0, at]) for at in range(count)]
    leave = [pltpu.make_async_copy(buffers[at], targets[at], sems.at[1, at]) for at in range(count)]
    for copy in arrive:
        copy.start()
    for first, second in zip(arrive, leave):
        first.wait()
        second.start()
    for copy in leave:
        copy.wait()


def moved(values):
    count = len(values)
    anywhere = pl.BlockSpec(memory_space=pl.ANY)
    return pl.pallas_call(
        functools.partial(copy_kernel, count),
        out_shape=[jax.ShapeDtypeStruct(each.shape, each.dtype) for each in values],
        in_specs=[anywhere] * count,
        out_specs=[anywhere] * count,
        scratch_shapes=[pltpu.VMEM(each.shape, each.dtype) for each in values]
        + [pltpu.SemaphoreType.DMA((2, count))],
        name="moved",
    )(*values)


def layer(remote, features, tokens, cotangent, adapter, *rest):
    seq_len, width = tokens.shape
    spread = rest[-1].shape[2]
    heads = width // HEAD_DIM
    anywhere = pl.BlockSpec(memory_space=pl.ANY)
    here = pl.BlockSpec(memory_space=pltpu.VMEM)
    shape = jax.ShapeDtypeStruct
    count = len(GROUPS)
    part = 896
    links = []
    if remote:
        links = [pltpu.SemaphoreType.DMA((count, 28))] * 2 + [pltpu.SemaphoreType.REGULAR((7,))]
        links += [pltpu.SemaphoreType.DMA((SQUARE_PHASE + 2, 10))] * 2
        grads = (
            shape((5, 16, width), F32),
            shape((16, features), F32),
            shape((5, 16, width), F32),
            shape((16, features), F32),
        )
    else:
        grads = (
            shape((2, LANES, spread), BF16),
            shape((2, 2, LANES, width), BF16),
            shape((2, 2, LANES, part), BF16),
            shape((2, 2, LANES, part), BF16),
        )
    deep = width + LANES
    return pl.pallas_call(
        functools.partial(layer_kernel, remote),
        out_shape=(shape((seq_len, width), BF16), shape((seq_len, width), BF16), *grads),
        in_specs=[here, anywhere, pl.BlockSpec(memory_space=pltpu.SMEM)] + [here] * 4 + [anywhere] * 5,
        out_specs=[anywhere] * 2 + [here if remote else anywhere] * 4,
        scratch_shapes=[
            pltpu.VMEM((deep, 4 * width), BF16),
            pltpu.VMEM((6, LANES, width), BF16),
            pltpu.VMEM((2, deep, spread), BF16),
            pltpu.VMEM((seq_len, heads * LANES), BF16),
            pltpu.VMEM((seq_len, heads * LANES), BF16),
            pltpu.VMEM((seq_len, heads * LANES), BF16),
            pltpu.VMEM((seq_len, heads * LANES), BF16),
            pltpu.VMEM((seq_len, deep), BF16),
            pltpu.VMEM((seq_len, deep), BF16),
            pltpu.VMEM((seq_len, deep), BF16),
            pltpu.VMEM((seq_len, deep), BF16),
            pltpu.VMEM((seq_len, width), F32),
            pltpu.VMEM((seq_len, deep), F32),
            pltpu.VMEM((seq_len, deep), F32),
            pltpu.VMEM((seq_len, 3 * LANES), BF16),
            pltpu.VMEM((seq_len, 3 * LANES), BF16),
            pltpu.VMEM((4, 16, spread // 2), BF16),
            pltpu.VMEM((4, 16, width), BF16),
            pltpu.VMEM((2, 4, 16, part), BF16),
            pltpu.SemaphoreType.DMA((32,)),
            *links,
        ],
        compiler_params=pltpu.CompilerParams(
            has_side_effects=True,
            vmem_limit_bytes=64 * 1024 * 1024,
            collective_id=0 if remote else None,
        ),
        name="layer" if remote else "layer_alone",
    )(tokens, cotangent, adapter, *rest)


def per_device(
    tokens,
    cotangent,
    adapter_ids,
    gain_one,
    shift_one,
    gain_two,
    shift_two,
    qkv_weight,
    out_weight,
    mlp_first,
    mlp_second,
    down_narrow,
    down_wide,
    up_narrow,
    up_wide,
):
    features = mlp_first.shape[1]
    depth = mlp_first.shape[0]
    mlp = jnp.stack(
        [
            jnp.concatenate([mlp_first, up_wide], axis=0),
            jnp.concatenate([mlp_second.T, down_wide], axis=0),
        ]
    )
    mlp = jnp.pad(mlp, ((0, 0), (0, 0), (0, -features % 256)))
    vectors = (gain_one, shift_one, gain_two, shift_two)
    weights = [qkv_weight, out_weight, down_narrow, up_narrow, mlp]
    remote = (lax.axis_size("rep"), lax.axis_size("shard")) == (4, 8)
    if not remote:
        parts = (qkv_weight, out_weight, down_narrow, up_narrow, mlp[:, :depth], mlp[:, depth:])
        parts = [
            lax.all_gather(each, "shard", axis=each.ndim - 2, tiled=True) for each in parts
        ]
        weights = parts[:4] + [jnp.concatenate(parts[4:], axis=1)]
    output, input_grad, *grads = layer(
        remote, features, tokens[0], cotangent[0], adapter_ids, *vectors, *weights
    )
    if remote:
        output, input_grad, *grads = moved([output, input_grad, *grads])
    else:
        grads = reduced(features, *grads)
    return (output[None], input_grad[None], *grads)


def reduced(features, wide, narrow, square, square_more):
    width = narrow.shape[3]
    downs, ups = [
        jnp.concatenate([square[0, side], square_more[0, side], square[1, side], square_more[1, side]], axis=1)
        for side in range(2)
    ]
    parts = [downs[:, : 3 * width], narrow[1, 0], narrow[0, 0], ups[:, : 3 * width], narrow[1, 1], narrow[0, 1]]
    parts = parts + [wide[1, :, :features], wide[0, :, :features]]
    share = lax.psum_scatter(jnp.concatenate(parts, axis=1), "shard", scatter_dimension=0, tiled=True)
    total = lax.psum(share, "rep").astype(F32)
    narrows = total[:, : 10 * width].reshape(-1, 10, width).transpose(1, 0, 2)
    wides = total[:, 10 * width :].reshape(-1, 2, features)
    return (narrows[:5], wides[:, 0], narrows[5:], wides[:, 1])


def solution(mesh):
    return jax.shard_map(
        per_device,
        mesh=mesh,
        in_specs=(
            P(("rep", "shard"), None, None),
            P(("rep", "shard"), None, None),
            P(("rep", "shard"), None),
            P(),
            P(),
            P(),
            P(),
            P(None, "shard", None),
            P("shard", None),
            P("shard", None),
            P(None, "shard"),
            P(None, "shard", None),
            P("shard", None),
            P(None, "shard", None),
            P("shard", None),
        ),
        out_specs=(
            P(("rep", "shard"), None, None),
            P(("rep", "shard"), None, None),
            P(None, "shard", None),
            P("shard", None),
            P(None, "shard", None),
            P("shard", None),
        ),
        check_vma=False,
    )
```

```python
import functools

import jax
import jax.numpy as jnp
from jax import lax
from jax.experimental import pallas as pl
from jax.experimental.pallas import tpu as pltpu
from jax.sharding import PartitionSpec as P

HEAD_DIM = 72
RANK = 16
GELU_SCALE = 0.7978845608028654
GELU_CUBE = 0.044715
MESH = pl.DeviceIdType.MESH
LANES = 128
BF16 = jnp.bfloat16
F32 = jnp.float32
CUTS = [(0, 1024), (1024, 1024), (2048, 1024), (3072, 1024), (4096, 256)]
CROSSED, PLAIN = 768, 256
GROUPS = [("down", 0, False), ("up", 0, False)]
GROUPS += [("square", part, True) for part in range(3)]
GROUPS += [("wide", 0, False)]
BATCHES = [[2, 0], [3, 1], [4, 5]]
for each in range(len(CUTS)):
    BATCHES.append([])
    if CUTS[each][1] > PLAIN:
        BATCHES[-1].append(len(GROUPS))
        GROUPS.append(("mlp", each, True))
    BATCHES[-1].append(len(GROUPS))
    GROUPS.append(("mlp", each, False))
FIRST_CUT = 3
SETTLE = 40
WIDE_PARTS, NARROW_PARTS = (1152, 1024), (640, 512)
SQUARE_PHASE = 4
SEND, OWN, PLANE, ACROSS, BESIDE, CORNER, COMPUTE = range(7)
ORDER = (
    (0, 0, 0), (1, 1, 0), (1, 0, 0), (1, 3, 0), (0, 2, 0), (3, 0, 0), (1, 2, 0), (3, 2, 0),
    (6, 0, 0), (2, 0, 0), (2, 2, 0), (3, 1, 0), (2, 0, 1), (3, 0, 1), (2, 0, 2), (3, 3, 0),
    (0, 1, 0), (1, 4, 0), (2, 2, 1), (0, 3, 0), (3, 2, 1), (3, 0, 2), (4, 2, 0), (2, 2, 2),
    (5, 2, 0), (5, 2, 1), (4, 2, 1), (1, 5, 0), (3, 0, 3), (4, 2, 2), (6, 1, 0), (2, 1, 0),
    (3, 4, 0), (3, 2, 2), (0, 4, 0), (5, 3, 0), (0, 5, 0), (2, 3, 0), (2, 3, 2), (2, 1, 1),
    (3, 1, 2), (1, 7, 0), (2, 1, 2), (3, 2, 3), (2, 3, 1), (3, 7, 0), (3, 3, 1), (1, 6, 0),
    (3, 1, 3), (3, 3, 3), (5, 4, 0), (4, 3, 0), (5, 2, 3), (3, 3, 2), (1, 8, 0), (2, 4, 0),
    (4, 3, 2), (2, 4, 1), (2, 5, 0), (5, 3, 1), (0, 7, 0), (2, 4, 2), (0, 6, 0), (5, 3, 3),
    (5, 2, 2), (2, 5, 1), (5, 3, 2), (4, 3, 1), (2, 5, 2), (3, 6, 0), (1, 9, 0), (4, 4, 1),
    (3, 1, 1), (3, 4, 1), (4, 4, 0), (3, 4, 2), (3, 4, 3), (5, 6, 0), (2, 7, 1), (2, 7, 2),
    (1, 11, 0), (3, 9, 0), (4, 4, 2), (5, 4, 2), (3, 5, 0), (2, 7, 0), (3, 5, 2), (3, 5, 1),
    (5, 4, 1), (3, 8, 0), (0, 9, 0), (2, 6, 0), (0, 8, 0), (5, 4, 3), (2, 6, 1), (6, 2, 0),
    (6, 3, 0), (2, 6, 2), (6, 4, 0), (6, 5, 0), (6, 6, 0), (3, 7, 2), (1, 10, 0), (6, 7, 0),
    (3, 6, 1), (6, 8, 0), (3, 7, 3), (3, 6, 2), (1, 12, 0), (1, 13, 0), (3, 11, 0), (0, 11, 0),
    (3, 5, 3), (3, 6, 3), (3, 10, 0), (2, 9, 2), (6, 9, 0), (6, 10, 0), (2, 9, 0), (3, 7, 1),
    (5, 6, 1), (6, 11, 0), (0, 10, 0), (6, 12, 0), (2, 8, 0), (6, 13, 0), (5, 8, 0), (5, 6, 2),
    (3, 13, 0), (2, 9, 1), (2, 8, 2), (6, 14, 0), (6, 15, 0), (6, 16, 0), (6, 17, 0), (3, 8, 1),
    (4, 8, 0), (1, 14, 0), (2, 11, 0), (2, 8, 1), (3, 12, 0), (6, 18, 0), (3, 9, 3), (4, 6, 2),
    (6, 19, 0), (3, 9, 2), (3, 9, 1), (5, 6, 3), (5, 10, 0), (4, 6, 1), (4, 8, 2), (6, 20, 0),
    (0, 13, 0), (6, 21, 0), (4, 6, 0), (3, 8, 2), (6, 22, 0), (6, 23, 0), (2, 10, 2), (3, 11, 1),
    (6, 24, 0), (2, 10, 0), (5, 8, 1), (2, 11, 2), (3, 8, 3), (0, 12, 0), (2, 10, 1), (6, 25, 0),
    (6, 26, 0), (4, 8, 1), (6, 27, 0), (2, 11, 1), (3, 11, 3), (3, 10, 2), (4, 10, 1), (0, 14, 0),
    (5, 8, 3), (3, 10, 1), (3, 10, 3), (2, 13, 0), (2, 12, 0), (2, 13, 2), (2, 12, 1), (4, 10, 2),
    (2, 12, 2), (5, 12, 0), (5, 8, 2), (4, 10, 0), (6, 28, 0), (2, 13, 1), (6, 29, 0), (6, 30, 0),
    (5, 10, 3), (5, 10, 1), (4, 12, 0), (3, 12, 1), (3, 12, 2), (3, 11, 2), (4, 12, 2), (5, 10, 2),
    (2, 14, 2), (3, 12, 3), (2, 14, 1), (3, 13, 1), (2, 14, 0), (6, 31, 0), (6, 32, 0), (4, 12, 1),
    (5, 12, 1), (5, 12, 3), (5, 12, 2), (3, 13, 3), (3, 13, 2), (3, 14, 1), (3, 14, 2), (3, 14, 3),
    (3, 14, 0), (6, 33, 0), (6, 34, 0), (6, 35, 0), (6, 36, 0),
)


def dot_nn(left, right):
    return jnp.dot(left, right, preferred_element_type=F32)


def dot_nt(left, right):
    return lax.dot_general(left, right, (((1,), (1,)), ((), ())), preferred_element_type=F32)


def dot_tn(left, right):
    return lax.dot_general(left, right, (((0,), (0,)), ((), ())), preferred_element_type=F32)


def repeat(low, high, step):
    def body(index, carry):
        step(index)
        return carry

    lax.fori_loop(low, high, body, 0)


def rows_of(index, count):
    return pl.ds(pl.multiple_of(index * count, count), count)


def layer_stats(value):
    average = jnp.mean(value, axis=-1, keepdims=True)
    centred = value - average
    spread = jnp.mean(centred * centred, axis=-1, keepdims=True)
    inverse = lax.rsqrt(spread + 1e-06)
    return (centred * inverse, inverse)


def norm_back(gradient, normal_part, inverse, gain):
    scaled = gradient * gain
    return inverse * (
        scaled
        - jnp.mean(scaled, axis=-1, keepdims=True)
        - normal_part * jnp.mean(scaled * normal_part, axis=-1, keepdims=True)
    )


class Gather:
    def __init__(self, whole, send, receive):
        self.whole, self.send, self.receive = whole, send, receive
        rep, shard = lax.axis_index("rep"), lax.axis_index("shard")
        self.y, self.c = rep // 2, lax.rem(rep, 2)
        self.z, self.x = shard // 2, lax.rem(shard, 2)

    def piece(self, at, y, c, z, x):
        kind, part, _ = GROUPS[at]
        square, down, mlp = self.whole
        width, depth = down.shape[2], down.shape[2]
        shard, slot = 2 * z + x, 4 * x + z
        extra = pl.ds(pl.multiple_of(depth + 16 * slot, 16), 16)
        if kind == "down":
            return down.at[pl.ds(3 * c, 3), rows_of(slot, 16)]
        if kind == "up":
            return square.at[extra, pl.ds(pl.multiple_of(2 * width * c, LANES), 2 * width)]
        if kind == "square":
            rows = pl.ds(pl.multiple_of(144 * shard + 48 * part, 16), 48)
            return square.at[rows, pl.ds(pl.multiple_of(width * (2 * y + c), LANES), width)]
        if kind == "wide":
            return mlp.at[c, extra, :]
        start, count = CUTS[part]
        rows = pl.ds(pl.multiple_of(144 * shard, 16), 144)
        if not GROUPS[at][2]:
            return mlp.at[c, rows, pl.ds(start + count - PLAIN, PLAIN)]
        return mlp.at[c, rows, pl.ds(pl.multiple_of(start + (CROSSED // 2) * y, LANES), CROSSED // 2)]

    def device(self, y=None, c=None, z=None, x=None):
        y = self.y if y is None else y
        c = self.c if c is None else c
        z = self.z if z is None else z
        x = self.x if x is None else x
        return (2 * y + c, 2 * z + x)

    def source(self, hop):
        return lax.rem(self.z + 4 - hop, 4)

    def copy(self, at, slot, y, z, x, device):
        piece = self.piece(at, y, self.c, z, x)
        return pltpu.make_async_remote_copy(
            piece,
            piece,
            self.send.at[at, slot],
            self.receive.at[at, slot],
            device_id=device,
            device_id_type=MESH,
        )

    def along_z(self, at, hop):
        return self.copy(at, hop - 1, self.y, self.z, self.x, self.device(z=lax.rem(self.z + hop, 4)))

    def over_x(self, at, hop):
        return self.copy(at, 3 + hop, self.y, self.source(hop), self.x, self.device(x=1 - self.x))

    def over_y(self, at, hop):
        return self.copy(at, 6 + hop, self.y, self.source(hop), self.x, self.device(y=1 - self.y))

    def corner(self, at, hop):
        return self.copy(at, 10 + hop, self.y, self.source(hop), 1 - self.x, self.device(y=1 - self.y))

    def to_core(self, at, slot, y, hop, x):
        return self.copy(at, slot, y, self.source(hop), x, self.device(c=1 - self.c))

    def core_z(self, at, hop):
        return self.to_core(at, 13 + hop, self.y, hop, self.x)

    def core_x(self, at, hop):
        return self.to_core(at, 17 + hop, self.y, hop, 1 - self.x)

    def core_y(self, at, hop):
        return self.to_core(at, 20 + hop, 1 - self.y, hop, self.x)

    def core_corner(self, at, hop):
        return self.to_core(at, 24 + hop, 1 - self.y, hop, 1 - self.x)

    def greet(self):
        ready = pltpu.get_barrier_semaphore()
        partners = [self.device(z=lax.rem(self.z + hop, 4)) for hop in (1, 2, 3)]
        partners += [self.device(x=1 - self.x), self.device(y=1 - self.y), self.device(c=1 - self.c)]
        partners.append(self.device(y=1 - self.y, c=1 - self.c))
        for partner in partners:
            pl.semaphore_signal(ready, 1, device_id=partner, device_id_type=MESH)
        return lambda: pl.semaphore_wait(ready, len(partners))

    def hop_of(self, index):
        near = 1 + 2 * ((3 - self.z) // 3)
        middle = 2 + lax.rem((self.z + 1) // 2, 2)
        return (near, middle, 6 - near - middle)[index]

    def step(self, what, at, index):
        crossed = GROUPS[at][2]
        if what == SEND:
            repeat(1, 4, lambda hop: self.along_z(at, hop).start())
        elif what == OWN:
            self.over_x(at, 0).start()
        elif what == PLANE:
            hop = self.hop_of(index)
            self.along_z(at, hop).wait_recv()
            if crossed:
                self.over_y(at, hop).start()
            self.over_x(at, hop).start()
            self.core_z(at, hop).start()
        elif what == ACROSS:
            hop = self.hop_of(index - 1) if index else 0
            self.over_x(at, hop).wait_recv()
            if crossed:
                self.corner(at, hop).start()
            self.core_x(at, hop).start()
        elif what == BESIDE:
            hop = self.hop_of(index)
            self.over_y(at, hop).wait_recv()
            self.core_y(at, hop).start()
        else:
            hop = self.hop_of(index - 1) if index else 0
            self.corner(at, hop).wait_recv()
            self.core_corner(at, hop).start()

    def copies_of(self, at):
        links, cores = [(self.along_z, 1), (self.over_x, 0)], [(self.core_z, 1), (self.core_x, 0)]
        if GROUPS[at][2]:
            links += [(self.over_y, 1), (self.corner, 0)]
            cores += [(self.core_y, 1), (self.core_corner, 0)]
        return links, cores

    def arrived(self, at):
        for copy, first in self.copies_of(at)[1]:
            repeat(first, 4, lambda hop: copy(at, hop).wait_recv())

    def sent(self, at):
        links, cores = self.copies_of(at)
        for copy, first in links + cores:
            repeat(first, 4, lambda hop: copy(at, hop).wait_send())


class Reduce:
    def __init__(self, net, free, phases, send, receive):
        self.net, self.free, self.phases = net, free, phases
        self.send, self.receive = send, receive
        self.partners = [
            net.device(c=1 - net.c),
            net.device(y=1 - net.y),
            net.device(x=1 - net.x),
        ]
        self.partners += [net.device(z=lax.rem(net.z + hop, 4)) for hop in (1, 2, 3)]
        self.partners.append(net.device(y=1 - net.y, c=1 - net.c))
        self.open = [False] * len(self.partners)

    def offer(self):
        for index, partner in enumerate(self.partners):
            pl.semaphore_signal(self.free.at[(0, 1, 2, 5, 4, 3, 6)[index]], 1, device_id=partner, device_id_type=MESH)

    def accept(self, index):
        if not self.open[index]:
            self.open[index] = True
            pl.semaphore_wait(self.free.at[index], 1)

    def copy(self, at, slot, source, target, index):
        return pltpu.make_async_remote_copy(
            source,
            target,
            self.send.at[at, slot],
            self.receive.at[at, slot],
            device_id=self.partners[index],
            device_id_type=MESH,
        )

    def across_cores(self, at):
        phase = self.phases[at]
        return self.copy(at, 0, phase.both(1 - self.net.c), phase.from_core, 0)

    def first_copies(self, at):
        phase, net = self.phases[at], self.net
        if not phase.by_x:
            return [self.copy(at, 1, phase.block(net.c, 1 - net.y), phase.from_first, 1)]
        return [
            self.copy(
                at,
                1 + side,
                phase.block(net.c, side).at[rows_of(1 - net.x, 64), :],
                phase.from_first.at[pl.ds(64 * side, 64), :],
                2,
            )
            for side in range(2)
        ]

    def second_copy(self, at):
        phase, net = self.phases[at], self.net
        if phase.by_x:
            source = phase.block(net.c, 1 - net.y).at[rows_of(net.x, 64), :]
        else:
            source = phase.block(net.c, net.y).at[rows_of(1 - net.x, 64), :]
        return self.copy(at, 3, source, phase.from_second, 1 if phase.by_x else 2)

    def across_z(self, at, hop):
        phase, net = self.phases[at], self.net
        there = lax.rem(net.z + hop, 4)
        source = phase.block(net.c, net.y).at[pl.ds(pl.multiple_of(64 * net.x + 16 * there, 16), 16), :]
        return self.copy(at, 3 + hop, source, phase.from_z.at[pl.ds(16 * (hop - 1), 16), :], 2 + hop)

    def result(self, at, index):
        net = self.net
        mine = self.phases[at].result(2 * net.y + net.c)
        return self.copy(at, 7 + index, mine, mine, (0, 1, 6)[index])

    def start_cores(self, at):
        self.accept(0)
        self.across_cores(at).start()

    def start_first(self, at):
        phase, net = self.phases[at], self.net
        self.across_cores(at).wait_recv()
        for side in range(2):
            add_into(phase.block(net.c, side), phase.core_part(side))
        self.accept(2 if phase.by_x else 1)
        for copy in self.first_copies(at):
            copy.start()

    def start_second(self, at):
        phase, net = self.phases[at], self.net
        for copy in self.first_copies(at):
            copy.wait_recv()
        if phase.by_x:
            for side in range(2):
                rows = rows_of(net.x, 64)
                add_into(phase.block(net.c, side).at[rows, :], phase.from_first.at[pl.ds(64 * side, 64), :])
        else:
            add_into(phase.block(net.c, net.y), phase.from_first)
        self.accept(1 if phase.by_x else 2)
        self.second_copy(at).start()

    def start_z(self, at):
        phase, net = self.phases[at], self.net
        self.second_copy(at).wait_recv()
        add_into(phase.block(net.c, net.y).at[rows_of(net.x, 64), :], phase.from_second)
        for hop in (1, 2, 3):
            self.accept(2 + hop)
            self.across_z(at, hop).start()

    def start_result(self, at):
        phase, net = self.phases[at], self.net
        for hop in (1, 2, 3):
            self.across_z(at, hop).wait_recv()
        mine = phase.block(net.c, net.y).at[pl.ds(pl.multiple_of(64 * net.x + 16 * net.z, 16), 16), :]
        total = mine[...].astype(F32)
        for hop in (0, 1, 2):
            total = total + phase.from_z[pl.ds(16 * hop, 16), :].astype(F32)
        phase.result(2 * net.y + net.c)[...] = total.astype(BF16)
        for index in range(3):
            self.accept((0, 1, 6)[index])
            self.result(at, index).start()

    def finish(self, at):
        for index in range(3):
            self.result(at, index).wait_recv()

    def sent(self, at):
        copies = [self.across_cores(at), *self.first_copies(at), self.second_copy(at)]
        copies += [self.across_z(at, hop) for hop in (1, 2, 3)]
        copies += [self.result(at, index) for index in range(3)]
        for copy in copies:
            copy.wait_send()


class Phase:
    def __init__(self, by_x, both, block, from_core, core_part, from_first, from_second, from_z, result):
        self.by_x, self.both, self.block = by_x, both, block
        self.from_core, self.core_part, self.result = from_core, core_part, result
        self.from_first, self.from_second, self.from_z = from_first, from_second, from_z


def add_into(target, other):
    def step(index):
        rows = rows_of(index, 32)
        target[rows, :] = (target[rows, :].astype(F32) + other[rows, :].astype(F32)).astype(BF16)

    repeat(0, target.shape[0] // 32, step)


def phases_of(mlp, result_wide, result_narrow, result_square):
    width = mlp.shape[1] - LANES
    part = result_square.shape[3]
    phases = []

    def spot(which, row, rows, column, count):
        return mlp.at[which, pl.ds(row, rows), pl.ds(column, count)]

    def wide_phase(by_x, first, count, column, result):
        def block(c, y):
            columns = pl.ds(pl.multiple_of(first + y * count, LANES), count)
            return mlp.at[c, pl.ds(width, LANES), columns]

        arrived = spot(0, 1024, LANES, first, 2 * count)
        phases.append(
            Phase(
                by_x,
                lambda c: mlp.at[c, pl.ds(width, LANES), pl.ds(first, 2 * count)],
                block,
                arrived,
                lambda side: arrived.at[:, pl.ds(count * side, count)],
                spot(1, 1024, LANES, column, count),
                spot(1, 1024, 64, 2176 + column, count),
                spot(1, 1088, 48, 2176 + column, count),
                result,
            )
        )

    def stacked_phase(by_x, which, row, column, count, land, places, result):
        def block(c, y):
            start = pl.multiple_of(row + 256 * c + LANES * y, LANES)
            return mlp.at[which, pl.ds(start, LANES), pl.ds(column, count)]

        def both(c):
            start = pl.multiple_of(row + 256 * c, LANES)
            return mlp.at[which, pl.ds(start, 256), pl.ds(column, count)]

        arrived = spot(1, places[0], 256, land, count)
        phases.append(
            Phase(
                by_x,
                both,
                block,
                arrived,
                lambda side: arrived.at[pl.ds(LANES * side, LANES), :],
                spot(1, places[1], LANES, land, count),
                spot(1, places[2], 64, land, count),
                spot(1, places[3], 48, land, count),
                result,
            )
        )

    wide_first = WIDE_PARTS[0]
    wide_phase(False, 0, wide_first, 0, lambda quarter: result_wide.at[quarter, :, pl.ds(0, wide_first)])
    wide_phase(
        True,
        2 * wide_first,
        WIDE_PARTS[1],
        wide_first,
        lambda quarter: result_wide.at[quarter, :, pl.ds(wide_first, WIDE_PARTS[1])],
    )
    start = 0
    for by_x, count in enumerate(NARROW_PARTS):
        stacked_phase(
            bool(by_x),
            1,
            512,
            width + start,
            count,
            2 * width + start,
            (512, 768, 896, 960),
            lambda quarter, columns=pl.ds(start, count): result_narrow.at[quarter, :, columns],
        )
        start += count
    for member in range(2):
        stacked_phase(
            bool(member),
            0,
            512,
            2048 + part * member,
            part,
            3 * width,
            (256 * member, 512 + LANES * member, 768 + 64 * member, 896 + 48 * member),
            lambda quarter, member=member: result_square.at[member, quarter],
        )
    return phases


def layer_kernel(
    remote,
    tokens,
    cotangent_from,
    adapter,
    gain_one_from,
    shift_one_from,
    gain_two_from,
    shift_two_from,
    qkv_from,
    out_from,
    down_from,
    up_from,
    mlp_from,
    output,
    input_grad,
    grads_one,
    grads_two,
    grads_three,
    grads_four,
    square,
    down,
    mlp,
    query,
    key,
    value,
    mixed,
    normed,
    attended,
    normed_two,
    cotangent,
    middle,
    after,
    back,
    inner,
    inner_back,
    result_wide,
    result_narrow,
    result_square,
    local_sem,
    *link_sems,
):
    seq_len, width = tokens.shape
    heads = width // HEAD_DIM
    scaling = HEAD_DIM ** (-0.5)
    block = 256
    blocks = seq_len // block
    side_columns = pl.ds(width, LANES)
    main = pl.ds(0, width)

    if remote:
        net = Gather((square, down, mlp), *link_sems[:2])
        shard, slot = 2 * net.z + net.x, 4 * net.x + net.z
        step, arrived, sent = net.step, net.arrived, net.sent
        all_here = net.greet()
        number = 4 * lax.rem(adapter[0, 0], 2) + adapter[0, 0] // 2
    else:
        shard = slot = 0
        step = arrived = sent = lambda *at: None
        number = adapter[0, 0]
    ranks = lax.broadcasted_iota(jnp.int32, (1, LANES), 1)
    chosen = jnp.where((ranks >= number * RANK) & (ranks < (number + 1) * RANK), 1.0, 0.0)

    own = []

    def bring(source, target):
        copy = pltpu.make_async_copy(source, target, local_sem.at[len(own)])
        copy.start()
        own.append(copy)

    rank_rows = rows_of(slot, down_from.shape[1])
    extra_rows = pl.ds(pl.multiple_of(width + down_from.shape[1] * slot, 16), down_from.shape[1])
    depth_rows = rows_of(shard, out_from.shape[0])
    bring(down_from, down.at[pl.ds(0, 5), rank_rows])
    bring(up_from.at[4], down.at[5, rank_rows])
    for member in range(4):
        bring(up_from.at[member], square.at[extra_rows, pl.ds(member * width, width)])
    for member in range(3):
        bring(qkv_from.at[member], square.at[depth_rows, pl.ds(member * width, width)])
    bring(out_from, square.at[depth_rows, pl.ds(3 * width, width)])
    bring(mlp_from.at[:, pl.ds(out_from.shape[0], down_from.shape[1]), :], mlp.at[:, extra_rows, :])
    bring(mlp_from.at[:, pl.ds(0, out_from.shape[0]), :], mlp.at[:, depth_rows, :])
    bring(cotangent_from, cotangent.at[:, main])
    gain_one, shift_one, gain_two, shift_two = [
        each[...].reshape(1, width) for each in (gain_one_from, shift_one_from, gain_two_from, shift_two_from)
    ]

    def first_norm(index):
        rows = rows_of(index, 64)
        normal, _ = layer_stats(tokens[rows, :].astype(F32))
        normed[rows, main] = (normal * gain_one + shift_one).astype(BF16)

    lane = lax.rem(lax.broadcasted_iota(jnp.int32, (64, heads * LANES), 1), LANES)
    minus = jnp.where((lane >= HEAD_DIM) & (lane < HEAD_DIM + 3), -1.0, 0.0).astype(BF16)

    def clear(index):
        rows = rows_of(index, 64)
        query[rows, :] = jnp.zeros_like(minus)
        value[rows, :] = jnp.zeros_like(minus)
        key[rows, :] = minus

    def start_block():
        repeat(0, seq_len // 64, first_norm)
        repeat(0, seq_len // 64, clear)

    def inner_of(index):
        rows = rows_of(index, block)
        three = dot_nt(normed[rows, main], down[0:3].reshape(3 * LANES, width))
        inner[rows, :] = (three * jnp.concatenate([chosen] * 3, axis=1)).astype(BF16)

        lines = dot_nt(cotangent[rows, main], down[5])
        cotangent[rows, side_columns] = (lines * chosen).astype(BF16)

    def inner_block():
        arrived(0)
        repeat(0, blocks, inner_of)

    def project(member, index):
        rows = rows_of(index, block)
        normed[rows, side_columns] = inner[rows, pl.ds(member * LANES, LANES)]
        lines = dot_nn(normed[rows, :], square[:, pl.ds(member * width, width)])
        attended[rows, main] = lines.astype(BF16)
        padded = (query, key, value)[member]
        for head in range(heads):
            padded[rows, LANES * head : LANES * head + HEAD_DIM] = attended[
                rows, HEAD_DIM * head : HEAD_DIM * (head + 1)
            ]

    lane = lax.broadcasted_iota(jnp.int32, (block, LANES), 1)

    def attend(head):
        columns = rows_of(head, LANES)
        for part in range(blocks):
            rows = pl.ds(part * block, block)
            lines = query[rows, columns]
            scores = dot_nt(lines, key[:, columns])
            top = jnp.max(scores, axis=-1, keepdims=True)
            exponent = jnp.exp((scores - top) * scaling)
            total = jnp.sum(exponent, axis=-1, keepdims=True)
            probs = (exponent * (1.0 / total)).astype(BF16)
            mixed[rows, columns] = dot_nn(probs, value[:, columns]).astype(BF16)
            level = top + jnp.log(total) * (1.0 / scaling)
            high = level.astype(BF16).astype(F32)
            mid = (level - high).astype(BF16).astype(F32)
            low = level - high - mid
            kept = jnp.where(lane == HEAD_DIM, high, lines.astype(F32))
            kept = jnp.where(lane == HEAD_DIM + 1, mid, kept)
            kept = jnp.where(lane == HEAD_DIM + 2, low, kept)
            query[rows, columns] = kept.astype(BF16)

    def join_heads():
        for head in range(heads):
            attended[:, HEAD_DIM * head : HEAD_DIM * (head + 1)] = mixed[
                :, LANES * head : LANES * head + HEAD_DIM
            ]

    def branch_out(index):
        rows = rows_of(index, block)
        attended[rows, side_columns] = (dot_nt(attended[rows, main], down[3]) * chosen).astype(BF16)
        total = tokens[rows, :].astype(F32) + dot_nn(attended[rows, :], square[:, pl.ds(3 * width, width)])
        middle[rows, :] = total
        normal, _ = layer_stats(total)
        lines = (normal * gain_two + shift_two).astype(BF16)
        normed_two[rows, main] = lines
        normed_two[rows, side_columns] = (dot_nt(lines, down[4]) * chosen).astype(BF16)

    def feed(cut, index):
        start, count = CUTS[cut]
        columns = pl.ds(start, count)
        rows = rows_of(index, block)
        before = dot_nn(normed_two[rows, :], mlp[0, :, columns])
        square_of = before * before
        tangent = jnp.tanh(GELU_SCALE * (before + GELU_CUBE * square_of * before))
        active = (0.5 * before * (1.0 + tangent)).astype(BF16)
        slope = 0.5 * (1.0 + tangent) + 0.5 * before * (1.0 - tangent * tangent) * (
            GELU_SCALE * (1.0 + 3.0 * GELU_CUBE * square_of)
        )
        gradient = dot_nn(cotangent[rows, :], mlp[1, :, columns])
        gradient = (gradient * slope).astype(BF16)
        mixed[rows, pl.ds(0, count)] = active
        mixed[rows, pl.ds(1024, count)] = gradient
        forward = dot_nt(active, mlp[1, :, columns])
        backward = dot_nt(gradient, mlp[0, :, columns])
        after[rows, :] = forward if cut == 0 else after[rows, :] + forward
        back[rows, :] = backward if cut == 0 else back[rows, :] + backward

    def feed_grads(cut):
        start, count = CUTS[cut]
        for which, lines in ((1, cotangent), (0, normed_two)):
            mlp[which, pl.ds(width, LANES), pl.ds(start, count)] = dot_tn(
                lines[:, side_columns], mixed[:, pl.ds(1024 * (1 - which), count)]
            ).astype(BF16)

    start_block()
    if remote:
        all_here()
    for copy in own:
        copy.wait()

    table = [((), lambda: None), ((), inner_block)]
    table += [
        ((1, 2, 3, 4) if (member, index) == (0, 0) else (), functools.partial(project, member, index))
        for member in range(3)
        for index in range(blocks)
    ]
    table += [((), functools.partial(attend, head)) for head in range(heads)]
    table += [((), join_heads)]
    table += [((5,) if index == 0 else (), functools.partial(branch_out, index)) for index in range(blocks)]
    for cut in range(len(CUTS)):
        for index in range(blocks):
            groups = BATCHES[FIRST_CUT + cut] if index == 0 else ()
            table.append((groups, functools.partial(feed, cut, index)))
    first_head = table.index(next(each for each in table if getattr(each[1], "func", None) is attend))
    place = 0 if remote else len(ORDER)
    waited = []
    if not remote:
        inner_block()
        for member in range(3):
            repeat(0, blocks, functools.partial(project, member))
        repeat(0, heads, attend)
        join_heads()
        repeat(0, blocks, branch_out)
        for cut in range(len(CUTS)):
            repeat(0, blocks, functools.partial(feed, cut))
            feed_grads(cut)
    while place < len(ORDER):
        what, at, index = ORDER[place]
        place += 1
        if what != COMPUTE:
            step(what, at, index)
            continue
        head = at - first_head
        if 0 <= head < heads:
            last = head + 1
            while ORDER[place][0] == COMPUTE and ORDER[place][1] - first_head < heads:
                last, place = last + 1, place + 1
            repeat(head, last, attend)
            continue
        groups, run = table[at]
        if groups and groups[0] >= BATCHES[FIRST_CUT][0]:
            later = {group for kind, group, _ in ORDER[max(place - SETTLE, 0) :] if kind != COMPUTE}
            later -= set(range(groups[0] if groups[0] == BATCHES[FIRST_CUT][0] else 0))
            for group in range(len(GROUPS)):
                if group not in later and group not in waited:
                    waited.append(group)
                    sent(group)
        for group in groups:
            arrived(group)
        run()
        if getattr(run, "func", None) is feed and run.args[1] == blocks - 1:
            feed_grads(run.args[0])
    for group in range(len(GROUPS)):
        if group not in waited:
            sent(group)

    outgoing = []

    def emit(source, target):
        copy = pltpu.make_async_copy(source, target, local_sem.at[len(own) + len(outgoing)])
        copy.start()
        outgoing.append(copy)

    phases = phases_of(mlp, result_wide, result_narrow, result_square)
    if remote:
        reduce = Reduce(net, link_sems[2], phases, *link_sems[3:])
        reduce.offer()
        reduce.start_cores(0)
        reduce.start_cores(1)

    def act(stage, at):
        if remote:
            getattr(reduce, stage)(at)

    staged = mlp.at[1, pl.ds(512, seq_len), main]
    branch = mlp.at[0, pl.ds(0, seq_len), main]
    flat = [mlp.at[1, pl.ds(0, seq_len), pl.ds(width * member, width)] for member in range(3)]
    flats = mlp.at[1, pl.ds(0, seq_len), pl.ds(0, 3 * width)]

    def second_norm_back(index):
        rows = rows_of(index, block)
        lines = (after[rows, side_columns] * chosen).astype(BF16)
        inner_back[rows, pl.ds(0, LANES)] = lines
        residual = middle[rows, :]
        staged[rows, :] = (residual + (after[rows, main] + dot_nn(lines, down[5]))).astype(BF16)
        lines = (back[rows, side_columns] * chosen).astype(BF16)
        inner_back[rows, pl.ds(LANES, LANES)] = lines
        gradient = back[rows, main] + dot_nn(lines, down[4])
        normal, inverse = layer_stats(residual)
        total = cotangent[rows, main].astype(F32) + norm_back(gradient, normal, inverse, gain_two)
        middle[rows, :] = total
        lines = total.astype(BF16)
        branch[rows, :] = lines
        both = dot_nt(lines, square[:, pl.ds(3 * width, width)])
        lines = (both[:, width:] * chosen).astype(BF16)
        inner_back[rows, pl.ds(2 * LANES, LANES)] = lines
        flat[0][rows, :] = (both[:, :width] + dot_nn(lines, down[3])).astype(BF16)

    repeat(0, blocks, second_norm_back)
    emit(staged, output)
    act("start_first", 0)
    act("start_first", 1)
    for head in range(heads):
        mixed[:, LANES * head : LANES * head + HEAD_DIM] = flat[0][
            :, HEAD_DIM * head : HEAD_DIM * (head + 1)
        ]
    narrow_blocks = mlp.at[1, pl.ds(512, 4 * LANES), pl.ds(width, width)]
    for index, (left, right) in enumerate(
        (
            (inner_back[:, pl.ds(LANES, LANES)], normed_two[:, main]),
            (inner_back[:, pl.ds(0, LANES)], cotangent[:, main]),
            (inner_back[:, pl.ds(2 * LANES, LANES)], attended[:, main]),
            (attended[:, side_columns], branch[...]),
        )
    ):
        narrow_blocks[pl.ds(LANES * index, LANES), :] = dot_tn(left, right).astype(BF16)
    act("start_cores", 2)
    act("start_cores", 3)
    spread = heads * LANES
    grads = [
        mlp.at[0, pl.ds(0, seq_len), pl.ds(0, spread)],
        mlp.at[0, pl.ds(0, seq_len), pl.ds(spread, spread)],
        mlp.at[0, pl.ds(512, seq_len), pl.ds(0, spread)],
    ]

    def attend_back(pair):
        for head in (2 * pair, 2 * pair + 1):
            columns = rows_of(head, LANES)
            lines, keys = query[:, columns], key[:, columns]
            gradient = mixed[:, columns]
            probs = jnp.exp(dot_nt(keys, lines) * scaling)
            grad_probs = dot_nt(value[:, columns], gradient)
            level = jnp.sum(probs * grad_probs, axis=0, keepdims=True)
            grad_scores = (probs * (grad_probs - level)).astype(BF16)
            grads[2][:, columns] = dot_nn(probs.astype(BF16), gradient).astype(BF16)
            grads[1][:, columns] = (dot_nn(grad_scores, lines) * scaling).astype(BF16)
            grads[0][:, columns] = (dot_tn(grad_scores, keys) * scaling).astype(BF16)

    repeat(0, 3, attend_back)
    for at in (0, 1):
        act("start_second", at)
    for at in (2, 3):
        act("start_first", at)
    repeat(3, 6, attend_back)
    for at in (0, 1):
        act("start_z", at)
    for at in (2, 3):
        act("start_second", at)
    repeat(6, heads // 2, attend_back)
    for at in (2, 3):
        act("start_z", at)
    part = result_square.shape[3]

    def put_square(side, member, value):
        for index in range(4):
            low, high = max(index * part, member * width), min((index + 1) * part, (member + 1) * width)
            if low < high:
                place = phases[SQUARE_PHASE + index % 2].block(index // 2, side)
                place[:, low - index * part : high - index * part] = value[
                    :, low - member * width : high - member * width
                ]

    for side in range(2):
        phases[SQUARE_PHASE + 1].block(1, side)[:, 3 * width - 3 * part :] = jnp.zeros((LANES, 4 * part - 3 * width), BF16)
    for member in range(3):
        for head in range(heads):
            flat[member][:, HEAD_DIM * head : HEAD_DIM * (head + 1)] = grads[member][
                :, LANES * head : LANES * head + HEAD_DIM
            ]
        lines = dot_nt(flat[member][...], square[pl.ds(width, LANES), pl.ds(member * width, width)])
        inner_back[:, pl.ds(member * LANES, LANES)] = (lines * chosen).astype(BF16)
        put_square(1, member, dot_tn(inner[:, pl.ds(member * LANES, LANES)], flat[member][...]).astype(BF16))
    downs = dot_tn(inner_back[...], normed[:, main]).astype(BF16)
    for member in range(3):
        put_square(0, member, downs[member * LANES : (member + 1) * LANES])
    last_phases = (SQUARE_PHASE, SQUARE_PHASE + 1)
    for at in last_phases:
        act("start_cores", at)
    for at in (0, 1):
        act("start_result", at)
    for at in last_phases:
        act("start_first", at)
    for at in (2, 3):
        act("start_result", at)

    def project_back(index):
        rows = rows_of(index, block)
        total = dot_nt(flats[rows, :], square[pl.ds(0, width), pl.ds(0, 3 * width)])
        back[rows, main] = total + dot_nn(inner_back[rows, :], down[0:3].reshape(3 * LANES, width))

    repeat(0, blocks, project_back)
    for at in last_phases:
        act("start_second", at)

    def first_norm_back(index):
        rows = rows_of(index, 64)
        normal, inverse = layer_stats(tokens[rows, :].astype(F32))
        total = middle[rows, :] + norm_back(back[rows, main], normal, inverse, gain_one)
        normed_two[rows, main] = total.astype(BF16)

    repeat(0, seq_len // 64, first_norm_back)
    emit(normed_two.at[:, main], input_grad)
    if remote:
        for at in last_phases:
            reduce.start_z(at)
        for at in range(SQUARE_PHASE):
            reduce.finish(at)
        one, two = WIDE_PARTS
        for which, grad in ((1, grads_two), (0, grads_four)):
            for side in range(2):
                quarter = result_wide.at[2 * side + which]
                grad[:, side * one : (side + 1) * one] = quarter[:, :one].astype(F32)
                low = 2 * one + side * two
                high = min(low + two, grad.shape[1])
                grad[:, low:high] = quarter[:, one : one + high - low].astype(F32)
        for side, grad in ((0, grads_one), (1, grads_three)):
            grad[4] = result_narrow[2 * side].astype(F32)
            grad[3] = result_narrow[2 * side + 1].astype(F32)
        for at in last_phases:
            reduce.start_result(at)
        for at in range(SQUARE_PHASE):
            reduce.sent(at)
        for at in last_phases:
            reduce.finish(at)
        for side, grad in ((0, grads_one), (1, grads_three)):
            for member in range(3):
                for index in range(4):
                    low, high = max(index * part, member * width), min((index + 1) * part, (member + 1) * width)
                    if low < high:
                        grad[member, :, low - member * width : high - member * width] = result_square[
                            index % 2, 2 * side + index // 2, :, low - index * part : high - index * part
                        ].astype(F32)
        for at in last_phases:
            reduce.sent(at)
    else:
        emit(mlp.at[:, pl.ds(width, LANES), :], grads_one)
        for index in range(4):
            c, y = index // 2, index % 2
            emit(narrow_blocks.at[pl.ds(LANES * index, LANES), :], grads_two.at[c, y])
            emit(phases[SQUARE_PHASE].block(c, y), grads_three.at[c, y])
            emit(phases[SQUARE_PHASE + 1].block(c, y), grads_four.at[c, y])
    for copy in outgoing:
        copy.wait()


def copy_kernel(count, *refs):
    sources, targets, buffers = refs[:count], refs[count : 2 * count], refs[2 * count : 3 * count]
    sems = refs[3 * count]
    arrive = [pltpu.make_async_copy(sources[at], buffers[at], sems.at[0, at]) for at in range(count)]
    leave = [pltpu.make_async_copy(buffers[at], targets[at], sems.at[1, at]) for at in range(count)]
    for copy in arrive:
        copy.start()
    for first, second in zip(arrive, leave):
        first.wait()
        second.start()
    for copy in leave:
        copy.wait()


def moved(values):
    count = len(values)
    anywhere = pl.BlockSpec(memory_space=pl.ANY)
    return pl.pallas_call(
        functools.partial(copy_kernel, count),
        out_shape=[jax.ShapeDtypeStruct(each.shape, each.dtype) for each in values],
        in_specs=[anywhere] * count,
        out_specs=[anywhere] * count,
        scratch_shapes=[pltpu.VMEM(each.shape, each.dtype) for each in values]
        + [pltpu.SemaphoreType.DMA((2, count))],
        name="moved",
    )(*values)


def layer(remote, features, tokens, cotangent, adapter, *rest):
    seq_len, width = tokens.shape
    spread = rest[-1].shape[2]
    heads = width // HEAD_DIM
    anywhere = pl.BlockSpec(memory_space=pl.ANY)
    here = pl.BlockSpec(memory_space=pltpu.VMEM)
    shape = jax.ShapeDtypeStruct
    count = len(GROUPS)
    part = 896
    links = []
    if remote:
        links = [pltpu.SemaphoreType.DMA((count, 28))] * 2 + [pltpu.SemaphoreType.REGULAR((7,))]
        links += [pltpu.SemaphoreType.DMA((SQUARE_PHASE + 2, 10))] * 2
        grads = (
            shape((5, 16, width), F32),
            shape((16, features), F32),
            shape((5, 16, width), F32),
            shape((16, features), F32),
        )
    else:
        grads = (
            shape((2, LANES, spread), BF16),
            shape((2, 2, LANES, width), BF16),
            shape((2, 2, LANES, part), BF16),
            shape((2, 2, LANES, part), BF16),
        )
    deep = width + LANES
    return pl.pallas_call(
        functools.partial(layer_kernel, remote),
        out_shape=(shape((seq_len, width), BF16), shape((seq_len, width), BF16), *grads),
        in_specs=[here, anywhere, pl.BlockSpec(memory_space=pltpu.SMEM)] + [here] * 4 + [anywhere] * 5,
        out_specs=[anywhere] * 2 + [here if remote else anywhere] * 4,
        scratch_shapes=[
            pltpu.VMEM((deep, 4 * width), BF16),
            pltpu.VMEM((6, LANES, width), BF16),
            pltpu.VMEM((2, deep, spread), BF16),
            pltpu.VMEM((seq_len, heads * LANES), BF16),
            pltpu.VMEM((seq_len, heads * LANES), BF16),
            pltpu.VMEM((seq_len, heads * LANES), BF16),
            pltpu.VMEM((seq_len, heads * LANES), BF16),
            pltpu.VMEM((seq_len, deep), BF16),
            pltpu.VMEM((seq_len, deep), BF16),
            pltpu.VMEM((seq_len, deep), BF16),
            pltpu.VMEM((seq_len, deep), BF16),
            pltpu.VMEM((seq_len, width), F32),
            pltpu.VMEM((seq_len, deep), F32),
            pltpu.VMEM((seq_len, deep), F32),
            pltpu.VMEM((seq_len, 3 * LANES), BF16),
            pltpu.VMEM((seq_len, 3 * LANES), BF16),
            pltpu.VMEM((4, 16, spread // 2), BF16),
            pltpu.VMEM((4, 16, width), BF16),
            pltpu.VMEM((2, 4, 16, part), BF16),
            pltpu.SemaphoreType.DMA((32,)),
            *links,
        ],
        compiler_params=pltpu.CompilerParams(
            has_side_effects=True,
            vmem_limit_bytes=64 * 1024 * 1024,
            collective_id=0 if remote else None,
        ),
        name="layer" if remote else "layer_alone",
    )(tokens, cotangent, adapter, *rest)


def per_device(
    tokens,
    cotangent,
    adapter_ids,
    gain_one,
    shift_one,
    gain_two,
    shift_two,
    qkv_weight,
    out_weight,
    mlp_first,
    mlp_second,
    down_narrow,
    down_wide,
    up_narrow,
    up_wide,
):
    features = mlp_first.shape[1]
    depth = mlp_first.shape[0]
    mlp = jnp.stack(
        [
            jnp.concatenate([mlp_first, up_wide], axis=0),
            jnp.concatenate([mlp_second.T, down_wide], axis=0),
        ]
    )
    mlp = jnp.pad(mlp, ((0, 0), (0, 0), (0, -features % 256)))
    vectors = (gain_one, shift_one, gain_two, shift_two)
    weights = [qkv_weight, out_weight, down_narrow, up_narrow, mlp]
    remote = (lax.axis_size("rep"), lax.axis_size("shard")) == (4, 8)
    if not remote:
        parts = (qkv_weight, out_weight, down_narrow, up_narrow, mlp[:, :depth], mlp[:, depth:])
        parts = [
            lax.all_gather(each, "shard", axis=each.ndim - 2, tiled=True) for each in parts
        ]
        weights = parts[:4] + [jnp.concatenate(parts[4:], axis=1)]
    output, input_grad, *grads = layer(
        remote, features, tokens[0], cotangent[0], adapter_ids, *vectors, *weights
    )
    if remote:
        output, input_grad, *grads = moved([output, input_grad, *grads])
    else:
        grads = reduced(features, *grads)
    return (output[None], input_grad[None], *grads)


def reduced(features, wide, narrow, square, square_more):
    width = narrow.shape[3]
    downs, ups = [
        jnp.concatenate([square[0, side], square_more[0, side], square[1, side], square_more[1, side]], axis=1)
        for side in range(2)
    ]
    parts = [downs[:, : 3 * width], narrow[1, 0], narrow[0, 0], ups[:, : 3 * width], narrow[1, 1], narrow[0, 1]]
    parts = parts + [wide[1, :, :features], wide[0, :, :features]]
    share = lax.psum_scatter(jnp.concatenate(parts, axis=1), "shard", scatter_dimension=0, tiled=True)
    total = lax.psum(share, "rep").astype(F32)
    narrows = total[:, : 10 * width].reshape(-1, 10, width).transpose(1, 0, 2)
    wides = total[:, 10 * width :].reshape(-1, 2, features)
    return (narrows[:5], wides[:, 0], narrows[5:], wides[:, 1])


def solution(mesh):
    return jax.shard_map(
        per_device,
        mesh=mesh,
        in_specs=(
            P(("rep", "shard"), None, None),
            P(("rep", "shard"), None, None),
            P(("rep", "shard"), None),
            P(),
            P(),
            P(),
            P(),
            P(None, "shard", None),
            P("shard", None),
            P("shard", None),
            P(None, "shard"),
            P(None, "shard", None),
            P("shard", None),
            P(None, "shard", None),
            P("shard", None),
        ),
        out_specs=(
            P(("rep", "shard"), None, None),
            P(("rep", "shard"), None, None),
            P(None, "shard", None),
            P("shard", None),
            P(None, "shard", None),
            P("shard", None),
        ),
        check_vma=False,
    )
```
